32 devices in a mesh: seq: 8 (over z, y), head: 4 (over x, core).
Axes of the slice: x: 2, y: 2, z: 4, core: 2. Of those that a mesh axis runs over, the one named last changes fastest.
Arguments:
- hidden: bfloat16 [16384, 768], P('seq'), may hold values from -6 to 6
- teacher: bfloat16 [16384, 768], P('seq'), may hold values from -6 to 6
- doc_starts: int32 [16], replicated, may hold values from 0 to 15872, as said below
- valid_mask: int32 [16384], P('seq'), may hold values from 0 to 1, as said below
- norm_gain: float32 [768], replicated, may hold values from 0.5 to 1.5
- w_gate: bfloat16 [768, 1536], P(None, 'head'), may hold values from -0.21875 to 0.21875
- w_inner: bfloat16 [768, 1536], P(None, 'head'), may hold values from -0.21875 to 0.21875
- w_pair: bfloat16 [768, 256], replicated, may hold values from -0.21875 to 0.21875
- w_step: bfloat16 [768, 24], P(None, 'head'), may hold values from -0.21875 to 0.21875
- conv_inner: bfloat16 [4, 1536], P(None, 'head'), may hold values from -3 to 3
- bias_inner: bfloat16 [1536], P('head'), may hold values from -1.5 to 1.5
- conv_pair: bfloat16 [4, 256], replicated, may hold values from -3 to 3
- bias_pair: bfloat16 [256], replicated, may hold values from -1.5 to 1.5
- step_bias: float32 [24], P('head'), may hold values from -4 to -1
- decay_log: float32 [24], P('head'), may hold values from -11 to 0
- skip_gain: float32 [24], P('head'), may hold values from 0.5 to 1.5
- gate_gain: float32 [1536], P('head'), may hold values from 0.5 to 1.5
- w_output: bfloat16 [1536, 768], P('head'), may hold values from -0.15625 to 0.15625
Outputs:
- output: bfloat16 [16384, 768], P('seq')
- loss: float32 [], replicated
- grad_hidden: bfloat16 [16384, 768], P('seq')
- grad_norm_gain: float32 [768], replicated
- grad_w_gate: float32 [768, 1536], P(None, 'head')
- grad_w_inner: float32 [768, 1536], P(None, 'head')
- grad_w_pair: float32 [768, 256], replicated
- grad_w_step: float32 [768, 24], P(None, 'head')
- grad_conv_inner: float32 [4, 1536], P(None, 'head')
- grad_bias_inner: float32 [1536], P('head')
- grad_conv_pair: float32 [4, 256], replicated
- grad_bias_pair: float32 [256], replicated
- grad_step_bias: float32 [24], P('head')
- grad_decay_log: float32 [24], P('head')
- grad_skip_gain: float32 [24], P('head')
- grad_gate_gain: float32 [1536], P('head')
- grad_w_output: float32 [1536, 768], P('head')
The draws below stay inside these ranges and needn't reach their ends.
Inputs may be any that keep to these rules, and one draw needn't show every extreme that they name: `doc_starts`: strictly increasing; entry 0 is 0; entries 1 to 7 lie below 1024; entry 8 is 15360; entries 9 to 14 lie between entry 8 and entry 15; entry 15 is 15872. `valid_mask`: the last token is valid.
All inputs are finite; a program needn't handle non-finite values.
Results may differ from the reference program's by a relative error of at most 0.004.
The reference program's roundings to bfloat16 on the way (of `lowered`, `inner_in`, `pair_in` and `normed_out`) count: a program that leaves them out, or rounds other values in their place, can miss the bound.
Values may be sent and summed in bfloat16 or wider, within the bound.
A program may use at most 192 MiB of HBM per device.

```python
import jax
import jax.numpy as jnp
from jax import lax

D = 768
HEADS = 24
HEAD_DIM = 64
STATE = 128
KERNEL = 4
GROUP = 256
TOK_DEV = 2048
INNER = 1536
TOKENS = 16384


def draw_doc_starts(key, part):
    head_count = TOK_DEV // 2 - 1
    early = jnp.sort(jax.random.permutation(jax.random.fold_in(key, 11), head_count)[:7].astype(jnp.int32)) + 1
    tail_count = TOK_DEV // 4 - 1
    late = jnp.sort(jax.random.permutation(jax.random.fold_in(key, 13), tail_count)[:6].astype(jnp.int32)) + (TOKENS - TOK_DEV // 2 + 1)
    first = jnp.zeros((1,), jnp.int32)
    middle = jnp.full((1,), TOKENS - TOK_DEV // 2, jnp.int32)
    final = jnp.full((1,), TOKENS - TOK_DEV // 4, jnp.int32)
    return jnp.concatenate([first, early, middle, late, final]).astype(jnp.int32)


def draw_valid_mask(key, part):
    positions = jnp.arange(TOKENS, dtype=jnp.int32)
    threshold = 250 + positions * 500 // TOKENS
    rolls = jax.random.randint(jax.random.fold_in(key, 21), (TOKENS,), 0, 1000, dtype=jnp.int32)
    picked = (rolls < threshold).astype(jnp.int32)
    return picked.at[TOKENS - 1].set(1)


def block_scale(own_key, shape, cuts, low, largest):
    loudness = 1.0
    for axis_at, shards_of in cuts:
        steps = jax.random.uniform(jax.random.fold_in(jax.random.fold_in(own_key, 6), axis_at), (shards_of,), jnp.float32, low / len(cuts), largest / len(cuts))
        loudness = loudness * jnp.repeat(jnp.exp(steps), shape[axis_at] // shards_of).reshape((-1,) + (1,) * (len(shape) - 1 - axis_at))
    return loudness


def noise(rng, shape, deviation, most, cuts=(), kind=jnp.bfloat16):
    values = deviation * jax.random.normal(rng, shape, jnp.float32)
    if cuts:
        values = values * block_scale(rng, shape, cuts, -0.22, 0.18)
    return jnp.clip(values, -most, most).astype(kind)


def setup_inputs(seed: int = 0) -> dict:
    arg_keys = jax.random.split(jax.random.key(seed), 19)
    return {
        "hidden": noise(arg_keys[0], (TOKENS, D), 1.0, 6.0, ((0, 8),)),
        "teacher": noise(arg_keys[1], (TOKENS, D), 1.0, 6.0, ((0, 8),)),
        "doc_starts": draw_doc_starts(jax.random.fold_in(arg_keys[18], 71), 0),
        "valid_mask": draw_valid_mask(jax.random.fold_in(arg_keys[18], 71), 0),
        "norm_gain": jnp.clip(1.0 + 0.1 * jax.random.normal(arg_keys[4], (D,), jnp.float32), 0.5, 1.5),
        "w_gate": noise(arg_keys[5], (D, INNER), D ** -0.5, 0.21875, ((1, 4),)),
        "w_inner": noise(arg_keys[6], (D, INNER), D ** -0.5, 0.21875, ((1, 4),)),
        "w_pair": noise(arg_keys[7], (D, 2 * STATE), D ** -0.5, 0.21875),
        "w_step": noise(arg_keys[8], (D, HEADS), D ** -0.5, 0.21875, ((1, 4),)),
        "conv_inner": noise(arg_keys[9], (KERNEL, INNER), KERNEL ** -0.5, 3.0, ((1, 4),)),
        "bias_inner": noise(arg_keys[10], (INNER,), 0.3, 1.5, ((0, 4),)),
        "conv_pair": noise(arg_keys[11], (KERNEL, 2 * STATE), KERNEL ** -0.5, 3.0),
        "bias_pair": noise(arg_keys[12], (2 * STATE,), 0.3, 1.5),
        "step_bias": jnp.clip(-4.0 + 3.0 * jax.random.uniform(arg_keys[13], (HEADS,), jnp.float32) ** block_scale(arg_keys[13], (HEADS,), ((0, 4),), -0.2, 0.2), -4.0, -1.0),
        "decay_log": jnp.clip(-11.0 + 11.0 * jax.random.uniform(arg_keys[14], (HEADS,), jnp.float32) ** block_scale(arg_keys[14], (HEADS,), ((0, 4),), -0.2, 0.2), -11.0, 0.0),
        "skip_gain": jnp.clip(0.5 + 1.0 * jax.random.uniform(arg_keys[15], (HEADS,), jnp.float32) ** block_scale(arg_keys[15], (HEADS,), ((0, 4),), -0.2, 0.2), 0.5, 1.5),
        "gate_gain": jnp.clip(1.0 + 0.1 * jax.random.normal(arg_keys[16], (INNER,), jnp.float32), 0.5, 1.5),
        "w_output": noise(arg_keys[17], (INNER, D), INNER ** -0.5, 0.15625, ((0, 4),)),
    }


EPSILON = 1e-05
PRECISE = lax.Precision.HIGHEST

@jax.custom_vjp
def low(v):
    return lax.optimization_barrier(v.astype(jnp.bfloat16)).astype(jnp.float32)

@jax.custom_vjp
def low_back(v):
    return v

def low_keep(v):
    return (low(v), None)

def low_pass(kept, grad):
    return (grad,)

def back_keep(v):
    return (v, None)

def back_low(kept, grad):
    return (low(grad),)
low.defvjp(low_keep, low_pass)
low_back.defvjp(back_keep, back_low)

def doc_numbers(positions, starts):
    return lax.optimization_barrier(jnp.sum((starts[None, :] <= positions[:, None]).astype(jnp.int32), axis=1)) - 1

def matmul(first_matrix, second_matrix):
    return jnp.dot(first_matrix, second_matrix, preferred_element_type=jnp.float32, precision=PRECISE)

def convolve(padded, weight, conv_bias, allowed):
    length = allowed.shape[0]
    running = jnp.zeros((length, weight.shape[1]), jnp.float32) + conv_bias[None, :]
    for tap_index in range(weight.shape[0]):
        running = running + padded[tap_index:tap_index + length] * weight[tap_index][None, :] * allowed[:, tap_index:tap_index + 1]
    return jax.nn.silu(running)

def group_step(carry_state, pieces):
    values, keys_b, reads_c, step_size, log_decay, doc_index, before = pieces
    cum_log = jnp.cumsum(log_decay, axis=0)
    row_index = jnp.arange(doc_index.shape[0], dtype=jnp.int32)
    joined = (doc_index[:, None] == doc_index[None, :]) & (row_index[:, None] >= row_index[None, :])
    log_gaps = cum_log[:, None, :] - cum_log[None, :, :]
    weights = jnp.where(joined[:, :, None], jnp.exp(jnp.where(joined[:, :, None], log_gaps, 0.0)), 0.0)
    scores = jnp.dot(reads_c, keys_b.T, precision=PRECISE)
    scaled = values * step_size[:, :, None]
    intra_part = jnp.einsum('ijh,jhp->ihp', scores[:, :, None] * weights, scaled, precision=PRECISE)
    inflow = jnp.exp(cum_log) * (doc_index == before).astype(jnp.float32)[:, None]
    inter_part = jnp.einsum('in,hpn->ihp', reads_c, carry_state, precision=PRECISE) * inflow[:, :, None]
    tail_weight = jnp.exp(cum_log[-1][None, :] - cum_log) * (doc_index == doc_index[-1]).astype(jnp.float32)[:, None]
    keep_factor = jnp.exp(cum_log[-1]) * (doc_index[-1] == before).astype(jnp.float32)
    new_state = carry_state * keep_factor[:, None, None] + jnp.einsum('jh,jhp,jn->hpn', tail_weight, scaled, keys_b, precision=PRECISE)
    return (new_state, intra_part + inter_part)

def reference(hidden, teacher, doc_starts, valid_mask, norm_gain, w_gate, w_inner, w_pair, w_step, conv_inner, bias_inner, conv_pair, bias_pair, step_bias, decay_log, skip_gain, gate_gain, w_output):
    positions = jnp.arange(TOKENS, dtype=jnp.int32)
    doc_index = doc_numbers(positions, doc_starts)
    sources = positions[:, None] - (KERNEL - 1) + jnp.arange(KERNEL, dtype=jnp.int32)[None, :]
    allowed = (doc_numbers(sources.reshape(-1), doc_starts).reshape(TOKENS, KERNEL) == doc_index[:, None]).astype(jnp.float32)
    group_count = TOKENS // GROUP
    before_group = jnp.concatenate([jnp.array([-1], jnp.int32), doc_index[GROUP - 1::GROUP][:-1]])

    def forward(hidden_in, norm_in, gate_weight, inner_weight, pair_weight, step_weight, conv_in, conv_in_bias, conv_pw, conv_pw_bias, step_offset, decay_in, skip_in, gate_in, out_weight):
        mean_sq = lax.optimization_barrier(jnp.mean(hidden_in * hidden_in, axis=1, keepdims=True))
        lowered = low(hidden_in * lax.rsqrt(mean_sq + EPSILON) * norm_in[None, :])
        gate_pre = low_back(matmul(lowered, gate_weight))
        inner_in = low(low_back(matmul(lowered, inner_weight)))
        pair_in = low(low_back(matmul(lowered, pair_weight)))
        step_raw = low_back(matmul(lowered, step_weight))
        values = convolve(jnp.concatenate([jnp.zeros((KERNEL - 1, INNER), jnp.float32), inner_in]), conv_in, conv_in_bias, allowed)
        pair_out = convolve(jnp.concatenate([jnp.zeros((KERNEL - 1, 2 * STATE), jnp.float32), pair_in]), conv_pw, conv_pw_bias, allowed)
        step_size = jax.nn.softplus(step_raw + step_offset[None, :])
        log_decay = -step_size * jnp.exp(decay_in)[None, :]
        shaped = values.reshape(group_count, GROUP, HEADS, HEAD_DIM)
        pieces = (shaped, pair_out[:, :STATE].reshape(group_count, GROUP, STATE), pair_out[:, STATE:].reshape(group_count, GROUP, STATE), step_size.reshape(group_count, GROUP, HEADS), log_decay.reshape(group_count, GROUP, HEADS), doc_index.reshape(group_count, GROUP), before_group)
        final_state, outs = lax.scan(jax.checkpoint(group_step), jnp.zeros((HEADS, HEAD_DIM, STATE), jnp.float32), pieces)
        direct = values.reshape(TOKENS, HEADS, HEAD_DIM) * skip_in[None, :, None]
        mixer_out = outs.reshape(TOKENS, INNER) + direct.reshape(TOKENS, INNER)
        gated_out = mixer_out * jax.nn.silu(gate_pre)
        gate_scale = lax.rsqrt(lax.optimization_barrier(jnp.mean(gated_out * gated_out, axis=1, keepdims=True)) + EPSILON)
        normed_out = low(gated_out * gate_scale * gate_in[None, :])
        branch = low_back(matmul(normed_out, out_weight))
        return hidden_in + branch
    operands = (hidden.astype(jnp.float32), norm_gain, w_gate.astype(jnp.float32), w_inner.astype(jnp.float32), w_pair.astype(jnp.float32), w_step.astype(jnp.float32), conv_inner.astype(jnp.float32), bias_inner.astype(jnp.float32), conv_pair.astype(jnp.float32), bias_pair.astype(jnp.float32), step_bias, decay_log, skip_gain, gate_gain, w_output.astype(jnp.float32))
    output_f, backward = jax.vjp(forward, *operands)
    mask_float = valid_mask.astype(jnp.float32)
    error_term = output_f - teacher.astype(jnp.float32)
    valid_count = jnp.sum(mask_float)
    loss_value = jnp.sum(mask_float[:, None] * error_term * error_term) / (D * valid_count)
    d_output = mask_float[:, None] * error_term * (TOKENS / valid_count)
    grads = backward(d_output)
    return (output_f.astype(jnp.bfloat16), loss_value, grads[0].astype(jnp.bfloat16), grads[1], grads[2], grads[3], grads[4], grads[5], grads[6], grads[7], grads[8], grads[9], grads[10], grads[11], grads[12], grads[13], grads[14])
```

```python
from functools import partial

import jax
import jax.numpy as jnp
from jax import lax
from jax.experimental import pallas as pl
from jax.experimental.pallas import tpu as pltpu
from jax.sharding import PartitionSpec as P

EPSILON = 1e-05
CHUNK = 128
BLOCK = 256
HEAD_DIM = 64
LANES = 128
FAR = float(1 << 24)
F32 = jnp.float32
BF16 = jnp.bfloat16
HIGHEST = lax.Precision.HIGHEST

DT, CUM, INFLOW, TAIL, RATE, START, END = 0, 8, 16, 24, 32, 40, 41


def dot(a, b, da=1, db=0):
    return lax.dot_general(a, b, (((da,), (db,)), ((), ())), preferred_element_type=F32)


def halves(v):
    high = v.astype(BF16)
    return high, (v - high.astype(F32)).astype(BF16)


def dot3(a, b, da=1, db=0):
    ah, al = halves(a)
    bh, bl = halves(b)
    return dot(ah, bh, da, db) + (dot(ah, bl, da, db) + dot(al, bh, da, db))


def column_sums(v):
    high, low = halves(v)
    ones = jnp.ones((8, v.shape[1]), BF16)
    return (dot(ones, high, 1, 1) + dot(ones, low, 1, 1))[:1]


def as_column(row):
    return jnp.transpose(jnp.broadcast_to(row, (8, row.shape[1])))[:, :1]


def expand(table, base, width):
    rows = table.shape[0]
    lane = lax.broadcasted_iota(jnp.int32, (rows, LANES), 1)
    parts = []
    for pair in range(width // LANES):
        first = jnp.broadcast_to(table[:, base + 2 * pair : base + 2 * pair + 1], (rows, LANES))
        second = jnp.broadcast_to(table[:, base + 2 * pair + 1 : base + 2 * pair + 2], (rows, LANES))
        parts.append(jnp.where(lane < HEAD_DIM, first, second))
    return jnp.concatenate(parts, axis=1)


def head_matrix(width):
    channel = lax.broadcasted_iota(jnp.int32, (width, LANES), 0)
    head = lax.broadcasted_iota(jnp.int32, (width, LANES), 1)
    return ((channel >> 6) == head).astype(BF16)


def head_sums(v):
    high, low = halves(v)
    matrix = head_matrix(v.shape[1])
    return dot(high, matrix) + dot(low, matrix)


def triangle(upper):
    row = lax.broadcasted_iota(jnp.int32, (CHUNK, CHUNK), 0)
    col = lax.broadcasted_iota(jnp.int32, (CHUNK, CHUNK), 1)
    return ((col >= row) if upper else (col <= row)).astype(F32)


def silu_parts(pre):
    gate = jax.nn.sigmoid(pre)
    return pre * gate, gate * (1.0 + pre * (1.0 - gate))


def project_kernel(
    idx, starts, hid, halo, tail, gain, wi, wp, ws, conv_i, conv_p, bias_i, bias_p, sbias, dlog,
    low, in_i, in_p, pre_i, pre_p, aux, halo_i, halo_p, sloc, pkl, fin, wide_i, wide_p, state, decay,
):
    step = pl.program_id(0)
    edge = tail.shape[0]
    width = wi.shape[1]

    @pl.when(step == 0)
    def _():
        state[...] = jnp.zeros_like(state)
        decay[...] = jnp.ones_like(decay)

    before = jnp.where(step == 0, tail[...].astype(F32), halo[...].astype(F32))
    rows = jnp.concatenate([before, hid[...].astype(F32)], axis=0)
    scale = lax.rsqrt(jnp.mean(rows * rows, axis=1, keepdims=True) + EPSILON)
    lowered = (rows * scale * gain[...]).astype(BF16)
    own = lowered[edge:]
    low[...] = own
    inner = dot(lowered, wi[...]).astype(BF16)
    pair = dot(lowered, wp[...]).astype(BF16)
    in_i[...] = inner[edge:]
    in_p[...] = pair[edge:]
    wide_i[...] = inner.astype(F32)
    wide_p[...] = pair.astype(F32)

    @pl.when(step == 0)
    def _():
        halo_i[...] = inner[:edge]
        halo_p[...] = pair[:edge]

    base = idx[1] + step * BLOCK
    pos = (base + lax.broadcasted_iota(jnp.int32, (BLOCK, LANES), 0)).astype(F32)
    begun = starts[...] <= pos
    start = jnp.max(jnp.where(begun, starts[...], -1.0), axis=1, keepdims=True)
    end = jnp.min(jnp.where(begun, FAR, starts[...]), axis=1, keepdims=True)
    within = pos[:, :1] - start
    keep = [(within >= float(3 - k)).astype(F32) for k in range(3)]

    def convolve(wide, weight, bias):
        total = bias[...] + wide[edge : edge + BLOCK] * weight[3:4]
        for k in range(3):
            total = total + wide[edge - 3 + k : edge - 3 + k + BLOCK] * weight[k : k + 1] * keep[k]
        return total

    conv_inner = convolve(wide_i, conv_i, bias_i)
    conv_pair = convolve(wide_p, conv_p, bias_p)
    pre_i[...] = conv_inner
    pre_p[...] = conv_pair
    values = conv_inner * jax.nn.sigmoid(conv_inner)
    maps = conv_pair[:, :LANES]
    maps = maps * jax.nn.sigmoid(maps)

    raw = dot(own, ws[...]) + sbias[...]
    dt = jnp.maximum(raw, 0.0) + jnp.log1p(jnp.exp(-jnp.abs(raw)))
    rate = jax.nn.sigmoid(raw)
    logs = -dt * jnp.exp(dlog[...])
    lane = lax.broadcasted_iota(jnp.int32, (CHUNK, LANES), 1)
    lower = triangle(False)
    for c in range(BLOCK // CHUNK):
        at = slice(c * CHUNK, (c + 1) * CHUNK)
        cum = jnp.dot(lower, logs[at], precision=HIGHEST, preferred_element_type=F32)
        last = cum[CHUNK - 1 :]
        first = (base + c * CHUNK).astype(F32)
        inflow = jnp.exp(cum) * (start[at] <= first - 1.0).astype(F32)
        outflow = jnp.exp(last - cum) * (end[at] > first + (CHUNK - 1.0)).astype(F32)
        table = jnp.where(lane < CUM, dt[at], pltpu.roll(cum, CUM, 1))
        table = jnp.where(lane < INFLOW, table, pltpu.roll(inflow, INFLOW, 1))
        table = jnp.where(lane < TAIL, table, pltpu.roll(outflow, TAIL, 1))
        table = jnp.where(lane < RATE, table, pltpu.roll(rate[at], RATE, 1))
        table = jnp.where(lane < START, table, jnp.where(lane < END, start[at], end[at]))
        aux[at, :] = table
        scaled = values[at] * expand(table, DT, width) * expand(table, TAIL, width)
        added = dot3(maps[at], scaled, 0, 0)
        kept = expand(jnp.broadcast_to(inflow[CHUNK - 1 :], (8, LANES)), 0, width)
        sloc[c] = state[...]
        pkl[c] = decay[...]
        state[...] = state[...] * kept[:1] + added
        decay[...] = decay[...] * kept
    fin[:CHUNK] = state[...]
    fin[CHUNK:] = decay[...]


def masks(table, first, transposed):
    row = lax.broadcasted_iota(jnp.int32, (CHUNK, CHUNK), 0)
    col = lax.broadcasted_iota(jnp.int32, (CHUNK, CHUNK), 1)
    at = (first + col).astype(F32)
    if transposed:
        return (col >= row) & (at < table[:, END : END + 1])
    return (col <= row) & (at >= table[:, START : START + 1])


def head_split(v, pair):
    lane = lax.broadcasted_iota(jnp.int32, (v.shape[0], LANES), 1)
    part = v[:, pair * LANES : (pair + 1) * LANES]
    return jnp.concatenate(
        [jnp.where(lane < HEAD_DIM, part, 0.0), jnp.where(lane < HEAD_DIM, 0.0, part)], axis=0
    ).astype(BF16)


def intra_kernel(idx, low, wg, pre_i, pre_p, aux, skip, gate, mixed):
    width = wg.shape[1]
    gate[...] = dot(low[...], wg[...])
    base = idx[1] + pl.program_id(0) * BLOCK
    maps, _ = silu_parts(pre_p[...])
    values, _ = silu_parts(pre_i[...])
    for c in range(BLOCK // CHUNK):
        at = slice(c * CHUNK, (c + 1) * CHUNK)
        table = aux[at, :]
        rows = jnp.transpose(table)
        joined = masks(table, base + c * CHUNK, False)
        scores = dot(maps[at, LANES:].astype(BF16), maps[at, :LANES].astype(BF16), 1, 1)
        scaled = values[at] * expand(table, DT, width)
        parts = []
        for pair in range(width // LANES):
            weights = []
            for h in (2 * pair, 2 * pair + 1):
                gap = table[:, CUM + h : CUM + h + 1] - rows[CUM + h : CUM + h + 1, :]
                weights.append((scores * jnp.exp(jnp.where(joined, gap, -1e30))).astype(BF16))
            parts.append(dot(jnp.concatenate(weights, axis=1), head_split(scaled, pair)))
        mixed[at, :] = jnp.concatenate(parts, axis=1) + values[at] * skip[...]


def mix_kernel(pre_c, aux, sloc, pkl, sin, local, gate, mixer, states, square):
    width = local.shape[1]
    reads, _ = silu_parts(pre_c[...])
    for c in range(BLOCK // CHUNK):
        at = slice(c * CHUNK, (c + 1) * CHUNK)
        state = sloc[c] + pkl[c, :1] * sin[...]
        states[c] = state
        mixer[at, :] = local[at, :] + expand(aux[at, :], INFLOW, width) * dot3(reads[at], state)
    act, _ = silu_parts(gate[...])
    gated = mixer[...] * act
    square[...] = column_sums(gated * gated)


def gate_scale(square, total):
    return as_column(lax.rsqrt(square / total + EPSILON))


def branch_kernel(idx, mixer, gate, square, gain, wo, send, stay, *, total):
    step = pl.program_id(0)
    act, _ = silu_parts(gate[...])
    gated = mixer[...] * act
    normed = (gated * gate_scale(square[...], total) * gain[...]).astype(BF16)
    part = dot(normed, wo[...])

    @pl.when(step < pl.num_programs(0) // 2)
    def _():
        send[...] = part.astype(send.dtype)

    @pl.when(step >= pl.num_programs(0) // 2)
    def _():
        stay[...] = part


def loss_kernel(idx, factor, hid, teacher, valid, mine, other, out, d_branch, d_out, error):
    @pl.when(pl.program_id(0) == 0)
    def _():
        error[...] = jnp.zeros_like(error)

    outf = hid[...].astype(F32) + (mine[...].astype(F32) + other[...].astype(F32))
    out[...] = outf.astype(BF16)
    term = outf - teacher[...].astype(F32)
    masked = as_column(valid[...].astype(F32)) * term
    error[...] += jnp.sum(masked * term, axis=0, keepdims=True)
    grad = masked * factor[0]
    d_out[...] = grad
    d_branch[...] = grad.astype(BF16)


def branch_back_kernel(idx, mine, other, mixer, gate, square, gain, wo, weighted, cross, g_gain, g_wo, *, total):
    step = pl.program_id(0)

    @pl.when(step == 0)
    def _():
        g_gain[...] = jnp.zeros_like(g_gain)
        g_wo[...] = jnp.zeros_like(g_wo)

    d_branch = jnp.where(step < pl.num_programs(0) // 2, mine[...], other[...])
    act, _ = silu_parts(gate[...])
    gated = mixer[...] * act
    scaled = gated * gate_scale(square[...], total)
    normed = (scaled * gain[...]).astype(BF16)
    g_wo[...] += dot(normed, d_branch, 0, 0)
    d_normed = dot(d_branch, wo[...], 1, 1)
    g_gain[...] += jnp.sum(d_normed * scaled, axis=0, keepdims=True)
    grad = d_normed * gain[...]
    weighted[...] = grad
    cross[...] = column_sums(grad * gated)


def gate_back_kernel(
    weighted, mixer, gate, square, cross, pre_c, aux, d_mixer, d_gate, gloc, pkl, fin, state, decay, *, total
):
    @pl.when(pl.program_id(0) == 0)
    def _():
        state[...] = jnp.zeros_like(state)
        decay[...] = jnp.ones_like(decay)

    width = mixer.shape[1]
    act, slope = silu_parts(gate[...])
    gated = mixer[...] * act
    row = lax.rsqrt(square[...] / total + EPSILON)
    scale = as_column(row)
    pull = as_column(row * row * row * cross[...] / total)
    d_gated = scale * weighted[...] - gated * pull
    dy = d_gated * act
    d_mixer[...] = dy
    d_gate[...] = (d_gated * mixer[...] * slope).astype(BF16)
    reads, _ = silu_parts(pre_c[...])
    for c in reversed(range(BLOCK // CHUNK)):
        at = slice(c * CHUNK, (c + 1) * CHUNK)
        inflow = expand(aux[at, :], INFLOW, width)
        gloc[c] = state[...]
        pkl[c] = decay[...]
        kept = inflow[CHUNK - 1 :]
        state[...] = state[...] * kept + dot3(reads[at], dy[at] * inflow, 0, 0)
        decay[...] = decay[...] * kept
    fin[:CHUNK] = state[...]
    fin[CHUNK:] = decay[...]


def intra_back_kernel(idx, d_mixer, pre_i, pre_p, aux, low, d_gate, d_scaled, d_maps, g_wg):
    @pl.when(pl.program_id(0) == 0)
    def _():
        g_wg[...] = jnp.zeros_like(g_wg)

    g_wg[...] += dot(low[...], d_gate[...], 0, 0)
    width = d_mixer.shape[1]
    base = idx[1] + pl.program_id(0) * BLOCK
    maps, _ = silu_parts(pre_p[...])
    values, _ = silu_parts(pre_i[...])
    for c in range(BLOCK // CHUNK):
        at = slice(c * CHUNK, (c + 1) * CHUNK)
        table = aux[at, :]
        rows = jnp.transpose(table)
        joined = masks(table, base + c * CHUNK, True)
        keys = maps[at, :LANES].astype(BF16)
        reads = maps[at, LANES:].astype(BF16)
        scores = dot(keys, reads, 1, 1)
        scaled = (values[at] * expand(table, DT, width)).astype(BF16)
        grads = d_mixer[at, :]
        d_scores = jnp.zeros((CHUNK, CHUNK), F32)
        parts = []
        for pair in range(width // LANES):
            split = head_split(grads, pair)
            d_weights = dot(scaled[:, pair * LANES : (pair + 1) * LANES], split, 1, 1)
            weights = []
            for side in range(2):
                h = 2 * pair + side
                gap = rows[CUM + h : CUM + h + 1, :] - table[:, CUM + h : CUM + h + 1]
                factor = jnp.exp(jnp.where(joined, gap, -1e30))
                weights.append((scores * factor).astype(BF16))
                d_scores = d_scores + factor * d_weights[:, side * CHUNK : (side + 1) * CHUNK]
            parts.append(dot(jnp.concatenate(weights, axis=1), split))
        d_scaled[at, :] = jnp.concatenate(parts, axis=1)
        low_scores = d_scores.astype(BF16)
        d_maps[at, :] = jnp.concatenate([dot(low_scores, reads), dot(low_scores, keys, 0, 0)], axis=1)


def conv_back(grad, within, inputs, edge_inputs, weight, shifted, first, last, acc):
    rows = grad.shape[0]

    @pl.when(first)
    def _():
        for ref in shifted:
            ref[...] = jnp.zeros_like(ref)

    total = grad * weight[3:4]
    edge = jnp.zeros((8, grad.shape[1]), F32)
    acc[3:4] += jnp.sum(grad * inputs, axis=0, keepdims=True)
    acc[4:5] += jnp.sum(grad, axis=0, keepdims=True)
    for k, ref in enumerate(shifted):
        ref[8 : 8 + rows] = grad * (within >= float(3 - k)).astype(F32)
        moved = ref[3 - k : 3 - k + 8 + rows]
        total = total + moved[8:] * weight[k : k + 1]
        edge = edge + moved[:8] * weight[k : k + 1]
        outer = jnp.where(last, edge_inputs, 0.0) * moved[:8]
        acc[k : k + 1] += jnp.sum(moved[8:] * inputs, axis=0, keepdims=True) + jnp.sum(outer, axis=0, keepdims=True)
        ref[8 + rows :] = ref[8:16]
    return total, edge


def scan_back_kernel(
    idx, d_scaled, d_maps, pre_i, pre_p, in_i, halo_i, aux, gloc, pkl, gin, states, d_mixer, mixer, skip, dlog, conv_i,
    d_inner, d_step, d_both, edge, tail, small, heads, *shifted,
):
    step = pl.program_id(0)
    blocks = pl.num_programs(0)
    first, last = step == 0, step == blocks - 1
    width = mixer.shape[1]

    @pl.when(first)
    def _():
        small[...] = jnp.zeros_like(small)
        heads[...] = jnp.zeros_like(heads)

    base = idx[1] + (blocks - 1 - step) * BLOCK
    maps, _ = silu_parts(pre_p[...])
    values, slope = silu_parts(pre_i[...])
    dy = d_mixer[...]
    upper = triangle(True)
    lane = lax.broadcasted_iota(jnp.int32, (CHUNK, LANES), 1)
    grown = jnp.exp(dlog[...])
    pieces = []
    for c in range(BLOCK // CHUNK):
        at = slice(c * CHUNK, (c + 1) * CHUNK)
        table = aux[at, :]
        sizes = expand(table, DT, width)
        inflow = expand(table, INFLOW, width)
        outflow = expand(table, TAIL, width)
        keys, reads = maps[at, :LANES], maps[at, LANES:]
        scaled = values[at] * sizes
        grad_state = gloc[c] + pkl[c, :1] * gin[...]
        state = states[c]
        passed = outflow * dot3(keys, grad_state)
        total = d_scaled[at, :] + passed
        d_reads = d_maps[at, LANES:] + dot3(dy[at] * inflow, state, 1, 1)
        d_keys = d_maps[at, :LANES] + dot3(scaled * outflow, grad_state, 1, 1)
        d_both[at, :] = jnp.concatenate([d_keys, d_reads], axis=1)
        plain = mixer[at, :] - skip[...] * values[at]
        d_cum = head_sums(dy[at] * plain - scaled * total)
        carried = jnp.sum(grad_state * state, axis=0, keepdims=True) * inflow[CHUNK - 1 :]
        carried = carried + jnp.sum(scaled * passed, axis=0, keepdims=True)
        after = head_sums(jnp.broadcast_to(carried, (8, width)))[:1]
        d_logs = jnp.dot(upper, d_cum, precision=HIGHEST, preferred_element_type=F32) + after
        d_raw = (head_sums(total * values[at]) - grown * d_logs) * pltpu.roll(table, LANES - RATE, 1)
        d_raw = jnp.where(lane < 8, d_raw, 0.0)
        d_step[at, :] = d_raw.astype(BF16)
        d_decay = jnp.where(lane < 8, -d_logs * table * grown, 0.0)
        heads[0:1] += jnp.sum(d_raw, axis=0, keepdims=True)
        heads[1:2] += jnp.sum(d_decay, axis=0, keepdims=True)
        pieces.append(total * sizes + dy[at] * skip[...])
    small[5:6] += jnp.sum(dy * values, axis=0, keepdims=True)
    grad = jnp.concatenate(pieces, axis=0) * slope
    pos = (base + lax.broadcasted_iota(jnp.int32, (BLOCK, 1), 0)).astype(F32)
    within = pos - aux[:, START : START + 1]
    edge_inputs = halo_i[8:].astype(F32)
    whole, outer = conv_back(
        grad, within, in_i[...].astype(F32), edge_inputs, conv_i, shifted, first, last, small
    )
    d_inner[...] = whole.astype(BF16)
    edge[...] = outer

    @pl.when(first)
    def _():
        tail[...] = whole[BLOCK - 16 :]


def pair_back_kernel(idx, d_maps, pre_p, in_p, halo_p, aux, conv_p, d_pair, edge, tail, small, *shifted):
    step = pl.program_id(0)
    blocks = pl.num_programs(0)
    first, last = step == 0, step == blocks - 1

    @pl.when(first)
    def _():
        small[...] = jnp.zeros_like(small)

    base = idx[1] + (blocks - 1 - step) * BLOCK
    _, slope = silu_parts(pre_p[...])
    grad = d_maps[...].astype(F32) * slope
    pos = (base + lax.broadcasted_iota(jnp.int32, (BLOCK, 1), 0)).astype(F32)
    within = pos - aux[:, START : START + 1]
    whole, outer = conv_back(
        grad, within, in_p[...].astype(F32), halo_p[8:].astype(F32), conv_p, shifted, first, last, small
    )
    d_pair[...] = whole.astype(BF16)
    edge[...] = outer

    @pl.when(first)
    def _():
        tail[...] = whole[BLOCK - 16 :]


def input_back_kernel(idx, d_gate, d_inner, d_step, wg, wi, ws, send, stay):
    part = dot(d_gate[...], wg[...], 1, 1) + dot(d_inner[...], wi[...], 1, 1) + dot(d_step[...], ws[...], 1, 1)

    @pl.when(pl.program_id(0) < pl.num_programs(0) // 2)
    def _():
        send[...] = part.astype(send.dtype)

    @pl.when(pl.program_id(0) >= pl.num_programs(0) // 2)
    def _():
        stay[...] = part


def weight_back_kernel(low, d_inner, d_step, d_pair, g_wi, g_ws, g_wp):
    @pl.when(pl.program_id(0) == 0)
    def _():
        g_wi[...] = jnp.zeros_like(g_wi)
        g_ws[...] = jnp.zeros_like(g_ws)
        g_wp[...] = jnp.zeros_like(g_wp)

    g_wi[...] += dot(low[...], d_inner[...], 0, 0)
    g_ws[...] += dot(low[...], d_step[...], 0, 0)
    g_wp[...] += dot(low[...], d_pair[...], 0, 0)


def norm_back_kernel(idx, mine, other, d_pair, wp, hid, d_out, gain, grad, g_norm):
    @pl.when(pl.program_id(0) == 0)
    def _():
        g_norm[...] = jnp.zeros_like(g_norm)

    d_low = (mine[...].astype(F32) + other[...].astype(F32)) + dot(d_pair[...], wp[...], 1, 1)
    rows = hid[...].astype(F32)
    scale = lax.rsqrt(jnp.mean(rows * rows, axis=1, keepdims=True) + EPSILON)
    g_norm[...] += jnp.sum(d_low * rows * scale, axis=0, keepdims=True)
    scaled = d_low * gain[...]
    pull = jnp.mean(scaled * rows, axis=1, keepdims=True) * (scale * scale * scale)
    grad[...] = (d_out[...] + scale * scaled - rows * pull).astype(BF16)


def call(kernel, grid, ins, outs, scratch=(), prefetch=0, flops=0, moved=0):
    def spec(shape, block, index):
        if block is None:
            return pl.BlockSpec(shape, lambda *_: (0,) * len(shape))
        return pl.BlockSpec(block, index)

    scalars = [a for a, *_ in ins[:prefetch]]
    arrays = ins[prefetch:]
    in_specs = [
        pl.BlockSpec(memory_space=pltpu.SMEM) if block == "smem" else spec(a.shape, block, index)
        for a, block, index in arrays
    ]
    out_specs = [spec(shape, block, index) for shape, _, block, index in outs]
    return pl.pallas_call(
        kernel,
        grid_spec=pltpu.PrefetchScalarGridSpec(
            num_scalar_prefetch=prefetch, grid=(grid,), in_specs=in_specs, out_specs=out_specs, scratch_shapes=list(scratch)
        ),
        out_shape=[jax.ShapeDtypeStruct(shape, dtype) for shape, dtype, _, _ in outs],
        compiler_params=pltpu.CompilerParams(
            dimension_semantics=("arbitrary",), vmem_limit_bytes=48 << 20
        ),
        cost_estimate=pl.CostEstimate(flops=int(flops), bytes_accessed=int(moved), transcendentals=0),
    )(*scalars, *[a for a, *_ in arrays])


def swap(value, axis, bit):
    route = [(i, i ^ bit) for i in range(lax.axis_size(axis))]
    return jax.tree.map(lambda v: lax.ppermute(v, axis, route), value)


def shifted(value, axis, distance):
    devices = range(lax.axis_size(axis))
    route = [(i - distance, i) for i in devices if i - distance in devices]
    return lax.ppermute(value, axis, route)


def bits(axis):
    size = lax.axis_size(axis)
    return [1 << b for b in range(size.bit_length() - 1)]


def total_over(value, axis):
    for bit in bits(axis):
        value = value + swap(value, axis, bit)
    return value


def carried(total, axis, backward):
    mine = lax.axis_index(axis)

    def join(early, late):
        decay = late[CHUNK : CHUNK + 1]
        return jnp.concatenate([late[:CHUNK] + decay * early[:CHUNK], late[CHUNK:] * early[CHUNK:]])

    reached = jnp.concatenate([jnp.zeros_like(total[:CHUNK]), jnp.ones_like(total[CHUNK:])])
    for bit in bits(axis):
        other = swap(total, axis, bit)
        later = ((mine & bit) == 0) if backward else ((mine & bit) != 0)
        reached = jnp.where(later, join(other, reached), reached)
        total = jnp.where(later, join(other, total), join(total, other))
    return reached[:CHUNK]


def sum_rows(value, axis, wire):
    mine = lax.axis_index(axis)
    order = bits(axis)
    for bit in order:
        half = value.shape[0] // 2
        upper = ((mine & bit) != 0).astype(jnp.int32)
        away = lax.dynamic_slice_in_dim(value, (1 - upper) * half, half)
        value = lax.dynamic_slice_in_dim(value, upper * half, half)
        value = value + swap(away.astype(wire), axis, bit).astype(F32)
    value = value.astype(wire)
    for bit in reversed(order):
        other = swap(value, axis, bit)
        upper = (mine & bit) != 0
        value = jnp.where(upper, jnp.concatenate([other, value]), jnp.concatenate([value, other]))
    return value.astype(F32)


def both_halves(mine, other, core):
    return jnp.where(core == 0, jnp.concatenate([mine, other]), jnp.concatenate([other, mine]))


def padded(row, lanes=LANES):
    return jnp.zeros((1, lanes), F32).at[0, : row.shape[0]].set(row)


def shards(
    hidden, teacher, doc_starts, valid_mask, norm_gain, w_gate, w_inner, w_pair, w_step, conv_inner, bias_inner,
    conv_pair, bias_pair, step_bias, decay_log, skip_gain, gate_gain, w_output,
):
    rows, model = hidden.shape
    width = w_inner.shape[1]
    pair_width = w_pair.shape[1]
    heads = step_bias.shape[0]
    blocks, chunks = rows // BLOCK, rows // CHUNK
    per = BLOCK // CHUNK
    half = blocks // 2
    inner_total = float(width * lax.axis_size("head"))
    core = lax.axis_index("head") & 1
    offset = lax.axis_index("seq") * rows
    idx = jnp.stack([core, offset]).astype(jnp.int32)
    edge_rows = 16

    starts = jnp.full((1, LANES), FAR, F32).at[0, : doc_starts.shape[0]].set(doc_starts.astype(F32))
    ws = jnp.zeros((model, LANES), BF16).at[:, :heads].set(w_step)
    sbias, dlog = padded(step_bias), padded(decay_log)
    skip = jnp.repeat(skip_gain, HEAD_DIM)[None, :]
    gain, out_gain = norm_gain[None, :], gate_gain[None, :]
    conv_i, conv_p = conv_inner.astype(F32), conv_pair.astype(F32)
    bias_i, bias_p = bias_inner.astype(F32)[None, :], bias_pair.astype(F32)[None, :]
    valid = valid_mask[None, :]

    tail = shifted(hidden[rows - edge_rows :], "seq", 1)
    count = total_over(jnp.full((8, LANES), jnp.sum(valid_mask.astype(F32))), "seq")[0, 0]
    factor = (rows * lax.axis_size("seq")) / count

    def by(w, column=0):
        return (BLOCK, w), lambda i, *_: (i, column)

    def back(w, column=0):
        return (BLOCK, w), lambda i, *_: (blocks - 1 - i, column)

    row = ((1, BLOCK), lambda i, *_: (0, i))
    row_back = ((1, BLOCK), lambda i, *_: (0, blocks - 1 - i))
    grid3 = lambda n: ((per, n, width), lambda i, *_: (i, 0, 0))
    back3 = lambda n: ((per, n, width), lambda i, *_: (blocks - 1 - i, 0, 0))
    whole = (None, None)

    def send_order(w):
        return (BLOCK, w), lambda i, s: (lax.rem(i + half * (1 - s[0]), blocks), 0)

    def own_order(w):
        return (BLOCK, w), lambda i, s: (lax.rem(i + half * s[0], blocks), 0)

    own_row = ((1, BLOCK), lambda i, s: (0, lax.rem(i + half * s[0], blocks)))
    send_row = ((1, BLOCK), lambda i, s: (0, lax.rem(i + half * (1 - s[0]), blocks)))
    head_half = lambda w: ((BLOCK, w), lambda i, s: (jnp.minimum(i, half - 1), 0))
    tail_half = lambda w: ((BLOCK, w), lambda i, s: (jnp.maximum(i - half, 0), 0))

    halo_block = ((edge_rows, model), lambda i, *_: (jnp.maximum(i * (BLOCK // edge_rows) - 1, 0), 0))
    (low, in_i, in_p, pre_i, pre_p, aux, halo_i, halo_p, sloc, pkl, fin) = call(
        project_kernel,
        blocks,
        [
            (idx, None, None), (starts, *whole), (hidden, *by(model)), (hidden, *halo_block), (tail, *whole),
            (gain, *whole), (w_inner, *whole), (w_pair, *whole), (ws, *whole), (conv_i, *whole), (conv_p, *whole),
            (bias_i, *whole), (bias_p, *whole), (sbias, *whole), (dlog, *whole),
        ],
        [
            ((rows, model), BF16, *by(model)), ((rows, width), BF16, *by(width)), ((rows, pair_width), BF16, *by(pair_width)),
            ((rows, width), F32, *by(width)), ((rows, pair_width), F32, *by(pair_width)), ((rows, LANES), F32, *by(LANES)),
            ((edge_rows, width), BF16, *whole), ((edge_rows, pair_width), BF16, *whole),
            ((chunks, CHUNK, width), F32, *grid3(CHUNK)), ((chunks, 8, width), F32, *grid3(8)),
            ((CHUNK + 8, width), F32, *whole),
        ],
        [
            pltpu.VMEM((BLOCK + edge_rows, width), F32), pltpu.VMEM((BLOCK + edge_rows, pair_width), F32),
            pltpu.VMEM((CHUNK, width), F32), pltpu.VMEM((8, width), F32),
        ],
        prefetch=1, flops=3e9, moved=2e7,
    )
    state_in = carried(fin, "seq", False)
    gate, local = call(
        intra_kernel,
        blocks,
        [
            (idx, None, None), (low, *by(model)), (w_gate, *whole), (pre_i, *by(width)), (pre_p, *by(pair_width)),
            (aux, *by(LANES)), (skip, *whole),
        ],
        [((rows, width), F32, *by(width)), ((rows, width), F32, *by(width))],
        prefetch=1, flops=4e9, moved=2e7,
    )
    mixer, states, square = call(
        mix_kernel,
        blocks,
        [
            (pre_p, *by(LANES, 1)), (aux, *by(LANES)), (sloc, *grid3(CHUNK)), (pkl, *grid3(8)), (state_in, *whole),
            (local, *by(width)), (gate, *by(width)),
        ],
        [((rows, width), F32, *by(width)), ((chunks, CHUNK, width), F32, *grid3(CHUNK)), ((1, rows), F32, *row)],
        flops=1e9, moved=2e7,
    )
    square = total_over(square, "head")
    send, stay = call(
        partial(branch_kernel, total=inner_total),
        blocks,
        [
            (idx, None, None), (mixer, *send_order(width)), (gate, *send_order(width)), (square, *send_row),
            (out_gain, *whole), (w_output, *whole),
        ],
        [((rows // 2, model), BF16, *head_half(model)), ((rows // 2, model), F32, *tail_half(model))],
        prefetch=1, flops=1.2e9, moved=1e7,
    )
    mine = (stay + swap(send, "head", 1).astype(F32)).astype(BF16)
    other = swap(mine, "head", 2)
    half_own = lambda w: ((BLOCK, w), lambda i, s: (i + half * s[0], 0))
    output_half, d_branch_half, d_out, error = call(
        loss_kernel,
        half,
        [
            (idx, None, None), (factor.reshape(1), "smem", None), (hidden, *half_own(model)), (teacher, *half_own(model)),
            (valid, (1, BLOCK), lambda i, s: (0, i + half * s[0])), (mine, *by(model)), (other, *by(model)),
        ],
        [
            ((rows // 2, model), BF16, *by(model)), ((rows // 2, model), BF16, *by(model)),
            ((rows // 2, model), F32, *by(model)), ((1, model), F32, *whole),
        ],
        prefetch=1, flops=1e8, moved=1.5e7,
    )
    d_branch_other = swap(d_branch_half, "head", 1)
    output = both_halves(output_half, swap(output_half, "head", 1), core)
    weighted, cross, g_gain, g_wo = call(
        partial(branch_back_kernel, total=inner_total),
        blocks,
        [
            (idx, None, None), (d_branch_half, *head_half(model)), (d_branch_other, *tail_half(model)),
            (mixer, *own_order(width)), (gate, *own_order(width)), (square, *own_row), (out_gain, *whole), (w_output, *whole),
        ],
        [
            ((rows, width), F32, *own_order(width)), ((1, rows), F32, *own_row), ((1, width), F32, *whole),
            ((width, model), F32, *whole),
        ],
        prefetch=1, flops=2.4e9, moved=1.5e7,
    )
    cross = total_over(cross, "head")
    d_mixer, d_gate, gloc, pkb, fin_back = call(
        partial(gate_back_kernel, total=inner_total),
        blocks,
        [
            (weighted, *back(width)), (mixer, *back(width)), (gate, *back(width)), (square, *row_back), (cross, *row_back),
            (pre_p, *back(LANES, 1)), (aux, *back(LANES)),
        ],
        [
            ((rows, width), F32, *back(width)), ((rows, width), BF16, *back(width)),
            ((chunks, CHUNK, width), F32, *back3(CHUNK)), ((chunks, 8, width), F32, *back3(8)), ((CHUNK + 8, width), F32, *whole),
        ],
        [pltpu.VMEM((CHUNK, width), F32), pltpu.VMEM((8, width), F32)],
        flops=1e9, moved=2e7,
    )
    grad_in = carried(fin_back, "seq", True)
    d_scaled, d_maps, g_wg = call(
        intra_back_kernel,
        blocks,
        [
            (idx, None, None), (d_mixer, *by(width)), (pre_i, *by(width)), (pre_p, *by(pair_width)), (aux, *by(LANES)),
            (low, *by(model)), (d_gate, *by(width)),
        ],
        [((rows, width), F32, *by(width)), ((rows, pair_width), F32, *by(pair_width)), ((model, width), F32, *whole)],
        prefetch=1, flops=6e9, moved=2e7,
    )
    d_inner, d_step, d_both, edge_i, tail_i, small_i, head_small = call(
        scan_back_kernel,
        blocks,
        [
            (idx, None, None), (d_scaled, *back(width)), (d_maps, *back(pair_width)), (pre_i, *back(width)),
            (pre_p, *back(pair_width)), (in_i, *back(width)), (halo_i, *whole), (aux, *back(LANES)), (gloc, *back3(CHUNK)),
            (pkb, *back3(8)), (grad_in, *whole), (states, *back3(CHUNK)), (d_mixer, *back(width)), (mixer, *back(width)),
            (skip, *whole), (dlog, *whole), (conv_i, *whole),
        ],
        [
            ((rows, width), BF16, *back(width)), ((rows, LANES), BF16, *back(LANES)), ((rows, pair_width), F32, *back(pair_width)),
            ((8, width), F32, *whole), ((16, width), F32, *whole), ((8, width), F32, *whole), ((8, LANES), F32, *whole),
        ],
        [pltpu.VMEM((BLOCK + 16, width), F32)] * 3,
        prefetch=1, flops=3e9, moved=3e7,
    )

    def finish(grads, tail, edge):
        after = shifted(edge, "seq", -1)
        fixed = jnp.concatenate([tail[:8], tail[8:] + after]).astype(BF16)
        return lax.dynamic_update_slice(grads, fixed, (rows - 16, 0))

    d_inner = finish(d_inner, tail_i, edge_i)
    half_rows = rows // 2
    away = lax.dynamic_slice_in_dim(d_both, (1 - core) * half_rows, half_rows)
    kept = lax.dynamic_slice_in_dim(d_both, core * half_rows, half_rows)
    kept = kept + swap(away, "head", 1)
    kept = kept + swap(kept, "head", 2)
    d_both = both_halves(kept, swap(kept, "head", 1), core)
    d_pair, edge_p, tail_p, small_p = call(
        pair_back_kernel,
        blocks,
        [
            (idx, None, None), (d_both, *back(pair_width)), (pre_p, *back(pair_width)), (in_p, *back(pair_width)),
            (halo_p, *whole), (aux, *back(LANES)), (conv_p, *whole),
        ],
        [
            ((rows, pair_width), BF16, *back(pair_width)), ((8, pair_width), F32, *whole), ((16, pair_width), F32, *whole),
            ((8, pair_width), F32, *whole),
        ],
        [pltpu.VMEM((BLOCK + 16, pair_width), F32)] * 3,
        prefetch=1, flops=1e8, moved=1e7,
    )
    d_pair = finish(d_pair, tail_p, edge_p)
    send, stay = call(
        input_back_kernel,
        blocks,
        [
            (idx, None, None), (d_gate, *send_order(width)), (d_inner, *send_order(width)), (d_step, *send_order(LANES)),
            (w_gate, *whole), (w_inner, *whole), (ws, *whole),
        ],
        [((rows // 2, model), BF16, *head_half(model)), ((rows // 2, model), F32, *tail_half(model))],
        prefetch=1, flops=2.6e9, moved=1e7,
    )
    mine = (stay + swap(send, "head", 1).astype(F32)).astype(BF16)
    other = swap(mine, "head", 2)
    g_wi, g_ws, g_wp = call(
        weight_back_kernel,
        blocks,
        [(low, *by(model)), (d_inner, *by(width)), (d_step, *by(LANES)), (d_pair, *by(pair_width))],
        [((model, width), F32, *whole), ((model, LANES), F32, *whole), ((model, pair_width), F32, *whole)],
        flops=2.4e9, moved=1e7,
    )
    grad_half, g_norm = call(
        norm_back_kernel,
        half,
        [
            (idx, None, None), (mine, *by(model)), (other, *by(model)), (d_pair, *half_own(pair_width)), (w_pair, *whole),
            (hidden, *half_own(model)), (d_out, *by(model)), (gain, *whole),
        ],
        [((rows // 2, model), BF16, *by(model)), ((1, model), F32, *whole)],
        prefetch=1, flops=5e8, moved=1e7,
    )
    grad_hidden = both_halves(grad_half, swap(grad_half, "head", 1), core)

    g_wo = sum_rows(g_wo, "seq", BF16)
    g_wg = sum_rows(g_wg, "seq", BF16)
    g_wi = sum_rows(g_wi, "seq", BF16)
    g_wp = sum_rows(g_wp, "seq", F32)
    lane_small = jnp.concatenate([small_i[:6], g_gain, jnp.zeros((1, width), F32)])
    by_head = total_over(lane_small, "seq")
    head_small = total_over(head_small, "seq")
    g_ws = sum_rows(g_ws[:, :heads], "seq", F32)
    pair_small = total_over(small_p, "seq")
    sums = jnp.concatenate([g_norm, error, jnp.zeros((6, model), F32)])
    sums = total_over(sums + swap(sums, "head", 1), "seq")
    loss = jnp.sum(sums[1]) / (count * model)
    return (
        output, loss, grad_hidden, sums[0], g_wg, g_wi, g_wp, g_ws, by_head[:4], by_head[4], pair_small[:4], pair_small[4],
        head_small[0, :heads], head_small[1, :heads], jnp.sum(by_head[5].reshape(heads, HEAD_DIM), axis=1), by_head[6], g_wo,
    )


def solution(mesh):
    seq, head, wide = P("seq", None), P("head"), P(None, "head")
    in_specs = (
        seq, seq, P(), P("seq"), P(), wide, wide, P(), wide, wide, head, P(), P(), head, head, head, head, P("head", None),
    )
    out_specs = (
        seq, P(), seq, P(), wide, wide, P(), wide, wide, head, P(), P(), head, head, head, head, P("head", None),
    )
    return jax.shard_map(shards, mesh=mesh, in_specs=in_specs, out_specs=out_specs, check_vma=False)
```

```python
from functools import partial

import jax
import jax.numpy as jnp
from jax import lax
from jax.experimental import pallas as pl
from jax.experimental.pallas import tpu as pltpu
from jax.sharding import PartitionSpec as P

EPSILON = 1e-05
CHUNK = 128
BLOCK = 256
HEAD_DIM = 64
LANES = 128
FAR = float(1 << 24)
F32 = jnp.float32
BF16 = jnp.bfloat16
HIGHEST = lax.Precision.HIGHEST

DT, CUM, INFLOW, TAIL, RATE, START, END = 0, 8, 16, 24, 32, 40, 41


def dot(a, b, da=1, db=0):
    return lax.dot_general(a, b, (((da,), (db,)), ((), ())), preferred_element_type=F32)


def halves(v):
    high = v.astype(BF16)
    return high, (v - high.astype(F32)).astype(BF16)


def dot3(a, b, da=1, db=0):
    ah, al = halves(a)
    bh, bl = halves(b)
    return dot(ah, bh, da, db) + (dot(ah, bl, da, db) + dot(al, bh, da, db))


def column_sums(v):
    high, low = halves(v)
    ones = jnp.ones((8, v.shape[1]), BF16)
    return (dot(ones, high, 1, 1) + dot(ones, low, 1, 1))[:1]


def as_column(row):
    return jnp.transpose(jnp.broadcast_to(row, (8, row.shape[1])))[:, :1]


def expand(table, base, width):
    rows = table.shape[0]
    lane = lax.broadcasted_iota(jnp.int32, (rows, LANES), 1)
    parts = []
    for pair in range(width // LANES):
        first = jnp.broadcast_to(table[:, base + 2 * pair : base + 2 * pair + 1], (rows, LANES))
        second = jnp.broadcast_to(table[:, base + 2 * pair + 1 : base + 2 * pair + 2], (rows, LANES))
        parts.append(jnp.where(lane < HEAD_DIM, first, second))
    return jnp.concatenate(parts, axis=1)


def head_matrix(width):
    channel = lax.broadcasted_iota(jnp.int32, (width, LANES), 0)
    head = lax.broadcasted_iota(jnp.int32, (width, LANES), 1)
    return ((channel >> 6) == head).astype(BF16)


def head_sums(v):
    high, low = halves(v)
    matrix = head_matrix(v.shape[1])
    return dot(high, matrix) + dot(low, matrix)


def triangle(upper):
    row = lax.broadcasted_iota(jnp.int32, (CHUNK, CHUNK), 0)
    col = lax.broadcasted_iota(jnp.int32, (CHUNK, CHUNK), 1)
    return ((col >= row) if upper else (col <= row)).astype(F32)


def silu_parts(pre):
    gate = jax.nn.sigmoid(pre)
    return pre * gate, gate * (1.0 + pre * (1.0 - gate))


def project_kernel(
    idx, starts, hid, halo, tail, gain, wi, wp, ws, conv_i, conv_p, bias_i, bias_p, sbias, dlog,
    low, in_i, in_p, pre_i, pre_p, aux, halo_i, halo_p, sloc, pkl, fin, wide_i, wide_p, state, decay,
):
    step = pl.program_id(0)
    edge = tail.shape[0]
    width = wi.shape[1]

    @pl.when(step == 0)
    def _():
        state[...] = jnp.zeros_like(state)
        decay[...] = jnp.ones_like(decay)

    before = jnp.where(step == 0, tail[...].astype(F32), halo[...].astype(F32))
    rows = jnp.concatenate([before, hid[...].astype(F32)], axis=0)
    scale = lax.rsqrt(jnp.mean(rows * rows, axis=1, keepdims=True) + EPSILON)
    lowered = (rows * scale * gain[...]).astype(BF16)
    own = lowered[edge:]
    low[...] = own
    inner = dot(lowered, wi[...]).astype(BF16)
    pair = dot(lowered, wp[...]).astype(BF16)
    in_i[...] = inner[edge:]
    in_p[...] = pair[edge:]
    wide_i[...] = inner.astype(F32)
    wide_p[...] = pair.astype(F32)

    @pl.when(step == 0)
    def _():
        halo_i[...] = inner[:edge]
        halo_p[...] = pair[:edge]

    base = idx[1] + step * BLOCK
    pos = (base + lax.broadcasted_iota(jnp.int32, (BLOCK, LANES), 0)).astype(F32)
    begun = starts[...] <= pos
    start = jnp.max(jnp.where(begun, starts[...], -1.0), axis=1, keepdims=True)
    end = jnp.min(jnp.where(begun, FAR, starts[...]), axis=1, keepdims=True)
    within = pos[:, :1] - start
    keep = [(within >= float(3 - k)).astype(F32) for k in range(3)]

    def convolve(wide, weight, bias):
        total = bias[...] + wide[edge : edge + BLOCK] * weight[3:4]
        for k in range(3):
            total = total + wide[edge - 3 + k : edge - 3 + k + BLOCK] * weight[k : k + 1] * keep[k]
        return total

    conv_inner = convolve(wide_i, conv_i, bias_i)
    conv_pair = convolve(wide_p, conv_p, bias_p)
    pre_i[...] = conv_inner
    pre_p[...] = conv_pair
    values = conv_inner * jax.nn.sigmoid(conv_inner)
    maps = conv_pair[:, :LANES]
    maps = maps * jax.nn.sigmoid(maps)

    raw = dot(own, ws[...]) + sbias[...]
    dt = jnp.maximum(raw, 0.0) + jnp.log1p(jnp.exp(-jnp.abs(raw)))
    rate = jax.nn.sigmoid(raw)
    logs = -dt * jnp.exp(dlog[...])
    lane = lax.broadcasted_iota(jnp.int32, (CHUNK, LANES), 1)
    lower = triangle(False)
    for c in range(BLOCK // CHUNK):
        at = slice(c * CHUNK, (c + 1) * CHUNK)
        cum = jnp.dot(lower, logs[at], precision=HIGHEST, preferred_element_type=F32)
        last = cum[CHUNK - 1 :]
        first = (base + c * CHUNK).astype(F32)
        inflow = jnp.exp(cum) * (start[at] <= first - 1.0).astype(F32)
        outflow = jnp.exp(last - cum) * (end[at] > first + (CHUNK - 1.0)).astype(F32)
        table = jnp.where(lane < CUM, dt[at], pltpu.roll(cum, CUM, 1))
        table = jnp.where(lane < INFLOW, table, pltpu.roll(inflow, INFLOW, 1))
        table = jnp.where(lane < TAIL, table, pltpu.roll(outflow, TAIL, 1))
        table = jnp.where(lane < RATE, table, pltpu.roll(rate[at], RATE, 1))
        table = jnp.where(lane < START, table, jnp.where(lane < END, start[at], end[at]))
        aux[at, :] = table
        scaled = values[at] * expand(table, DT, width) * expand(table, TAIL, width)
        added = dot3(maps[at], scaled, 0, 0)
        kept = expand(jnp.broadcast_to(inflow[CHUNK - 1 :], (8, LANES)), 0, width)
        sloc[c] = state[...]
        pkl[c] = decay[...]
        state[...] = state[...] * kept[:1] + added
        decay[...] = decay[...] * kept
    fin[:CHUNK] = state[...]
    fin[CHUNK:] = decay[...]


def masks(table, first, transposed):
    row = lax.broadcasted_iota(jnp.int32, (CHUNK, CHUNK), 0)
    col = lax.broadcasted_iota(jnp.int32, (CHUNK, CHUNK), 1)
    at = (first + col).astype(F32)
    if transposed:
        return (col >= row) & (at < table[:, END : END + 1])
    return (col <= row) & (at >= table[:, START : START + 1])


def head_split(v, pair):
    lane = lax.broadcasted_iota(jnp.int32, (v.shape[0], LANES), 1)
    part = v[:, pair * LANES : (pair + 1) * LANES]
    return jnp.concatenate(
        [jnp.where(lane < HEAD_DIM, part, 0.0), jnp.where(lane < HEAD_DIM, 0.0, part)], axis=0
    ).astype(BF16)


def intra_kernel(idx, low, wg, pre_i, pre_p, aux, skip, gate, mixed):
    width = wg.shape[1]
    gate[...] = dot(low[...], wg[...])
    base = idx[1] + pl.program_id(0) * BLOCK
    maps, _ = silu_parts(pre_p[...])
    values, _ = silu_parts(pre_i[...])
    for c in range(BLOCK // CHUNK):
        at = slice(c * CHUNK, (c + 1) * CHUNK)
        table = aux[at, :]
        rows = jnp.transpose(table)
        joined = masks(table, base + c * CHUNK, False)
        scores = dot(maps[at, LANES:].astype(BF16), maps[at, :LANES].astype(BF16), 1, 1)
        scaled = values[at] * expand(table, DT, width)
        parts = []
        for pair in range(width // LANES):
            weights = []
            for h in (2 * pair, 2 * pair + 1):
                gap = table[:, CUM + h : CUM + h + 1] - rows[CUM + h : CUM + h + 1, :]
                weights.append((scores * jnp.exp(jnp.where(joined, gap, -1e30))).astype(BF16))
            parts.append(dot(jnp.concatenate(weights, axis=1), head_split(scaled, pair)))
        mixed[at, :] = jnp.concatenate(parts, axis=1) + values[at] * skip[...]


def mix_kernel(pre_c, aux, sloc, pkl, sin, local, gate, mixer, states, square):
    width = local.shape[1]
    reads, _ = silu_parts(pre_c[...])
    for c in range(BLOCK // CHUNK):
        at = slice(c * CHUNK, (c + 1) * CHUNK)
        state = sloc[c] + pkl[c, :1] * sin[...]
        states[c] = state
        mixer[at, :] = local[at, :] + expand(aux[at, :], INFLOW, width) * dot3(reads[at], state)
    act, _ = silu_parts(gate[...])
    gated = mixer[...] * act
    square[...] = column_sums(gated * gated)


def gate_scale(square, total):
    return as_column(lax.rsqrt(square / total + EPSILON))


def core_bit():
    return lax.rem(lax.axis_index("head"), 2)


def core_peer():
    return lax.axis_index("head") + 1 - 2 * core_bit()


def enter(peers):
    barrier = pltpu.get_barrier_semaphore()
    for peer in peers:
        pl.semaphore_signal(barrier, inc=1, device_id=peer, device_id_type=pl.DeviceIdType.MESH)
    pl.semaphore_wait(barrier, len(peers))


def to_peer(src, dst, sends, lands, slot):
    return pltpu.make_async_remote_copy(
        src_ref=src, dst_ref=dst, send_sem=sends.at[slot], recv_sem=lands.at[slot],
        device_id={"head": core_peer()}, device_id_type=pl.DeviceIdType.MESH,
    )


def add_halves(part, mine, away, land, send_sem, land_sem):
    step = pl.program_id(0)
    half = pl.num_programs(0) // 2

    def copy(slot):
        return to_peer(away.at[slot], land.at[slot], send_sem, land_sem, slot)

    @pl.when(step < half)
    def _():
        away[step] = part.astype(away.dtype)
        copy(step).start()

    @pl.when(step >= half)
    def _():
        copy(step - half).wait_recv()
        mine[...] = (part + land[step - half].astype(F32)).astype(mine.dtype)

    @pl.when(step == 2 * half - 1)
    def _():
        def drain(slot, carry):
            copy(slot).wait_send()
            return carry

        lax.fori_loop(0, half, drain, 0)


def branch_kernel(mixer, gate, square, gain, wo, mine, away, land, send_sem, land_sem, *, total):
    @pl.when(pl.program_id(0) == 0)
    def _():
        enter([{"head": core_peer()}])

    act, _ = silu_parts(gate[...])
    gated = mixer[...] * act
    normed = (gated * gate_scale(square[...], total) * gain[...]).astype(BF16)
    add_halves(dot(normed, wo[...]), mine, away, land, send_sem, land_sem)


def both_cores(buffers, wholes, sems):
    step = pl.program_id(0)
    half = pl.num_programs(0)
    local, send, land = sems

    def copies(k, slot):
        rows = pl.ds(pl.multiple_of((core_bit() * half + slot) * BLOCK, BLOCK), BLOCK)
        here = pltpu.make_async_copy(buffers[k].at[slot], wholes[k].at[rows], local.at[k * half + slot])
        there = to_peer(buffers[k].at[slot], wholes[k].at[rows], send, land, k * half + slot)
        return here, there

    for k in range(len(wholes)):
        for copy in copies(k, step):
            copy.start()

    @pl.when(step == half - 1)
    def _():
        for k in range(len(wholes)):

            def drain(slot, carry, k=k):
                here, there = copies(k, slot)
                here.wait()
                there.wait()
                return carry

            lax.fori_loop(0, half, drain, 0)


def loss_kernel(factor, hid, teacher, valid, mine, other, out, d_branch, d_out, error, out_block, grad_block, *sems):
    step = pl.program_id(0)

    @pl.when(step == 0)
    def _():
        error[...] = jnp.zeros_like(error)
        enter([{"head": core_peer()}])

    outf = hid[...].astype(F32) + (mine[...].astype(F32) + other[...].astype(F32))
    term = outf - teacher[...].astype(F32)
    masked = as_column(valid[...].astype(F32)) * term
    error[...] += jnp.sum(masked * term, axis=0, keepdims=True)
    grad = masked * factor[0]
    d_out[...] = grad
    out_block[step] = outf.astype(BF16)
    grad_block[step] = grad.astype(BF16)
    both_cores([out_block, grad_block], [out, d_branch], sems)


def branch_back_kernel(d_branch, mixer, gate, square, gain, wo, weighted, cross, g_gain, g_wo, *, total):
    step = pl.program_id(0)

    @pl.when(step == 0)
    def _():
        g_gain[...] = jnp.zeros_like(g_gain)
        g_wo[...] = jnp.zeros_like(g_wo)

    act, _ = silu_parts(gate[...])
    gated = mixer[...] * act
    scaled = gated * gate_scale(square[...], total)
    normed = (scaled * gain[...]).astype(BF16)
    g_wo[...] += dot(normed, d_branch[...], 0, 0)
    d_normed = dot(d_branch[...], wo[...], 1, 1)
    g_gain[...] += jnp.sum(d_normed * scaled, axis=0, keepdims=True)
    grad = d_normed * gain[...]
    weighted[...] = grad
    cross[...] = column_sums(grad * gated)


def gate_back_kernel(
    weighted, mixer, gate, square, cross, pre_c, aux, d_mixer, d_gate, gloc, pkl, fin, state, decay, *, total
):
    @pl.when(pl.program_id(0) == 0)
    def _():
        state[...] = jnp.zeros_like(state)
        decay[...] = jnp.ones_like(decay)

    width = mixer.shape[1]
    act, slope = silu_parts(gate[...])
    gated = mixer[...] * act
    row = lax.rsqrt(square[...] / total + EPSILON)
    scale = as_column(row)
    pull = as_column(row * row * row * cross[...] / total)
    d_gated = scale * weighted[...] - gated * pull
    dy = d_gated * act
    d_mixer[...] = dy
    d_gate[...] = (d_gated * mixer[...] * slope).astype(BF16)
    reads, _ = silu_parts(pre_c[...])
    for c in reversed(range(BLOCK // CHUNK)):
        at = slice(c * CHUNK, (c + 1) * CHUNK)
        inflow = expand(aux[at, :], INFLOW, width)
        gloc[c] = state[...]
        pkl[c] = decay[...]
        kept = inflow[CHUNK - 1 :]
        state[...] = state[...] * kept + dot3(reads[at], dy[at] * inflow, 0, 0)
        decay[...] = decay[...] * kept
    fin[:CHUNK] = state[...]
    fin[CHUNK:] = decay[...]


def intra_back_kernel(idx, d_mixer, pre_i, pre_p, aux, low, d_gate, d_scaled, d_maps, g_wg):
    @pl.when(pl.program_id(0) == 0)
    def _():
        g_wg[...] = jnp.zeros_like(g_wg)

    g_wg[...] += dot(low[...], d_gate[...], 0, 0)
    width = d_mixer.shape[1]
    base = idx[1] + pl.program_id(0) * BLOCK
    maps, _ = silu_parts(pre_p[...])
    values, _ = silu_parts(pre_i[...])
    for c in range(BLOCK // CHUNK):
        at = slice(c * CHUNK, (c + 1) * CHUNK)
        table = aux[at, :]
        rows = jnp.transpose(table)
        joined = masks(table, base + c * CHUNK, True)
        keys = maps[at, :LANES].astype(BF16)
        reads = maps[at, LANES:].astype(BF16)
        scores = dot(keys, reads, 1, 1)
        scaled = (values[at] * expand(table, DT, width)).astype(BF16)
        grads = d_mixer[at, :]
        d_scores = jnp.zeros((CHUNK, CHUNK), F32)
        parts = []
        for pair in range(width // LANES):
            split = head_split(grads, pair)
            d_weights = dot(scaled[:, pair * LANES : (pair + 1) * LANES], split, 1, 1)
            weights = []
            for side in range(2):
                h = 2 * pair + side
                gap = rows[CUM + h : CUM + h + 1, :] - table[:, CUM + h : CUM + h + 1]
                factor = jnp.exp(jnp.where(joined, gap, -1e30))
                weights.append((scores * factor).astype(BF16))
                d_scores = d_scores + factor * d_weights[:, side * CHUNK : (side + 1) * CHUNK]
            parts.append(dot(jnp.concatenate(weights, axis=1), split))
        d_scaled[at, :] = jnp.concatenate(parts, axis=1)
        low_scores = d_scores.astype(BF16)
        d_maps[at, :] = jnp.concatenate([dot(low_scores, reads), dot(low_scores, keys, 0, 0)], axis=1)


def conv_back(grad, within, inputs, edge_inputs, weight, shifted, first, last, acc):
    rows = grad.shape[0]

    @pl.when(first)
    def _():
        for ref in shifted:
            ref[...] = jnp.zeros_like(ref)

    total = grad * weight[3:4]
    edge = jnp.zeros((8, grad.shape[1]), F32)
    acc[3:4] += jnp.sum(grad * inputs, axis=0, keepdims=True)
    acc[4:5] += jnp.sum(grad, axis=0, keepdims=True)
    for k, ref in enumerate(shifted):
        ref[8 : 8 + rows] = grad * (within >= float(3 - k)).astype(F32)
        moved = ref[3 - k : 3 - k + 8 + rows]
        total = total + moved[8:] * weight[k : k + 1]
        edge = edge + moved[:8] * weight[k : k + 1]
        outer = jnp.where(last, edge_inputs, 0.0) * moved[:8]
        acc[k : k + 1] += jnp.sum(moved[8:] * inputs, axis=0, keepdims=True) + jnp.sum(outer, axis=0, keepdims=True)
        ref[8 + rows :] = ref[8:16]
    return total, edge


def scan_back_kernel(
    idx, d_scaled, d_maps, pre_i, pre_p, in_i, in_p, halo_i, halo_p, aux, gloc, pkl, gin, states, d_mixer, mixer, skip, dlog,
    conv_i, conv_p, d_inner, d_step, d_pair, edge, tail, small, small_p, heads, *shifted,
):
    step = pl.program_id(0)
    blocks = pl.num_programs(0)
    first, last = step == 0, step == blocks - 1
    width = mixer.shape[1]

    @pl.when(first)
    def _():
        small[...] = jnp.zeros_like(small)
        small_p[...] = jnp.zeros_like(small_p)
        heads[...] = jnp.zeros_like(heads)

    base = idx[1] + (blocks - 1 - step) * BLOCK
    maps, slope_p = silu_parts(pre_p[...])
    values, slope = silu_parts(pre_i[...])
    dy = d_mixer[...]
    upper = triangle(True)
    lane = lax.broadcasted_iota(jnp.int32, (CHUNK, LANES), 1)
    grown = jnp.exp(dlog[...])
    pieces, pieces_p = [], []
    for c in range(BLOCK // CHUNK):
        at = slice(c * CHUNK, (c + 1) * CHUNK)
        table = aux[at, :]
        sizes = expand(table, DT, width)
        inflow = expand(table, INFLOW, width)
        outflow = expand(table, TAIL, width)
        keys, reads = maps[at, :LANES], maps[at, LANES:]
        scaled = values[at] * sizes
        grad_state = gloc[c] + pkl[c, :1] * gin[...]
        state = states[c]
        passed = outflow * dot3(keys, grad_state)
        total = d_scaled[at, :] + passed
        d_reads = d_maps[at, LANES:] + dot3(dy[at] * inflow, state, 1, 1)
        d_keys = d_maps[at, :LANES] + dot3(scaled * outflow, grad_state, 1, 1)
        pieces_p.append(jnp.concatenate([d_keys, d_reads], axis=1))
        plain = mixer[at, :] - skip[...] * values[at]
        d_cum = head_sums(dy[at] * plain - scaled * total)
        carried = jnp.sum(grad_state * state, axis=0, keepdims=True) * inflow[CHUNK - 1 :]
        carried = carried + jnp.sum(scaled * passed, axis=0, keepdims=True)
        after = head_sums(jnp.broadcast_to(carried, (8, width)))[:1]
        d_logs = jnp.dot(upper, d_cum, precision=HIGHEST, preferred_element_type=F32) + after
        d_raw = (head_sums(total * values[at]) - grown * d_logs) * pltpu.roll(table, LANES - RATE, 1)
        d_raw = jnp.where(lane < 8, d_raw, 0.0)
        d_step[at, :] = d_raw.astype(BF16)
        d_decay = jnp.where(lane < 8, -d_logs * table * grown, 0.0)
        heads[0:1] += jnp.sum(d_raw, axis=0, keepdims=True)
        heads[1:2] += jnp.sum(d_decay, axis=0, keepdims=True)
        pieces.append(total * sizes + dy[at] * skip[...])
    small[5:6] += jnp.sum(dy * values, axis=0, keepdims=True)
    grad = jnp.concatenate(pieces, axis=0) * slope
    pos = (base + lax.broadcasted_iota(jnp.int32, (BLOCK, 1), 0)).astype(F32)
    within = pos - aux[:, START : START + 1]
    whole, outer = conv_back(
        grad, within, in_i[...].astype(F32), halo_i[8:].astype(F32), conv_i, shifted[:3], first, last, small
    )
    grad_p = jnp.concatenate(pieces_p, axis=0) * slope_p
    whole_p, outer_p = conv_back(
        grad_p, within, in_p[...].astype(F32), halo_p[8:].astype(F32), conv_p, shifted[3:], first, last, small_p
    )
    d_inner[...] = whole.astype(BF16)
    d_pair[...] = whole_p
    edge[...] = jnp.concatenate([outer, outer_p], axis=1)

    @pl.when(first)
    def _():
        tail[...] = jnp.concatenate([whole[BLOCK - 16 :], whole_p[BLOCK - 16 :]], axis=1)


def dot_split(a, b, da=1, db=0):
    high, low = halves(b)
    return dot(a, high, da, db) + dot(a, low, da, db)


def input_back_kernel(
    d_gate, d_inner, d_step, d_pair, wg, wi, ws, wp, edge, tail, mine, fix_i, fix_p,
    block_i, block_p, after, away, land, send_sem, land_sem, edge_send, edge_land,
):
    step = pl.program_id(0)
    blocks = pl.num_programs(0)
    seq, devices = lax.axis_index("seq"), lax.axis_size("seq")
    behind, ahead = lax.rem(seq + devices - 1, devices), lax.rem(seq + 1, devices)
    width = wi.shape[1]
    moved = pltpu.make_async_remote_copy(
        src_ref=edge, dst_ref=after, send_sem=edge_send, recv_sem=edge_land,
        device_id={"seq": behind}, device_id_type=pl.DeviceIdType.MESH,
    )

    @pl.when(step == 0)
    def _():
        enter([{"head": core_peer()}, {"seq": behind}, {"seq": ahead}])
        moved.start()

    block_i[...] = d_inner[...]
    block_p[...] = d_pair[...]
    block = lax.rem(step + blocks // 2 * (1 - core_bit()), blocks)

    @pl.when(block == blocks - 1)
    def _():
        moved.wait_recv()
        more = jnp.where(seq == devices - 1, 0.0, after[...])
        fixed = jnp.concatenate([tail[:8], tail[8:] + more], axis=0)
        fix_i[...] = fixed[:, :width].astype(BF16)
        fix_p[...] = fixed[:, width:]
        block_i[BLOCK - 16 :] = fixed[:, :width].astype(BF16)
        block_p[BLOCK - 16 :] = fixed[:, width:]

    part = dot(d_gate[...], wg[...], 1, 1) + dot(block_i[...], wi[...], 1, 1) + dot(d_step[...], ws[...], 1, 1)
    high, low = halves(block_p[...])
    part = part + (dot(high, wp[...], 1, 1) + dot(low, wp[...], 1, 1))
    add_halves(part, mine, away, land, send_sem, land_sem)

    @pl.when(step == blocks - 1)
    def _():
        moved.wait_send()


def pair_weight_kernel(low, d_step, d_pair, fix_p, g_ws, g_wp):
    step = pl.program_id(0)

    @pl.when(step == 0)
    def _():
        g_ws[...] = jnp.zeros_like(g_ws)
        g_wp[...] = jnp.zeros_like(g_wp)

    grads = jnp.where(step == pl.num_programs(0) - 1, fix_p[...], d_pair[BLOCK - 16 :])
    grads = jnp.concatenate([d_pair[: BLOCK - 16], grads], axis=0)
    g_ws[...] += dot(d_step[...], low[...], 0, 0)[:8]
    g_wp[...] += dot_split(low[...], grads, 0, 0)


def inner_weight_kernel(low, d_inner, fix_i, g_wi):
    step = pl.program_id(0)

    @pl.when(step == 0)
    def _():
        g_wi[...] = jnp.zeros_like(g_wi)

    grads = jnp.where(step == pl.num_programs(0) - 1, fix_i[...], d_inner[BLOCK - 16 :])
    grads = jnp.concatenate([d_inner[: BLOCK - 16], grads], axis=0)
    g_wi[...] += dot(low[...], grads, 0, 0)


def norm_back_kernel(
    mine, other, hid, d_out, gain, error, grad, sums, block, row, land, local, send, arrive, row_send, row_land
):
    step = pl.program_id(0)
    seq, devices = lax.axis_index("seq"), lax.axis_size("seq")
    head = lax.axis_index("head")
    group = 2 * devices
    me = 2 * seq + core_bit()

    def device(distance):
        to = lax.rem(me + distance, group)
        return {"seq": to // 2, "head": head - core_bit() + lax.rem(to, 2)}

    def hand(distance):
        return pltpu.make_async_remote_copy(
            src_ref=row, dst_ref=land.at[me], send_sem=row_send.at[distance], recv_sem=row_land.at[distance],
            device_id=device(distance), device_id_type=pl.DeviceIdType.MESH,
        )

    def each(body):
        def run(distance, carry):
            body(distance)
            return carry

        lax.fori_loop(1, group, run, 0)

    @pl.when(step == 0)
    def _():
        barrier = pltpu.get_barrier_semaphore()
        each(
            lambda d: pl.semaphore_signal(
                barrier, inc=1, device_id=device(d), device_id_type=pl.DeviceIdType.MESH
            )
        )
        pl.semaphore_wait(barrier, group - 1)
        row[:1] = jnp.zeros_like(row[:1])
        row[1:] = error[...]

    d_low = mine[...].astype(F32) + other[...].astype(F32)
    rows = hid[...].astype(F32)
    scale = lax.rsqrt(jnp.mean(rows * rows, axis=1, keepdims=True) + EPSILON)
    row[:1] += jnp.sum(d_low * rows * scale, axis=0, keepdims=True)
    scaled = d_low * gain[...]
    pull = jnp.mean(scaled * rows, axis=1, keepdims=True) * (scale * scale * scale)
    block[step] = (d_out[...] + scale * scaled - rows * pull).astype(BF16)

    @pl.when(step == pl.num_programs(0) - 1)
    def _():
        each(lambda d: hand(d).start())

    both_cores([block], [grad], [local, send, arrive])

    @pl.when(step == pl.num_programs(0) - 1)
    def _():
        land[me] = row[...]
        each(lambda d: hand(d).wait())
        sums[...] = lax.fori_loop(1, group, lambda d, total: total + land[d], land[0])


def call(kernel, grid, ins, outs, scratch=(), prefetch=0, flops=0, moved=0, collective=None, vmem=14):
    def spec(shape, block, index):
        if block is None:
            return pl.BlockSpec(shape, lambda *_: (0,) * len(shape))
        if isinstance(block, str):
            return pl.BlockSpec(memory_space=pltpu.SMEM if block == "smem" else pl.ANY)
        return pl.BlockSpec(block, index)

    scalars = [a for a, *_ in ins[:prefetch]]
    arrays = ins[prefetch:]
    extra = {} if collective is None else {"collective_id": collective, "has_side_effects": True}
    return pl.pallas_call(
        kernel,
        grid_spec=pltpu.PrefetchScalarGridSpec(
            num_scalar_prefetch=prefetch,
            grid=(grid,),
            in_specs=[spec(a.shape, block, index) for a, block, index in arrays],
            out_specs=[spec(shape, block, index) for shape, _, block, index in outs],
            scratch_shapes=list(scratch),
        ),
        out_shape=[jax.ShapeDtypeStruct(shape, dtype) for shape, dtype, _, _ in outs],
        compiler_params=pltpu.CompilerParams(
            dimension_semantics=("arbitrary",), vmem_limit_bytes=vmem << 20, **extra
        ),
        cost_estimate=pl.CostEstimate(flops=int(flops), bytes_accessed=int(moved), transcendentals=0),
    )(*scalars, *[a for a, *_ in arrays])


def swap(value, axis, bit):
    route = [(i, i ^ bit) for i in range(lax.axis_size(axis))]
    return jax.tree.map(lambda v: lax.ppermute(v, axis, route), value)


def shifted(value, axis, distance):
    devices = range(lax.axis_size(axis))
    route = [(i - distance, i) for i in devices if i - distance in devices]
    return lax.ppermute(value, axis, route)


def bits(axis):
    size = lax.axis_size(axis)
    return [1 << b for b in range(size.bit_length() - 1)]


def total_over(value, axis):
    for bit in bits(axis):
        value = value + swap(value, axis, bit)
    return value


def carried(total, axis, backward):
    mine = lax.axis_index(axis)

    def join(early, late):
        decay = late[CHUNK : CHUNK + 1]
        return jnp.concatenate([late[:CHUNK] + decay * early[:CHUNK], late[CHUNK:] * early[CHUNK:]])

    reached = jnp.concatenate([jnp.zeros_like(total[:CHUNK]), jnp.ones_like(total[CHUNK:])])
    for bit in bits(axis):
        other = swap(total, axis, bit)
        later = ((mine & bit) == 0) if backward else ((mine & bit) != 0)
        reached = jnp.where(later, join(other, reached), reached)
        total = jnp.where(later, join(other, total), join(total, other))
    return reached[:CHUNK]


def reduce_kernel(plain, wide, wires, axis, *refs):
    count = plain + wide
    take = iter(range(len(refs)))

    def some(number):
        return [refs[next(take)] for _ in range(number)]

    ins, outs = some(count), some(count)
    first, land1, second, land2, done = (some(count) for _ in range(5))
    fold1, half, fold2, quarter = (some(wide) for _ in range(4))
    sems = some(16)
    members = first[0].shape[0]
    me = lax.axis_index(axis)
    side, place = lax.rem(me, 2), me // 2
    partner = {axis: me + 1 - 2 * side}
    head = lax.axis_index("head")
    core, plane = lax.rem(head, 2), head // 2
    beside, across = {"head": head + 1 - 2 * core}, {"head": head + 2 - 4 * plane}
    source = ins[:plain] + quarter

    def copy(src, dst, sem, slot, to):
        return pltpu.make_async_remote_copy(
            src_ref=src, dst_ref=dst, send_sem=sems[2 * sem].at[slot], recv_sem=sems[2 * sem + 1].at[slot],
            device_id=to, device_id_type=pl.DeviceIdType.MESH,
        )

    def member(d):
        return lax.rem(place + d, members)

    def to_member(d):
        return {axis: 2 * member(d) + side}

    def halve(k):
        return copy(first[k], land1[k], 0, k, partner)

    def scatter(k, d):
        return copy(second[k].at[member(d)], land2[k].at[d], 1, k * members + d, to_member(d))

    def gather(k, d):
        return copy(done[k].at[side, place], done[k].at[side, place], 2, k * members + d, to_member(d))

    def gathered(k, d):
        other = lax.rem(place + members - d, members)
        return copy(done[k].at[side, other], done[k].at[side, other], 2, k * members + d, partner)

    def widen(k):
        return copy(done[k].at[side], done[k].at[side], 3, k, partner)

    def widened(k):
        return copy(done[k].at[1 - side], done[k].at[1 - side], 3, k, partner)

    def fold_core(w):
        return copy(ins[plain + w].at[1 - core], fold1[w], 4, w, beside)

    def fold_plane(w):
        return copy(half[w].at[1 - plane], fold2[w], 5, w, across)

    def spread_plane(w, at):
        ref = outs[plain + w].at[core, at]
        return copy(ref, ref, 6, w, across)

    def spread_core(w, at):
        ref = outs[plain + w].at[at]
        return copy(ref, ref, 7, w, beside)

    def each(body):
        def step(d, carry):
            body(d)
            return carry

        lax.fori_loop(1, members, step, 0)

    def split(k):
        first[k][...] = source[k][1 - side].astype(wires[k])

    def pass_on(k):
        halve(k).wait_recv()
        second[k][...] = (source[k][side] + land1[k][...].astype(F32)).astype(wires[k])
        each(lambda d: scatter(k, d).start())

    def finish(k):
        def add(d, total):
            scatter(k, d).wait_recv()
            return total + land2[k][d].astype(F32)

        total = lax.fori_loop(1, members, add, source[k][side, place] + land1[k][place].astype(F32))
        done[k][side, place] = total.astype(wires[k])
        each(lambda d: gather(k, d).start())

    def collect(k):
        each(lambda d: gathered(k, d).wait_recv())
        widen(k).start()

    def store(k, out):
        out[side] = done[k][side].astype(F32)
        widened(k).wait_recv()
        out[1 - side] = done[k][1 - side].astype(F32)

    barrier = pltpu.get_barrier_semaphore()

    def greet(to):
        pl.semaphore_signal(barrier, inc=1, device_id=to, device_id_type=pl.DeviceIdType.MESH)

    for to in (partner, beside, across):
        greet(to)
    each(lambda d: greet(to_member(d)))
    for k in range(plain):
        split(k)
    pl.semaphore_wait(barrier, members + 2)
    for w in range(wide):
        fold_core(w).start()
    halve(0).start()
    for k in range(plain):
        if k + 1 < plain:
            halve(k + 1).start()
        pass_on(k)
        if k == 0:
            for w in range(wide):
                fold_core(w).wait_recv()
                half[w][...] = ins[plain + w][core] + fold1[w][...]
                fold_plane(w).start()
    for k in range(plain):
        finish(k)
    for w in range(wide):
        fold_plane(w).wait_recv()
        quarter[w][...] = half[w][plane] + fold2[w][...]
        split(plain + w)
        halve(plain + w).start()
    for k in range(plain):
        collect(k)
    for w in range(wide):
        pass_on(plain + w)
    for k in range(plain):
        store(k, outs[k])
    for w in range(wide):
        finish(plain + w)
    for w in range(wide):
        collect(plain + w)
    for w in range(wide):
        store(plain + w, outs[plain + w].at[core, plane])
        spread_plane(w, plane).start()
    for w in range(wide):
        spread_plane(w, 1 - plane).wait_recv()
        spread_core(w, core).start()
    for w in range(wide):
        spread_core(w, 1 - core).wait_recv()
        fold_core(w).wait_send()
        fold_plane(w).wait_send()
        spread_plane(w, plane).wait_send()
        spread_core(w, core).wait_send()
    for k in range(count):
        halve(k).wait_send()
        widen(k).wait_send()

        def drain(d, k=k):
            scatter(k, d).wait_send()
            gather(k, d).wait_send()

        each(drain)


def reduce_over(arrays, wires, wide_arrays, axis, collective):
    size = lax.axis_size(axis)
    members = size // 2
    split = [a.reshape(2, members, a.shape[0] // size, a.shape[1]) for a in arrays]
    split += [a.reshape(2, 2, 2, members, a.shape[0] // (4 * size), a.shape[1]) for a in wide_arrays]
    plain, wide = len(arrays), len(wide_arrays)
    wires = list(wires) + [F32] * wide
    n = plain + wide
    vmem = pl.BlockSpec(memory_space=pltpu.VMEM)
    moved = sum(a.size * 4 for a in split)
    tail = [a.shape[-3:] for a in split]
    part = [pltpu.VMEM(shape, w) for shape, w in zip(tail, wires)]
    last = [a.shape for a in split[plain:]]
    dma = pltpu.SemaphoreType.DMA
    outs = pl.pallas_call(
        partial(reduce_kernel, plain, wide, wires, axis),
        out_shape=[jax.ShapeDtypeStruct(a.shape, F32) for a in split],
        in_specs=[vmem] * n,
        out_specs=[vmem] * n,
        scratch_shapes=part * 4
        + [pltpu.VMEM((2,) + shape, w) for shape, w in zip(tail, wires)]
        + [pltpu.VMEM(shape[1:], F32) for shape in last] * 2
        + [pltpu.VMEM(shape[2:], F32) for shape in last] * 2
        + [dma((n,))] * 2 + [dma((n * members,))] * 4 + [dma((n,))] * 2 + [dma((wide,))] * 8,
        compiler_params=pltpu.CompilerParams(
            collective_id=collective, has_side_effects=True, vmem_limit_bytes=24 << 20
        ),
        cost_estimate=pl.CostEstimate(flops=0, bytes_accessed=40 * moved, transcendentals=0),
    )(*split)
    return [o.reshape(a.shape) for o, a in zip(outs, list(arrays) + list(wide_arrays))]


def padded(row, lanes=LANES):
    return jnp.zeros((1, lanes), F32).at[0, : row.shape[0]].set(row)


def shards(
    hidden, teacher, doc_starts, valid_mask, norm_gain, w_gate, w_inner, w_pair, w_step, conv_inner, bias_inner,
    conv_pair, bias_pair, step_bias, decay_log, skip_gain, gate_gain, w_output,
):
    rows, model = hidden.shape
    width = w_inner.shape[1]
    pair_width = w_pair.shape[1]
    heads = step_bias.shape[0]
    blocks, chunks = rows // BLOCK, rows // CHUNK
    per = BLOCK // CHUNK
    half = blocks // 2
    inner_total = float(width * lax.axis_size("head"))
    core = lax.axis_index("head") & 1
    offset = lax.axis_index("seq") * rows
    idx = jnp.stack([core, offset]).astype(jnp.int32)
    edge_rows = 16

    starts = jnp.full((1, LANES), FAR, F32).at[0, : doc_starts.shape[0]].set(doc_starts.astype(F32))
    ws = jnp.zeros((model, LANES), BF16).at[:, :heads].set(w_step)
    sbias, dlog = padded(step_bias), padded(decay_log)
    skip = jnp.repeat(skip_gain, HEAD_DIM)[None, :]
    gain, out_gain = norm_gain[None, :], gate_gain[None, :]
    conv_i, conv_p = conv_inner.astype(F32), conv_pair.astype(F32)
    bias_i, bias_p = bias_inner.astype(F32)[None, :], bias_pair.astype(F32)[None, :]
    valid = valid_mask[None, :]

    tail = shifted(hidden[rows - edge_rows :], "seq", 1)
    count = total_over(jnp.full((8, LANES), jnp.sum(valid_mask.astype(F32))), "seq")[0, 0]
    factor = (rows * lax.axis_size("seq")) / count

    def by(w, column=0):
        return (BLOCK, w), lambda i, *_: (i, column)

    def back(w, column=0):
        return (BLOCK, w), lambda i, *_: (blocks - 1 - i, column)

    row = ((1, BLOCK), lambda i, *_: (0, i))
    row_back = ((1, BLOCK), lambda i, *_: (0, blocks - 1 - i))
    grid3 = lambda n: ((per, n, width), lambda i, *_: (i, 0, 0))
    back3 = lambda n: ((per, n, width), lambda i, *_: (blocks - 1 - i, 0, 0))
    whole = (None, None)

    def send_order(w):
        return (BLOCK, w), lambda i: (lax.rem(i + half * (1 - core_bit()), blocks), 0)

    send_row = ((1, BLOCK), lambda i: (0, lax.rem(i + half * (1 - core_bit()), blocks)))
    half_own = lambda w: ((BLOCK, w), lambda i: (i + half * core_bit(), 0))
    tail_half = lambda w: ((BLOCK, w), lambda i: (jnp.maximum(i - half, 0), 0))
    dma = pltpu.SemaphoreType.DMA
    swap_scratch = [pltpu.VMEM((half, BLOCK, model), BF16)] * 2 + [dma((half,))] * 2

    halo_block = ((edge_rows, model), lambda i, *_: (jnp.maximum(i * (BLOCK // edge_rows) - 1, 0), 0))
    (low, in_i, in_p, pre_i, pre_p, aux, halo_i, halo_p, sloc, pkl, fin) = call(
        project_kernel,
        blocks,
        [
            (idx, None, None), (starts, *whole), (hidden, *by(model)), (hidden, *halo_block), (tail, *whole),
            (gain, *whole), (w_inner, *whole), (w_pair, *whole), (ws, *whole), (conv_i, *whole), (conv_p, *whole),
            (bias_i, *whole), (bias_p, *whole), (sbias, *whole), (dlog, *whole),
        ],
        [
            ((rows, model), BF16, *by(model)), ((rows, width), BF16, *by(width)), ((rows, pair_width), BF16, *by(pair_width)),
            ((rows, width), F32, *by(width)), ((rows, pair_width), F32, *by(pair_width)), ((rows, LANES), F32, *by(LANES)),
            ((edge_rows, width), BF16, *whole), ((edge_rows, pair_width), BF16, *whole),
            ((chunks, CHUNK, width), F32, *grid3(CHUNK)), ((chunks, 8, width), F32, *grid3(8)),
            ((CHUNK + 8, width), F32, *whole),
        ],
        [
            pltpu.VMEM((BLOCK + edge_rows, width), F32), pltpu.VMEM((BLOCK + edge_rows, pair_width), F32),
            pltpu.VMEM((CHUNK, width), F32), pltpu.VMEM((8, width), F32),
        ],
        prefetch=1, flops=3e9, moved=2e7,
    )
    state_in = carried(fin, "seq", False)
    gate, local = call(
        intra_kernel,
        blocks,
        [
            (idx, None, None), (low, *by(model)), (w_gate, *whole), (pre_i, *by(width)), (pre_p, *by(pair_width)),
            (aux, *by(LANES)), (skip, *whole),
        ],
        [((rows, width), F32, *by(width)), ((rows, width), F32, *by(width))],
        prefetch=1, flops=4e9, moved=2e7,
    )
    mixer, states, square = call(
        mix_kernel,
        blocks,
        [
            (pre_p, *by(LANES, 1)), (aux, *by(LANES)), (sloc, *grid3(CHUNK)), (pkl, *grid3(8)), (state_in, *whole),
            (local, *by(width)), (gate, *by(width)),
        ],
        [((rows, width), F32, *by(width)), ((chunks, CHUNK, width), F32, *grid3(CHUNK)), ((1, rows), F32, *row)],
        flops=1e9, moved=2e7,
    )
    square = total_over(square, "head")
    (mine,) = call(
        partial(branch_kernel, total=inner_total),
        blocks,
        [
            (mixer, *send_order(width)), (gate, *send_order(width)), (square, *send_row), (out_gain, *whole), (w_output, *whole),
        ],
        [((rows // 2, model), BF16, *tail_half(model))],
        swap_scratch,
        flops=1.2e9, moved=1e7, collective=2,
    )
    other = swap(mine, "head", 2)
    output, d_branch, d_out, error = call(
        loss_kernel,
        half,
        [
            (factor.reshape(1), "smem", None), (hidden, *half_own(model)), (teacher, *half_own(model)),
            (valid, (1, BLOCK), lambda i: (0, i + half * core_bit())), (mine, *by(model)), (other, *by(model)),
        ],
        [
            ((rows, model), BF16, "any", None), ((rows, model), BF16, "any", None),
            ((rows // 2, model), F32, *by(model)), ((1, model), F32, *whole),
        ],
        [pltpu.VMEM((half, BLOCK, model), BF16)] * 2 + [dma((2 * half,))] * 3,
        flops=1e8, moved=1.5e7, collective=3,
    )
    weighted, cross, g_gain, g_wo = call(
        partial(branch_back_kernel, total=inner_total),
        blocks,
        [
            (d_branch, *by(model)), (mixer, *by(width)), (gate, *by(width)), (square, *row), (out_gain, *whole),
            (w_output, *whole),
        ],
        [
            ((rows, width), F32, *by(width)), ((1, rows), F32, *row), ((1, width), F32, *whole),
            ((width, model), F32, *whole),
        ],
        flops=2.4e9, moved=1.5e7,
    )
    cross = total_over(cross, "head")
    d_mixer, d_gate, gloc, pkb, fin_back = call(
        partial(gate_back_kernel, total=inner_total),
        blocks,
        [
            (weighted, *back(width)), (mixer, *back(width)), (gate, *back(width)), (square, *row_back), (cross, *row_back),
            (pre_p, *back(LANES, 1)), (aux, *back(LANES)),
        ],
        [
            ((rows, width), F32, *back(width)), ((rows, width), BF16, *back(width)),
            ((chunks, CHUNK, width), F32, *back3(CHUNK)), ((chunks, 8, width), F32, *back3(8)), ((CHUNK + 8, width), F32, *whole),
        ],
        [pltpu.VMEM((CHUNK, width), F32), pltpu.VMEM((8, width), F32)],
        flops=1e9, moved=2e7,
    )
    grad_in = carried(fin_back, "seq", True)
    d_scaled, d_maps, g_wg = call(
        intra_back_kernel,
        blocks,
        [
            (idx, None, None), (d_mixer, *by(width)), (pre_i, *by(width)), (pre_p, *by(pair_width)), (aux, *by(LANES)),
            (low, *by(model)), (d_gate, *by(width)),
        ],
        [((rows, width), F32, *by(width)), ((rows, pair_width), F32, *by(pair_width)), ((model, width), F32, *whole)],
        prefetch=1, flops=6e9, moved=2e7,
    )
    both = width + pair_width
    d_inner, d_step, d_pair, edge, tail, small_i, small_p, head_small = call(
        scan_back_kernel,
        blocks,
        [
            (idx, None, None), (d_scaled, *back(width)), (d_maps, *back(pair_width)), (pre_i, *back(width)),
            (pre_p, *back(pair_width)), (in_i, *back(width)), (in_p, *back(pair_width)), (halo_i, *whole), (halo_p, *whole),
            (aux, *back(LANES)), (gloc, *back3(CHUNK)), (pkb, *back3(8)), (grad_in, *whole), (states, *back3(CHUNK)),
            (d_mixer, *back(width)), (mixer, *back(width)), (skip, *whole), (dlog, *whole), (conv_i, *whole), (conv_p, *whole),
        ],
        [
            ((rows, width), BF16, *back(width)), ((rows, LANES), BF16, *back(LANES)), ((rows, pair_width), F32, *back(pair_width)),
            ((8, both), F32, *whole), ((16, both), F32, *whole), ((8, width), F32, *whole), ((8, pair_width), F32, *whole),
            ((8, LANES), F32, *whole),
        ],
        [pltpu.VMEM((BLOCK + 16, width), F32)] * 3 + [pltpu.VMEM((BLOCK + 16, pair_width), F32)] * 3,
        prefetch=1, flops=3e9, moved=3e7, vmem=16,
    )
    mine, fix_i, fix_p = call(
        input_back_kernel,
        blocks,
        [
            (d_gate, *send_order(width)), (d_inner, *send_order(width)), (d_step, *send_order(LANES)),
            (d_pair, *send_order(pair_width)), (w_gate, *whole), (w_inner, *whole), (ws, *whole), (w_pair, *whole),
            (edge, *whole), (tail, *whole),
        ],
        [
            ((rows // 2, model), BF16, *tail_half(model)), ((16, width), BF16, *whole), ((16, pair_width), F32, *whole),
        ],
        [pltpu.VMEM((BLOCK, width), BF16), pltpu.VMEM((BLOCK, pair_width), F32), pltpu.VMEM((8, both), F32)]
        + swap_scratch + [dma] * 2,
        flops=2.6e9, moved=1e7, collective=4,
    )
    other = swap(mine, "head", 2)
    g_ws, g_wp = call(
        pair_weight_kernel,
        blocks,
        [(low, *by(model)), (d_step, *by(LANES)), (d_pair, *by(pair_width)), (fix_p, *whole)],
        [((8, model), F32, *whole), ((model, pair_width), F32, *whole)],
        flops=1.6e9, moved=1e7,
    )
    (g_wi,) = call(
        inner_weight_kernel,
        blocks,
        [(low, *by(model)), (d_inner, *by(width)), (fix_i, *whole)],
        [((model, width), F32, *whole)],
        flops=1.2e9, moved=1e7,
    )
    pack = jnp.concatenate([
        small_i[:6], g_gain, jnp.zeros((1, width), F32), g_ws[:, :width], g_ws[:, width:],
        jnp.pad(head_small, ((0, 32), (0, width - LANES))),
    ])
    quarters = 4 * lax.axis_size("seq")
    small_p = jnp.pad(small_p, ((0, quarters - 8), (0, 0)))
    g_wo, g_wg, g_wi, pack, g_wp, small_p = reduce_over(
        [g_wo, g_wg, g_wi, pack], [BF16, BF16, BF16, F32], [g_wp, small_p], "seq", 1
    )
    grad_hidden, sums = call(
        norm_back_kernel,
        half,
        [
            (mine, *by(model)), (other, *by(model)), (hidden, *half_own(model)), (d_out, *by(model)), (gain, *whole),
            (error, *whole),
        ],
        [((rows, model), BF16, "any", None), ((2, model), F32, *whole)],
        [
            pltpu.VMEM((half, BLOCK, model), BF16), pltpu.VMEM((2, model), F32),
            pltpu.VMEM((2 * lax.axis_size("seq"), 2, model), F32),
        ]
        + [dma((half,))] * 3 + [dma((2 * lax.axis_size("seq"),))] * 2,
        flops=5e8, moved=1e7, collective=5,
    )
    by_head, g_ws = pack[:8], jnp.concatenate([pack[8:16], pack[16:24]], axis=1)[:heads].T
    pair_small, head_small = small_p[:8], pack[24:32, :LANES]
    loss = jnp.sum(sums[1]) / (count * model)
    return (
        output, loss, grad_hidden, sums[0], g_wg, g_wi, g_wp, g_ws, by_head[:4], by_head[4], pair_small[:4], pair_small[4],
        head_small[0, :heads], head_small[1, :heads], jnp.sum(by_head[5].reshape(heads, HEAD_DIM), axis=1), by_head[6], g_wo,
    )


def solution(mesh):
    seq, head, wide = P("seq", None), P("head"), P(None, "head")
    in_specs = (
        seq, seq, P(), P("seq"), P(), wide, wide, P(), wide, wide, head, P(), P(), head, head, head, head, P("head", None),
    )
    out_specs = (
        seq, P(), seq, P(), wide, wide, P(), wide, wide, head, P(), P(), head, head, head, head, P("head", None),
    )
    return jax.shard_map(shards, mesh=mesh, in_specs=in_specs, out_specs=out_specs, check_vma=False)
```

```python
from functools import partial

import jax
import jax.numpy as jnp
from jax import lax
from jax.experimental import pallas as pl
from jax.experimental.pallas import tpu as pltpu
from jax.sharding import PartitionSpec as P

EPSILON = 1e-05
CHUNK = 128
BLOCK = 256
HEAD_DIM = 64
LANES = 128
FAR = float(1 << 24)
F32 = jnp.float32
BF16 = jnp.bfloat16
HIGHEST = lax.Precision.HIGHEST

DT, CUM, INFLOW, TAIL, RATE, START, END = 0, 8, 16, 24, 32, 40, 41


def dot(a, b, da=1, db=0):
    return lax.dot_general(a, b, (((da,), (db,)), ((), ())), preferred_element_type=F32)


def halves(v):
    high = v.astype(BF16)
    return high, (v - high.astype(F32)).astype(BF16)


def dot3(a, b, da=1, db=0):
    ah, al = halves(a)
    bh, bl = halves(b)
    return dot(ah, bh, da, db) + (dot(ah, bl, da, db) + dot(al, bh, da, db))


def column_sums(v):
    high, low = halves(v)
    ones = jnp.ones((8, v.shape[1]), BF16)
    return (dot(ones, high, 1, 1) + dot(ones, low, 1, 1))[:1]


def as_column(row):
    return jnp.transpose(jnp.broadcast_to(row, (8, row.shape[1])))[:, :1]


def expand(table, base, width):
    rows = table.shape[0]
    lane = lax.broadcasted_iota(jnp.int32, (rows, LANES), 1)
    parts = []
    for pair in range(width // LANES):
        first = jnp.broadcast_to(table[:, base + 2 * pair : base + 2 * pair + 1], (rows, LANES))
        second = jnp.broadcast_to(table[:, base + 2 * pair + 1 : base + 2 * pair + 2], (rows, LANES))
        parts.append(jnp.where(lane < HEAD_DIM, first, second))
    return jnp.concatenate(parts, axis=1)


def head_matrix(width):
    channel = lax.broadcasted_iota(jnp.int32, (width, LANES), 0)
    head = lax.broadcasted_iota(jnp.int32, (width, LANES), 1)
    return ((channel >> 6) == head).astype(BF16)


def head_sums(v):
    high, low = halves(v)
    matrix = head_matrix(v.shape[1])
    return dot(high, matrix) + dot(low, matrix)


def triangle(upper):
    row = lax.broadcasted_iota(jnp.int32, (CHUNK, CHUNK), 0)
    col = lax.broadcasted_iota(jnp.int32, (CHUNK, CHUNK), 1)
    return ((col >= row) if upper else (col <= row)).astype(F32)


def silu_parts(pre):
    gate = jax.nn.sigmoid(pre)
    return pre * gate, gate * (1.0 + pre * (1.0 - gate))


def project_kernel(
    idx, starts, hid, halo, tail, gain, wi, wp, ws, conv_i, conv_p, bias_i, bias_p, sbias, dlog,
    low, in_i, in_p, pre_i, pre_p, aux, halo_i, halo_p, sloc, pkl, fin, wide_i, wide_p, state, decay,
):
    step = pl.program_id(0)
    edge = tail.shape[0]
    width = wi.shape[1]

    @pl.when(step == 0)
    def _():
        state[...] = jnp.zeros_like(state)
        decay[...] = jnp.ones_like(decay)

    before = jnp.where(step == 0, tail[...].astype(F32), halo[...].astype(F32))
    rows = jnp.concatenate([before, hid[...].astype(F32)], axis=0)
    scale = lax.rsqrt(jnp.mean(rows * rows, axis=1, keepdims=True) + EPSILON)
    lowered = (rows * scale * gain[...]).astype(BF16)
    own = lowered[edge:]
    low[...] = own
    inner = dot(lowered, wi[...]).astype(BF16)
    pair = dot(lowered, wp[...]).astype(BF16)
    in_i[...] = inner[edge:]
    in_p[...] = pair[edge:]
    wide_i[...] = inner.astype(F32)
    wide_p[...] = pair.astype(F32)

    @pl.when(step == 0)
    def _():
        halo_i[...] = inner[:edge]
        halo_p[...] = pair[:edge]

    base = idx[1] + step * BLOCK
    pos = (base + lax.broadcasted_iota(jnp.int32, (BLOCK, LANES), 0)).astype(F32)
    begun = starts[...] <= pos
    start = jnp.max(jnp.where(begun, starts[...], -1.0), axis=1, keepdims=True)
    end = jnp.min(jnp.where(begun, FAR, starts[...]), axis=1, keepdims=True)
    within = pos[:, :1] - start
    keep = [(within >= float(3 - k)).astype(F32) for k in range(3)]

    def convolve(wide, weight, bias):
        total = bias[...] + wide[edge : edge + BLOCK] * weight[3:4]
        for k in range(3):
            total = total + wide[edge - 3 + k : edge - 3 + k + BLOCK] * weight[k : k + 1] * keep[k]
        return total

    conv_inner = convolve(wide_i, conv_i, bias_i)
    conv_pair = convolve(wide_p, conv_p, bias_p)
    pre_i[...] = conv_inner
    pre_p[...] = conv_pair
    values = conv_inner * jax.nn.sigmoid(conv_inner)
    maps = conv_pair[:, :LANES]
    maps = maps * jax.nn.sigmoid(maps)

    raw = dot(own, ws[...]) + sbias[...]
    dt = jnp.maximum(raw, 0.0) + jnp.log1p(jnp.exp(-jnp.abs(raw)))
    rate = jax.nn.sigmoid(raw)
    logs = -dt * jnp.exp(dlog[...])
    lane = lax.broadcasted_iota(jnp.int32, (CHUNK, LANES), 1)
    lower = triangle(False)
    for c in range(BLOCK // CHUNK):
        at = slice(c * CHUNK, (c + 1) * CHUNK)
        cum = jnp.dot(lower, logs[at], precision=HIGHEST, preferred_element_type=F32)
        last = cum[CHUNK - 1 :]
        first = (base + c * CHUNK).astype(F32)
        inflow = jnp.exp(cum) * (start[at] <= first - 1.0).astype(F32)
        outflow = jnp.exp(last - cum) * (end[at] > first + (CHUNK - 1.0)).astype(F32)
        table = jnp.where(lane < CUM, dt[at], pltpu.roll(cum, CUM, 1))
        table = jnp.where(lane < INFLOW, table, pltpu.roll(inflow, INFLOW, 1))
        table = jnp.where(lane < TAIL, table, pltpu.roll(outflow, TAIL, 1))
        table = jnp.where(lane < RATE, table, pltpu.roll(rate[at], RATE, 1))
        table = jnp.where(lane < START, table, jnp.where(lane < END, start[at], end[at]))
        aux[at, :] = table
        scaled = values[at] * expand(table, DT, width) * expand(table, TAIL, width)
        added = dot3(maps[at], scaled, 0, 0)
        kept = expand(jnp.broadcast_to(inflow[CHUNK - 1 :], (8, LANES)), 0, width)
        sloc[c] = state[...]
        pkl[c] = decay[...]
        state[...] = state[...] * kept[:1] + added
        decay[...] = decay[...] * kept
    fin[:CHUNK] = state[...]
    fin[CHUNK:] = decay[...]


def masks(table, first, transposed):
    row = lax.broadcasted_iota(jnp.int32, (CHUNK, CHUNK), 0)
    col = lax.broadcasted_iota(jnp.int32, (CHUNK, CHUNK), 1)
    at = (first + col).astype(F32)
    if transposed:
        return (col >= row) & (at < table[:, END : END + 1])
    return (col <= row) & (at >= table[:, START : START + 1])


def head_split(v, pair):
    lane = lax.broadcasted_iota(jnp.int32, (v.shape[0], LANES), 1)
    part = v[:, pair * LANES : (pair + 1) * LANES]
    return jnp.concatenate(
        [jnp.where(lane < HEAD_DIM, part, 0.0), jnp.where(lane < HEAD_DIM, 0.0, part)], axis=0
    ).astype(BF16)


def intra_kernel(idx, low, wg, pre_i, pre_p, aux, skip, gate, mixed):
    width = wg.shape[1]
    gate[...] = dot(low[...], wg[...])
    base = idx[1] + pl.program_id(0) * BLOCK
    maps, _ = silu_parts(pre_p[...])
    values, _ = silu_parts(pre_i[...])
    for c in range(BLOCK // CHUNK):
        at = slice(c * CHUNK, (c + 1) * CHUNK)
        table = aux[at, :]
        rows = jnp.transpose(table)
        joined = masks(table, base + c * CHUNK, False)
        scores = dot(maps[at, LANES:].astype(BF16), maps[at, :LANES].astype(BF16), 1, 1)
        scaled = values[at] * expand(table, DT, width)
        parts = []
        for pair in range(width // LANES):
            weights = []
            for h in (2 * pair, 2 * pair + 1):
                gap = table[:, CUM + h : CUM + h + 1] - rows[CUM + h : CUM + h + 1, :]
                weights.append((scores * jnp.exp(jnp.where(joined, gap, -1e30))).astype(BF16))
            parts.append(dot(jnp.concatenate(weights, axis=1), head_split(scaled, pair)))
        mixed[at, :] = jnp.concatenate(parts, axis=1) + values[at] * skip[...]


def mix_kernel(pre_c, aux, sloc, pkl, sin, local, gate, mixer, states, square):
    width = local.shape[1]
    reads, _ = silu_parts(pre_c[...])
    for c in range(BLOCK // CHUNK):
        at = slice(c * CHUNK, (c + 1) * CHUNK)
        state = sloc[c] + pkl[c, :1] * sin[...]
        states[c] = state
        mixer[at, :] = local[at, :] + expand(aux[at, :], INFLOW, width) * dot3(reads[at], state)
    act, _ = silu_parts(gate[...])
    gated = mixer[...] * act
    square[...] = column_sums(gated * gated)


def gate_scale(square, total):
    return as_column(lax.rsqrt(square / total + EPSILON))


def core_bit():
    return lax.rem(lax.axis_index("head"), 2)


def core_peer():
    return lax.axis_index("head") + 1 - 2 * core_bit()


def enter(peers):
    barrier = pltpu.get_barrier_semaphore()
    for peer in peers:
        pl.semaphore_signal(barrier, inc=1, device_id=peer, device_id_type=pl.DeviceIdType.MESH)
    pl.semaphore_wait(barrier, len(peers))


def to_peer(src, dst, sends, lands, slot):
    return pltpu.make_async_remote_copy(
        src_ref=src, dst_ref=dst, send_sem=sends.at[slot], recv_sem=lands.at[slot],
        device_id={"head": core_peer()}, device_id_type=pl.DeviceIdType.MESH,
    )


def add_halves(part, mine, away, land, send_sem, land_sem):
    step = pl.program_id(0)
    half = pl.num_programs(0) // 2

    def copy(slot):
        return to_peer(away.at[slot], land.at[slot], send_sem, land_sem, slot)

    @pl.when(step < half)
    def _():
        away[step] = part.astype(away.dtype)
        copy(step).start()

    @pl.when(step >= half)
    def _():
        copy(step - half).wait_recv()
        mine[...] = (part + land[step - half].astype(F32)).astype(mine.dtype)

    @pl.when(step == 2 * half - 1)
    def _():
        def drain(slot, carry):
            copy(slot).wait_send()
            return carry

        lax.fori_loop(0, half, drain, 0)


def branch_kernel(mixer, gate, square, gain, wo, mine, away, land, send_sem, land_sem, *, total):
    @pl.when(pl.program_id(0) == 0)
    def _():
        enter([{"head": core_peer()}])

    act, _ = silu_parts(gate[...])
    gated = mixer[...] * act
    normed = (gated * gate_scale(square[...], total) * gain[...]).astype(BF16)
    add_halves(dot(normed, wo[...]), mine, away, land, send_sem, land_sem)


def both_cores(buffers, wholes, sems):
    step = pl.program_id(0)
    half = pl.num_programs(0)
    local, send, land = sems

    def copies(k, slot):
        rows = pl.ds(pl.multiple_of((core_bit() * half + slot) * BLOCK, BLOCK), BLOCK)
        here = pltpu.make_async_copy(buffers[k].at[slot], wholes[k].at[rows], local.at[k * half + slot])
        there = to_peer(buffers[k].at[slot], wholes[k].at[rows], send, land, k * half + slot)
        return here, there

    for k in range(len(wholes)):
        for copy in copies(k, step):
            copy.start()

    @pl.when(step == half - 1)
    def _():
        for k in range(len(wholes)):

            def drain(slot, carry, k=k):
                here, there = copies(k, slot)
                here.wait()
                there.wait()
                return carry

            lax.fori_loop(0, half, drain, 0)


def loss_kernel(factor, hid, teacher, valid, mine, other, out, d_branch, d_out, error, out_block, grad_block, *sems):
    step = pl.program_id(0)

    @pl.when(step == 0)
    def _():
        error[...] = jnp.zeros_like(error)
        enter([{"head": core_peer()}])

    outf = hid[...].astype(F32) + (mine[...].astype(F32) + other[...].astype(F32))
    term = outf - teacher[...].astype(F32)
    masked = as_column(valid[...].astype(F32)) * term
    error[...] += jnp.sum(masked * term, axis=0, keepdims=True)
    grad = masked * factor[0]
    d_out[...] = grad
    out_block[step] = outf.astype(BF16)
    grad_block[step] = grad.astype(BF16)
    both_cores([out_block, grad_block], [out, d_branch], sems)


def branch_back_kernel(d_branch, mixer, gate, square, gain, wo, weighted, cross, g_gain, g_wo, *, total):
    step = pl.program_id(0)

    @pl.when(step == 0)
    def _():
        g_gain[...] = jnp.zeros_like(g_gain)
        g_wo[...] = jnp.zeros_like(g_wo)

    act, _ = silu_parts(gate[...])
    gated = mixer[...] * act
    scaled = gated * gate_scale(square[...], total)
    normed = (scaled * gain[...]).astype(BF16)
    g_wo[...] += dot(normed, d_branch[...], 0, 0)
    d_normed = dot(d_branch[...], wo[...], 1, 1)
    g_gain[...] += jnp.sum(d_normed * scaled, axis=0, keepdims=True)
    grad = d_normed * gain[...]
    weighted[...] = grad
    cross[...] = column_sums(grad * gated)


def gate_back_kernel(
    weighted, mixer, gate, square, cross, pre_c, aux, d_mixer, d_gate, gloc, pkl, fin, state, decay, *, total
):
    @pl.when(pl.program_id(0) == 0)
    def _():
        state[...] = jnp.zeros_like(state)
        decay[...] = jnp.ones_like(decay)

    width = mixer.shape[1]
    act, slope = silu_parts(gate[...])
    gated = mixer[...] * act
    row = lax.rsqrt(square[...] / total + EPSILON)
    scale = as_column(row)
    pull = as_column(row * row * row * cross[...] / total)
    d_gated = scale * weighted[...] - gated * pull
    dy = d_gated * act
    d_mixer[...] = dy
    d_gate[...] = (d_gated * mixer[...] * slope).astype(BF16)
    reads, _ = silu_parts(pre_c[...])
    for c in reversed(range(BLOCK // CHUNK)):
        at = slice(c * CHUNK, (c + 1) * CHUNK)
        inflow = expand(aux[at, :], INFLOW, width)
        gloc[c] = state[...]
        pkl[c] = decay[...]
        kept = inflow[CHUNK - 1 :]
        state[...] = state[...] * kept + dot3(reads[at], dy[at] * inflow, 0, 0)
        decay[...] = decay[...] * kept
    fin[:CHUNK] = state[...]
    fin[CHUNK:] = decay[...]


def intra_back_kernel(idx, d_mixer, pre_i, pre_p, aux, low, d_gate, d_scaled, d_maps, g_wg):
    @pl.when(pl.program_id(0) == 0)
    def _():
        g_wg[...] = jnp.zeros_like(g_wg)

    g_wg[...] += dot(low[...], d_gate[...], 0, 0)
    width = d_mixer.shape[1]
    base = idx[1] + pl.program_id(0) * BLOCK
    maps, _ = silu_parts(pre_p[...])
    values, _ = silu_parts(pre_i[...])
    for c in range(BLOCK // CHUNK):
        at = slice(c * CHUNK, (c + 1) * CHUNK)
        table = aux[at, :]
        rows = jnp.transpose(table)
        joined = masks(table, base + c * CHUNK, True)
        keys = maps[at, :LANES].astype(BF16)
        reads = maps[at, LANES:].astype(BF16)
        scores = dot(keys, reads, 1, 1)
        scaled = (values[at] * expand(table, DT, width)).astype(BF16)
        grads = d_mixer[at, :]
        d_scores = jnp.zeros((CHUNK, CHUNK), F32)
        parts = []
        for pair in range(width // LANES):
            split = head_split(grads, pair)
            d_weights = dot(scaled[:, pair * LANES : (pair + 1) * LANES], split, 1, 1)
            weights = []
            for side in range(2):
                h = 2 * pair + side
                gap = rows[CUM + h : CUM + h + 1, :] - table[:, CUM + h : CUM + h + 1]
                factor = jnp.exp(jnp.where(joined, gap, -1e30))
                weights.append((scores * factor).astype(BF16))
                d_scores = d_scores + factor * d_weights[:, side * CHUNK : (side + 1) * CHUNK]
            parts.append(dot(jnp.concatenate(weights, axis=1), split))
        d_scaled[at, :] = jnp.concatenate(parts, axis=1)
        low_scores = d_scores.astype(BF16)
        d_maps[at, :] = jnp.concatenate([dot(low_scores, reads), dot(low_scores, keys, 0, 0)], axis=1)


def conv_back(grad, within, inputs, edge_inputs, weight, shifted, first, last, acc):
    rows = grad.shape[0]

    @pl.when(first)
    def _():
        for ref in shifted:
            ref[...] = jnp.zeros_like(ref)

    total = grad * weight[3:4]
    edge = jnp.zeros((8, grad.shape[1]), F32)
    acc[3:4] += jnp.sum(grad * inputs, axis=0, keepdims=True)
    acc[4:5] += jnp.sum(grad, axis=0, keepdims=True)
    for k, ref in enumerate(shifted):
        ref[8 : 8 + rows] = grad * (within >= float(3 - k)).astype(F32)
        moved = ref[3 - k : 3 - k + 8 + rows]
        total = total + moved[8:] * weight[k : k + 1]
        edge = edge + moved[:8] * weight[k : k + 1]
        outer = jnp.where(last, edge_inputs, 0.0) * moved[:8]
        acc[k : k + 1] += jnp.sum(moved[8:] * inputs, axis=0, keepdims=True) + jnp.sum(outer, axis=0, keepdims=True)
        ref[8 + rows :] = ref[8:16]
    return total, edge


def scan_back_kernel(
    idx, d_scaled, d_maps, pre_i, pre_p, in_i, in_p, halo_i, halo_p, aux, gloc, pkl, gin, states, d_mixer, mixer, skip, dlog,
    conv_i, conv_p, d_inner, d_step, d_pair, edge, tail, small, small_p, heads, *shifted,
):
    step = pl.program_id(0)
    blocks = pl.num_programs(0)
    first, last = step == 0, step == blocks - 1
    width = mixer.shape[1]

    @pl.when(first)
    def _():
        small[...] = jnp.zeros_like(small)
        small_p[...] = jnp.zeros_like(small_p)
        heads[...] = jnp.zeros_like(heads)

    base = idx[1] + (blocks - 1 - step) * BLOCK
    maps, slope_p = silu_parts(pre_p[...])
    values, slope = silu_parts(pre_i[...])
    dy = d_mixer[...]
    upper = triangle(True)
    lane = lax.broadcasted_iota(jnp.int32, (CHUNK, LANES), 1)
    grown = jnp.exp(dlog[...])
    pieces, pieces_p = [], []
    for c in range(BLOCK // CHUNK):
        at = slice(c * CHUNK, (c + 1) * CHUNK)
        table = aux[at, :]
        sizes = expand(table, DT, width)
        inflow = expand(table, INFLOW, width)
        outflow = expand(table, TAIL, width)
        keys, reads = maps[at, :LANES], maps[at, LANES:]
        scaled = values[at] * sizes
        grad_state = gloc[c] + pkl[c, :1] * gin[...]
        state = states[c]
        passed = outflow * dot3(keys, grad_state)
        total = d_scaled[at, :] + passed
        d_reads = d_maps[at, LANES:] + dot3(dy[at] * inflow, state, 1, 1)
        d_keys = d_maps[at, :LANES] + dot3(scaled * outflow, grad_state, 1, 1)
        pieces_p.append(jnp.concatenate([d_keys, d_reads], axis=1))
        plain = mixer[at, :] - skip[...] * values[at]
        d_cum = head_sums(dy[at] * plain - scaled * total)
        carried = jnp.sum(grad_state * state, axis=0, keepdims=True) * inflow[CHUNK - 1 :]
        carried = carried + jnp.sum(scaled * passed, axis=0, keepdims=True)
        after = head_sums(jnp.broadcast_to(carried, (8, width)))[:1]
        d_logs = jnp.dot(upper, d_cum, precision=HIGHEST, preferred_element_type=F32) + after
        d_raw = (head_sums(total * values[at]) - grown * d_logs) * pltpu.roll(table, LANES - RATE, 1)
        d_raw = jnp.where(lane < 8, d_raw, 0.0)
        d_step[at, :] = d_raw.astype(BF16)
        d_decay = jnp.where(lane < 8, -d_logs * table * grown, 0.0)
        heads[0:1] += jnp.sum(d_raw, axis=0, keepdims=True)
        heads[1:2] += jnp.sum(d_decay, axis=0, keepdims=True)
        pieces.append(total * sizes + dy[at] * skip[...])
    small[5:6] += jnp.sum(dy * values, axis=0, keepdims=True)
    grad = jnp.concatenate(pieces, axis=0) * slope
    pos = (base + lax.broadcasted_iota(jnp.int32, (BLOCK, 1), 0)).astype(F32)
    within = pos - aux[:, START : START + 1]
    whole, outer = conv_back(
        grad, within, in_i[...].astype(F32), halo_i[8:].astype(F32), conv_i, shifted[:3], first, last, small
    )
    grad_p = jnp.concatenate(pieces_p, axis=0) * slope_p
    whole_p, outer_p = conv_back(
        grad_p, within, in_p[...].astype(F32), halo_p[8:].astype(F32), conv_p, shifted[3:], first, last, small_p
    )
    d_inner[...] = whole.astype(BF16)
    d_pair[...] = whole_p
    edge[...] = jnp.concatenate([outer, outer_p], axis=1)

    @pl.when(first)
    def _():
        tail[...] = jnp.concatenate([whole[BLOCK - 16 :], whole_p[BLOCK - 16 :]], axis=1)


def dot_split(a, b, da=1, db=0):
    high, low = halves(b)
    return dot(a, high, da, db) + dot(a, low, da, db)


def device_copy(src, dst, sems, slot, to):
    return pltpu.make_async_remote_copy(
        src_ref=src, dst_ref=dst, send_sem=sems[0].at[slot], recv_sem=sems[1].at[slot],
        device_id=to, device_id_type=pl.DeviceIdType.MESH,
    )


def loop(start, stop, body):
    def run(d, carry):
        body(d)
        return carry

    lax.fori_loop(start, stop, run, 0)


def rows_at(ref, index, size):
    return ref.at[pl.ds(pl.multiple_of(index * size, size), size)]


class SeqSum:
    def __init__(self, source, first, land1, second, land2, done, sems):
        self.source, self.first, self.land1, self.second, self.land2, self.done = source, first, land1, second, land2, done
        self.sems = [sems[i : i + 2] for i in range(0, 8, 2)]
        self.wire = first.dtype
        self.members = land2.shape[0]
        self.piece = first.shape[0] // self.members
        me = lax.axis_index("seq")
        self.side, self.place = lax.rem(me, 2), me // 2
        self.partner = {"seq": me + 1 - 2 * self.side}

    def half(self, ref, side):
        return rows_at(ref, side, self.members * self.piece)

    def member(self, d):
        return lax.rem(self.place + d, self.members)

    def to_member(self, d):
        return {"seq": 2 * self.member(d) + self.side}

    def halve(self):
        return device_copy(self.first, self.land1, self.sems[0], 0, self.partner)

    def scatter(self, d):
        src = rows_at(self.second, self.member(d), self.piece)
        return device_copy(src, self.land2.at[d], self.sems[1], d, self.to_member(d))

    def part(self, place):
        return rows_at(self.done, self.side * self.members + place, self.piece)

    def gather(self, d):
        ref = self.part(self.place)
        return device_copy(ref, ref, self.sems[2], d, self.to_member(d))

    def gathered(self, d):
        ref = self.part(lax.rem(self.place + self.members - d, self.members))
        return device_copy(ref, ref, self.sems[2], d, self.partner)

    def widen(self, side):
        ref = self.half(self.done, side)
        return device_copy(ref, ref, self.sems[3], 0, self.partner)

    def begin(self):
        self.first[...] = self.half(self.source, 1 - self.side)[...].astype(self.wire)
        self.halve().start()

    def pass_on(self):
        self.halve().wait_recv()
        self.second[...] = (self.half(self.source, self.side)[...] + self.land1[...].astype(F32)).astype(self.wire)
        loop(1, self.members, lambda d: self.scatter(d).start())

    def finish(self):
        own = rows_at(self.source, self.side * self.members + self.place, self.piece)[...]
        own = own + rows_at(self.land1, self.place, self.piece)[...].astype(F32)

        def add(d, total):
            self.scatter(d).wait_recv()
            return total + self.land2[d].astype(F32)

        self.part(self.place)[...] = lax.fori_loop(1, self.members, add, own).astype(self.wire)
        loop(1, self.members, lambda d: self.gather(d).start())

    def collect(self):
        loop(1, self.members, lambda d: self.gathered(d).wait_recv())
        self.widen(self.side).start()

    def store(self, out):
        self.half(out, self.side)[...] = self.half(self.done, self.side)[...].astype(F32)
        self.widen(1 - self.side).wait_recv()
        self.half(out, 1 - self.side)[...] = self.half(self.done, 1 - self.side)[...].astype(F32)

    def drain(self):
        self.halve().wait_send()
        self.widen(self.side).wait_send()

        def both(d):
            self.scatter(d).wait_send()
            self.gather(d).wait_send()

        loop(1, self.members, both)

    @staticmethod
    def scratch(rows, lanes, wire, size):
        members = size // 2
        half = pltpu.VMEM((members * rows, lanes), wire)
        dma = pltpu.SemaphoreType.DMA
        return [half, half, half, pltpu.VMEM((members, rows, lanes), wire), pltpu.VMEM((2 * members * rows, lanes), wire)] + [
            dma((1,)), dma((1,)), dma((members,)), dma((members,)), dma((members,)), dma((members,)), dma((1,)), dma((1,)),
        ]


SUM_REFS = 13


class HeadSum:
    def __init__(self, source, out, fold1, half, fold2, quarter, sems):
        self.source, self.out, self.fold1, self.held, self.fold2, self.quarter = source, out, fold1, half, fold2, quarter
        self.sems = [sems[i : i + 2] for i in range(0, 8, 2)]
        self.rows = source.shape[0]
        head = lax.axis_index("head")
        self.core, self.plane = lax.rem(head, 2), head // 2
        self.beside, self.across = {"head": head + 1 - 2 * self.core}, {"head": head + 2 - 4 * self.plane}

    def fold_core(self):
        return device_copy(rows_at(self.source, 1 - self.core, self.rows // 2), self.fold1, self.sems[0], 0, self.beside)

    def fold_plane(self):
        return device_copy(rows_at(self.held, 1 - self.plane, self.rows // 4), self.fold2, self.sems[1], 0, self.across)

    def spread_plane(self, plane):
        ref = rows_at(self.out, 2 * self.core + plane, self.rows // 4)
        return device_copy(ref, ref, self.sems[2], 0, self.across)

    def spread_core(self, core):
        ref = rows_at(self.out, core, self.rows // 2)
        return device_copy(ref, ref, self.sems[3], 0, self.beside)

    def fold(self):
        self.fold_core().wait_recv()
        self.held[...] = rows_at(self.source, self.core, self.rows // 2)[...] + self.fold1[...]
        self.fold_plane().start()

    def settle(self):
        self.fold_plane().wait_recv()
        self.quarter[...] = jnp.zeros_like(self.quarter)
        self.quarter[: self.rows // 4] = rows_at(self.held, self.plane, self.rows // 4)[...] + self.fold2[...]

    def spread(self, total):
        rows_at(self.out, 2 * self.core + self.plane, self.rows // 4)[...] = total[: self.rows // 4]
        self.spread_plane(self.plane).start()

    def spread_more(self):
        self.spread_plane(1 - self.plane).wait_recv()
        self.spread_core(self.core).start()

    def finish(self):
        self.spread_core(1 - self.core).wait_recv()
        self.fold_core().wait_send()
        self.fold_plane().wait_send()
        self.spread_plane(self.plane).wait_send()
        self.spread_core(self.core).wait_send()

    @staticmethod
    def scratch(rows, lanes, padded_rows):
        dma = pltpu.SemaphoreType.DMA
        shapes = [(rows // 2, lanes), (rows // 2, lanes), (rows // 4, lanes), (padded_rows, lanes)]
        return [pltpu.VMEM(shape, F32) for shape in shapes] + [dma((1,))] * 8


HEAD_REFS = 12


def dot_split(a, b, da=1, db=0):
    high, low = halves(b)
    return dot(a, high, da, db) + dot(a, low, da, db)


def tail_kernel(
    low, d_gate, d_inner, d_step, d_pair, wg, wi, ws, wp, edge, tail, hid, d_out, gain, error, g_wo, g_wg, small_i, g_gain,
    small_p, heads,
    grad, sums, out_wo, out_wg, out_wi, out_pack, out_wp, out_small,
    block_i, block_p, after, away, land, mine, other, row, row_land, g_wi, g_ws, pack, g_wp, pair_small, sum_small, sum_wp,
    spread_wp, spread_small, grad_own, grad_other,
    core_send, core_land, x_send, x_land, edge_send, edge_land, grad_send, grad_land, row_send, row_arrive, *more,
):
    step = pl.program_id(0)
    blocks = pl.num_programs(0)
    half = blocks // 2
    seq, devices = lax.axis_index("seq"), lax.axis_size("seq")
    head, core = lax.axis_index("head"), core_bit()
    width = wi.shape[1]
    behind = lax.rem(seq + devices - 1, devices)
    group = 2 * devices
    me = 2 * seq + core
    beside, across = {"head": core_peer()}, {"head": lax.rem(head + 2, 4)}

    more = list(more)

    def take(number):
        taken = more[:number]
        del more[:number]
        return taken

    head_sums_ = []
    for source, out in ((g_wp, spread_wp), (pair_small, spread_small)):
        refs = take(HEAD_REFS)
        head_sums_.append(HeadSum(source, out, *refs[:4], refs[4:]))
    sources = [g_wo, g_wg, g_wi, pack, head_sums_[0].quarter, head_sums_[1].quarter]
    seq_sums = []
    for source in sources:
        refs = take(SUM_REFS)
        seq_sums.append(SeqSum(source, *refs[:5], refs[5:]))
    s_wo, s_wg, s_wi, s_pack, s_wp, s_small = seq_sums
    wide = list(zip(head_sums_, (s_wp, s_small), (sum_wp, sum_small)))

    def device(distance):
        to = lax.rem(me + distance, group)
        return {"seq": to // 2, "head": head - core + lax.rem(to, 2)}

    def hand(distance):
        return device_copy(row, row_land.at[me], (row_send, row_arrive), distance, device(distance))

    moved = device_copy(edge, after, (edge_send, edge_land), 0, {"seq": behind})

    def core_copy(slot):
        return device_copy(away.at[slot], land.at[slot], (core_send, core_land), slot, beside)

    def x_copy(slot):
        return device_copy(mine.at[slot], other.at[slot], (x_send, x_land), slot, across)

    def grad_copy(slot):
        return device_copy(grad_own.at[slot], grad_other.at[slot], (grad_send, grad_land), slot, beside)

    @pl.when(step == 0)
    def _():
        barrier = pltpu.get_barrier_semaphore()

        def greet(to):
            pl.semaphore_signal(barrier, inc=1, device_id=to, device_id_type=pl.DeviceIdType.MESH)

        loop(1, group, lambda d: greet(device(d)))
        greet(across)
        for ref in (g_wi, g_ws, pack, g_wp, pair_small):
            ref[...] = jnp.zeros_like(ref)
        pl.semaphore_wait(barrier, group)
        moved.start()
        s_wo.begin()
        s_wg.begin()

    block_i[...] = d_inner[...]
    block_p[...] = d_pair[...]
    block = lax.rem(step + half * (1 - core), blocks)

    @pl.when(block == blocks - 1)
    def _():
        moved.wait_recv()
        extra = jnp.where(seq == devices - 1, 0.0, after[...])
        fixed = jnp.concatenate([tail[:8], tail[8:] + extra], axis=0)
        block_i[BLOCK - 16 :] = fixed[:, :width].astype(BF16)
        block_p[BLOCK - 16 :] = fixed[:, width:]

    part = dot(d_gate[...], wg[...], 1, 1) + dot(block_i[...], wi[...], 1, 1) + dot(d_step[...], ws[...], 1, 1)
    high, rest = halves(block_p[...])
    part = part + (dot(high, wp[...], 1, 1) + dot(rest, wp[...], 1, 1))

    @pl.when(step < half)
    def _():
        away[step] = part.astype(away.dtype)
        core_copy(step).start()

    @pl.when(step >= half)
    def _():
        core_copy(step - half).wait_recv()
        mine[step - half] = (part + land[step - half].astype(F32)).astype(BF16)
        x_copy(step - half).start()

    g_ws[...] += dot(d_step[...], low[...], 0, 0)[:8]
    g_wp[...] += dot_split(low[...], block_p[...], 0, 0)
    g_wi[: low.shape[1]] += dot(low[...], block_i[...], 0, 0)

    def norm_back(slot):
        x_copy(slot).wait_recv()
        at = pl.ds(slot * BLOCK, BLOCK)
        d_low = mine[slot].astype(F32) + other[slot].astype(F32)
        rows = hid[at, :].astype(F32)
        scale = lax.rsqrt(jnp.mean(rows * rows, axis=1, keepdims=True) + EPSILON)
        row[:1] += jnp.sum(d_low * rows * scale, axis=0, keepdims=True)
        scaled = d_low * gain[...]
        pull = jnp.mean(scaled * rows, axis=1, keepdims=True) * (scale * scale * scale)
        block = (d_out[at, :] + scale * scaled - rows * pull).astype(BF16)
        grad_own[slot] = block
        grad_copy(slot).start()
        rows_at(grad, core * half + slot, BLOCK)[...] = block

    @pl.when(step == half + 1)
    def _():
        s_wo.pass_on()

    @pl.when(step == blocks - 1)
    def _():
        s_wi.begin()
        pack[:6] = small_i[:6]
        pack[6:7] = g_gain[...]
        pack[8:16] = g_ws[:, :width]
        pack[16:24] = g_ws[:, width:]
        pack[24:32, : heads.shape[1]] = heads[...]
        pair_small[:8] = small_p[...]
        for h_sum, _, _ in wide:
            h_sum.fold_core().start()
        row[:1] = jnp.zeros_like(row[:1])
        row[1:] = error[...]
        s_pack.begin()
        s_wg.pass_on()
        for h_sum, _, _ in wide:
            h_sum.fold()
        s_wo.finish()
        norm_back(0)
        s_wi.pass_on()
        s_pack.pass_on()
        s_wg.finish()
        norm_back(1)
        s_wo.collect()
        s_wi.finish()
        s_pack.finish()
        norm_back(2)
        s_wg.collect()
        norm_back(3)
        loop(1, group, lambda d: hand(d).start())
        for h_sum, s_sum, _ in wide:
            h_sum.settle()
            s_sum.begin()
        s_wi.collect()
        for _, s_sum, _ in wide:
            s_sum.pass_on()
        s_wo.store(out_wo)
        s_pack.collect()
        for _, s_sum, _ in wide:
            s_sum.finish()
        s_wg.store(out_wg)
        for _, s_sum, _ in wide:
            s_sum.collect()
        s_wi.store(out_wi)
        for h_sum, s_sum, total in wide:
            s_sum.store(total)
            h_sum.spread(total)
        s_pack.store(out_pack)
        for h_sum, _, _ in wide:
            h_sum.spread_more()
        row_land[me] = row[...]
        loop(1, group, lambda d: hand(d).wait())
        sums[...] = lax.fori_loop(1, group, lambda d, total: total + row_land[d], row_land[0])
        for (h_sum, _, _), out in zip(wide, (out_wp, out_small)):
            h_sum.finish()
            out[...] = h_sum.out[...]
        for s_sum in seq_sums:
            s_sum.drain()
        moved.wait_send()

        def drain(slot):
            core_copy(slot).wait_send()
            x_copy(slot).wait_send()
            grad_copy(slot).wait()
            rows_at(grad, (1 - core) * half + slot, BLOCK)[...] = grad_other[slot]

        loop(0, half, drain)


def call(kernel, grid, ins, outs, scratch=(), prefetch=0, flops=0, moved=0, collective=None, vmem=14):
    def spec(shape, block, index):
        if block is None:
            return pl.BlockSpec(shape, lambda *_: (0,) * len(shape))
        if isinstance(block, str):
            return pl.BlockSpec(memory_space={"smem": pltpu.SMEM, "vmem": pltpu.VMEM, "any": pl.ANY}[block])
        return pl.BlockSpec(block, index)

    scalars = [a for a, *_ in ins[:prefetch]]
    arrays = ins[prefetch:]
    extra = {} if collective is None else {"collective_id": collective, "has_side_effects": True}
    return pl.pallas_call(
        kernel,
        grid_spec=pltpu.PrefetchScalarGridSpec(
            num_scalar_prefetch=prefetch,
            grid=(grid,),
            in_specs=[spec(a.shape, block, index) for a, block, index in arrays],
            out_specs=[spec(shape, block, index) for shape, _, block, index in outs],
            scratch_shapes=list(scratch),
        ),
        out_shape=[jax.ShapeDtypeStruct(shape, dtype) for shape, dtype, _, _ in outs],
        compiler_params=pltpu.CompilerParams(
            dimension_semantics=("arbitrary",), vmem_limit_bytes=vmem << 20, **extra
        ),
        cost_estimate=pl.CostEstimate(flops=int(flops), bytes_accessed=int(moved), transcendentals=0),
    )(*scalars, *[a for a, *_ in arrays])


def swap(value, axis, bit):
    route = [(i, i ^ bit) for i in range(lax.axis_size(axis))]
    return jax.tree.map(lambda v: lax.ppermute(v, axis, route), value)


def shifted(value, axis, distance):
    devices = range(lax.axis_size(axis))
    route = [(i - distance, i) for i in devices if i - distance in devices]
    return lax.ppermute(value, axis, route)


def bits(axis):
    size = lax.axis_size(axis)
    return [1 << b for b in range(size.bit_length() - 1)]


def total_over(value, axis):
    for bit in bits(axis):
        value = value + swap(value, axis, bit)
    return value


def carried(total, axis, backward):
    mine = lax.axis_index(axis)

    def join(early, late):
        decay = late[CHUNK : CHUNK + 1]
        return jnp.concatenate([late[:CHUNK] + decay * early[:CHUNK], late[CHUNK:] * early[CHUNK:]])

    reached = jnp.concatenate([jnp.zeros_like(total[:CHUNK]), jnp.ones_like(total[CHUNK:])])
    for bit in bits(axis):
        other = swap(total, axis, bit)
        later = ((mine & bit) == 0) if backward else ((mine & bit) != 0)
        reached = jnp.where(later, join(other, reached), reached)
        total = jnp.where(later, join(other, total), join(total, other))
    return reached[:CHUNK]


def padded(row, lanes=LANES):
    return jnp.zeros((1, lanes), F32).at[0, : row.shape[0]].set(row)


def shards(
    hidden, teacher, doc_starts, valid_mask, norm_gain, w_gate, w_inner, w_pair, w_step, conv_inner, bias_inner,
    conv_pair, bias_pair, step_bias, decay_log, skip_gain, gate_gain, w_output,
):
    rows, model = hidden.shape
    width = w_inner.shape[1]
    pair_width = w_pair.shape[1]
    heads = step_bias.shape[0]
    blocks, chunks = rows // BLOCK, rows // CHUNK
    per = BLOCK // CHUNK
    half = blocks // 2
    inner_total = float(width * lax.axis_size("head"))
    core = lax.axis_index("head") & 1
    offset = lax.axis_index("seq") * rows
    idx = jnp.stack([core, offset]).astype(jnp.int32)
    edge_rows = 16

    starts = jnp.full((1, LANES), FAR, F32).at[0, : doc_starts.shape[0]].set(doc_starts.astype(F32))
    ws = jnp.zeros((model, LANES), BF16).at[:, :heads].set(w_step)
    sbias, dlog = padded(step_bias), padded(decay_log)
    skip = jnp.repeat(skip_gain, HEAD_DIM)[None, :]
    gain, out_gain = norm_gain[None, :], gate_gain[None, :]
    conv_i, conv_p = conv_inner.astype(F32), conv_pair.astype(F32)
    bias_i, bias_p = bias_inner.astype(F32)[None, :], bias_pair.astype(F32)[None, :]
    valid = valid_mask[None, :]

    tail = shifted(hidden[rows - edge_rows :], "seq", 1)
    count = total_over(jnp.full((8, LANES), jnp.sum(valid_mask.astype(F32))), "seq")[0, 0]
    factor = (rows * lax.axis_size("seq")) / count

    def by(w, column=0):
        return (BLOCK, w), lambda i, *_: (i, column)

    def back(w, column=0):
        return (BLOCK, w), lambda i, *_: (blocks - 1 - i, column)

    row = ((1, BLOCK), lambda i, *_: (0, i))
    row_back = ((1, BLOCK), lambda i, *_: (0, blocks - 1 - i))
    grid3 = lambda n: ((per, n, width), lambda i, *_: (i, 0, 0))
    back3 = lambda n: ((per, n, width), lambda i, *_: (blocks - 1 - i, 0, 0))
    whole = (None, None)

    def send_order(w):
        return (BLOCK, w), lambda i: (lax.rem(i + half * (1 - core_bit()), blocks), 0)

    send_row = ((1, BLOCK), lambda i: (0, lax.rem(i + half * (1 - core_bit()), blocks)))
    half_own = lambda w: ((BLOCK, w), lambda i: (i + half * core_bit(), 0))
    tail_half = lambda w: ((BLOCK, w), lambda i: (jnp.maximum(i - half, 0), 0))
    dma = pltpu.SemaphoreType.DMA
    swap_scratch = [pltpu.VMEM((half, BLOCK, model), F32)] * 2 + [dma((half,))] * 2

    halo_block = ((edge_rows, model), lambda i, *_: (jnp.maximum(i * (BLOCK // edge_rows) - 1, 0), 0))
    (low, in_i, in_p, pre_i, pre_p, aux, halo_i, halo_p, sloc, pkl, fin) = call(
        project_kernel,
        blocks,
        [
            (idx, None, None), (starts, *whole), (hidden, *by(model)), (hidden, *halo_block), (tail, *whole),
            (gain, *whole), (w_inner, *whole), (w_pair, *whole), (ws, *whole), (conv_i, *whole), (conv_p, *whole),
            (bias_i, *whole), (bias_p, *whole), (sbias, *whole), (dlog, *whole),
        ],
        [
            ((rows, model), BF16, *by(model)), ((rows, width), BF16, *by(width)), ((rows, pair_width), BF16, *by(pair_width)),
            ((rows, width), F32, *by(width)), ((rows, pair_width), F32, *by(pair_width)), ((rows, LANES), F32, *by(LANES)),
            ((edge_rows, width), BF16, *whole), ((edge_rows, pair_width), BF16, *whole),
            ((chunks, CHUNK, width), F32, *grid3(CHUNK)), ((chunks, 8, width), F32, *grid3(8)),
            ((CHUNK + 8, width), F32, *whole),
        ],
        [
            pltpu.VMEM((BLOCK + edge_rows, width), F32), pltpu.VMEM((BLOCK + edge_rows, pair_width), F32),
            pltpu.VMEM((CHUNK, width), F32), pltpu.VMEM((8, width), F32),
        ],
        prefetch=1, flops=3e9, moved=2e7,
    )
    state_in = carried(fin, "seq", False)
    gate, local = call(
        intra_kernel,
        blocks,
        [
            (idx, None, None), (low, *by(model)), (w_gate, *whole), (pre_i, *by(width)), (pre_p, *by(pair_width)),
            (aux, *by(LANES)), (skip, *whole),
        ],
        [((rows, width), F32, *by(width)), ((rows, width), F32, *by(width))],
        prefetch=1, flops=4e9, moved=2e7,
    )
    mixer, states, square = call(
        mix_kernel,
        blocks,
        [
            (pre_p, *by(LANES, 1)), (aux, *by(LANES)), (sloc, *grid3(CHUNK)), (pkl, *grid3(8)), (state_in, *whole),
            (local, *by(width)), (gate, *by(width)),
        ],
        [((rows, width), F32, *by(width)), ((chunks, CHUNK, width), F32, *grid3(CHUNK)), ((1, rows), F32, *row)],
        flops=1e9, moved=2e7,
    )
    square = total_over(square, "head")
    (mine,) = call(
        partial(branch_kernel, total=inner_total),
        blocks,
        [
            (mixer, *send_order(width)), (gate, *send_order(width)), (square, *send_row), (out_gain, *whole), (w_output, *whole),
        ],
        [((rows // 2, model), BF16, *tail_half(model))],
        swap_scratch,
        flops=1.2e9, moved=1e7, collective=2,
    )
    other = swap(mine, "head", 2)
    output, d_branch, d_out, error = call(
        loss_kernel,
        half,
        [
            (factor.reshape(1), "smem", None), (hidden, *half_own(model)), (teacher, *half_own(model)),
            (valid, (1, BLOCK), lambda i: (0, i + half * core_bit())), (mine, *by(model)), (other, *by(model)),
        ],
        [
            ((rows, model), BF16, "any", None), ((rows, model), BF16, "any", None),
            ((rows // 2, model), F32, *by(model)), ((1, model), F32, *whole),
        ],
        [pltpu.VMEM((half, BLOCK, model), BF16)] * 2 + [dma((2 * half,))] * 3,
        flops=1e8, moved=1.5e7, collective=3,
    )
    weighted, cross, g_gain, g_wo = call(
        partial(branch_back_kernel, total=inner_total),
        blocks,
        [
            (d_branch, *by(model)), (mixer, *by(width)), (gate, *by(width)), (square, *row), (out_gain, *whole),
            (w_output, *whole),
        ],
        [
            ((rows, width), F32, *by(width)), ((1, rows), F32, *row), ((1, width), F32, *whole),
            ((width, model), F32, *whole),
        ],
        flops=2.4e9, moved=1.5e7,
    )
    cross = total_over(cross, "head")
    d_mixer, d_gate, gloc, pkb, fin_back = call(
        partial(gate_back_kernel, total=inner_total),
        blocks,
        [
            (weighted, *back(width)), (mixer, *back(width)), (gate, *back(width)), (square, *row_back), (cross, *row_back),
            (pre_p, *back(LANES, 1)), (aux, *back(LANES)),
        ],
        [
            ((rows, width), F32, *back(width)), ((rows, width), BF16, *back(width)),
            ((chunks, CHUNK, width), F32, *back3(CHUNK)), ((chunks, 8, width), F32, *back3(8)), ((CHUNK + 8, width), F32, *whole),
        ],
        [pltpu.VMEM((CHUNK, width), F32), pltpu.VMEM((8, width), F32)],
        flops=1e9, moved=2e7,
    )
    grad_in = carried(fin_back, "seq", True)
    d_scaled, d_maps, g_wg = call(
        intra_back_kernel,
        blocks,
        [
            (idx, None, None), (d_mixer, *by(width)), (pre_i, *by(width)), (pre_p, *by(pair_width)), (aux, *by(LANES)),
            (low, *by(model)), (d_gate, *by(width)),
        ],
        [((rows, width), F32, *by(width)), ((rows, pair_width), F32, *by(pair_width)), ((model, width), F32, *whole)],
        prefetch=1, flops=6e9, moved=2e7,
    )
    both = width + pair_width
    d_inner, d_step, d_pair, edge, tail, small_i, small_p, head_small = call(
        scan_back_kernel,
        blocks,
        [
            (idx, None, None), (d_scaled, *back(width)), (d_maps, *back(pair_width)), (pre_i, *back(width)),
            (pre_p, *back(pair_width)), (in_i, *back(width)), (in_p, *back(pair_width)), (halo_i, *whole), (halo_p, *whole),
            (aux, *back(LANES)), (gloc, *back3(CHUNK)), (pkb, *back3(8)), (grad_in, *whole), (states, *back3(CHUNK)),
            (d_mixer, *back(width)), (mixer, *back(width)), (skip, *whole), (dlog, *whole), (conv_i, *whole), (conv_p, *whole),
        ],
        [
            ((rows, width), BF16, *back(width)), ((rows, LANES), BF16, *back(LANES)), ((rows, pair_width), F32, *back(pair_width)),
            ((8, both), F32, *whole), ((16, both), F32, *whole), ((8, width), F32, *whole), ((8, pair_width), F32, *whole),
            ((8, LANES), F32, *whole),
        ],
        [pltpu.VMEM((BLOCK + 16, width), F32)] * 3 + [pltpu.VMEM((BLOCK + 16, pair_width), F32)] * 3,
        prefetch=1, flops=3e9, moved=3e7, vmem=16,
    )
    size = lax.axis_size("seq")

    def piece(total_rows, tile):
        return -(-total_rows // (size * tile)) * tile

    r_wo, r_w, r_pack, r_wp, r_small = piece(width, 16), piece(model, 16), 8, piece(model // 4, 8), 8
    vmem = ("vmem", None)
    core_wire = F32 if size <= 8 else BF16
    once = lambda w: ((rows // 2, w), lambda i: (core_bit(), 0))
    sums_shapes = [(r_wo, model, BF16), (r_w, width, BF16), (r_w, width, BF16), (r_pack, width, F32), (r_wp, pair_width, F32),
                   (r_small, pair_width, F32)]
    pad_rows = lambda a, r: a if a.shape[0] == r * size else jnp.pad(a, ((0, r * size - a.shape[0]), (0, 0)))
    scratch = [
        pltpu.VMEM((BLOCK, width), BF16), pltpu.VMEM((BLOCK, pair_width), F32), pltpu.VMEM((8, both), F32),
        pltpu.VMEM((half, BLOCK, model), core_wire), pltpu.VMEM((half, BLOCK, model), core_wire),
        pltpu.VMEM((half, BLOCK, model), BF16), pltpu.VMEM((half, BLOCK, model), BF16),
        pltpu.VMEM((2, model), F32), pltpu.VMEM((2 * size, 2, model), F32),
        pltpu.VMEM((r_w * size, width), F32), pltpu.VMEM((8, model), F32), pltpu.VMEM((r_pack * size, width), F32),
        pltpu.VMEM((model, pair_width), F32), pltpu.VMEM((32, pair_width), F32),
        pltpu.VMEM((r_small * size, pair_width), F32), pltpu.VMEM((r_wp * size, pair_width), F32),
        pltpu.VMEM((model, pair_width), F32), pltpu.VMEM((32, pair_width), F32),
        pltpu.VMEM((half, BLOCK, model), BF16), pltpu.VMEM((half, BLOCK, model), BF16),
        dma((half,)), dma((half,)), dma((half,)), dma((half,)), dma((1,)), dma((1,)), dma((half,)), dma((half,)),
        dma((2 * size,)), dma((2 * size,)),
    ]
    scratch += HeadSum.scratch(model, pair_width, r_wp * size) + HeadSum.scratch(32, pair_width, r_small * size)
    for r, lanes, wire in sums_shapes:
        scratch += SeqSum.scratch(r, lanes, wire, size)
    grad_hidden, sums, g_wo, g_wg, g_wi, pack, g_wp, small_p = call(
        tail_kernel,
        blocks,
        [
            (low, *send_order(model)), (d_gate, *send_order(width)), (d_inner, *send_order(width)), (d_step, *send_order(LANES)),
            (d_pair, *send_order(pair_width)), (w_gate, *whole), (w_inner, *whole), (ws, *whole), (w_pair, *whole),
            (edge, *whole), (tail, *whole), (hidden, *once(model)), (d_out, *vmem), (gain, *whole), (error, *whole),
            (pad_rows(g_wo, r_wo), *vmem), (pad_rows(g_wg, r_w), *vmem), (small_i, *whole), (g_gain, *whole), (small_p, *whole),
            (head_small, *whole),
        ],
        [
            ((rows, model), BF16, *vmem), ((2, model), F32, *vmem), ((r_wo * size, model), F32, *vmem),
            ((r_w * size, width), F32, *vmem), ((r_w * size, width), F32, *vmem), ((r_pack * size, width), F32, *vmem),
            ((model, pair_width), F32, *vmem), ((32, pair_width), F32, *vmem),
        ],
        scratch,
        flops=6e9, moved=4e7, collective=4, vmem=40 if size <= 8 else 60,
    )
    g_wo, g_wg, g_wi = g_wo[:width], g_wg[:model], g_wi[:model]
    by_head, g_ws = pack[:8], jnp.concatenate([pack[8:16], pack[16:24]], axis=1)[:heads].T
    pair_small, head_small = small_p[:8], pack[24:32, :LANES]
    loss = jnp.sum(sums[1]) / (count * model)
    return (
        output, loss, grad_hidden, sums[0], g_wg, g_wi, g_wp, g_ws, by_head[:4], by_head[4], pair_small[:4], pair_small[4],
        head_small[0, :heads], head_small[1, :heads], jnp.sum(by_head[5].reshape(heads, HEAD_DIM), axis=1), by_head[6], g_wo,
    )


def solution(mesh):
    seq, head, wide = P("seq", None), P("head"), P(None, "head")
    in_specs = (
        seq, seq, P(), P("seq"), P(), wide, wide, P(), wide, wide, head, P(), P(), head, head, head, head, P("head", None),
    )
    out_specs = (
        seq, P(), seq, P(), wide, wide, P(), wide, wide, head, P(), P(), head, head, head, head, P("head", None),
    )
    return jax.shard_map(shards, mesh=mesh, in_specs=in_specs, out_specs=out_specs, check_vma=False)
```

```python
from functools import partial

import jax
import jax.numpy as jnp
from jax import lax
from jax.experimental import pallas as pl
from jax.experimental.pallas import tpu as pltpu
from jax.sharding import PartitionSpec as P

EPSILON = 1e-05
CHUNK = 128
BLOCK = 256
HEAD_DIM = 64
LANES = 128
FAR = float(1 << 24)
F32 = jnp.float32
BF16 = jnp.bfloat16
HIGHEST = lax.Precision.HIGHEST

DT, CUM, INFLOW, TAIL, RATE, START, END = 0, 8, 16, 24, 32, 40, 41


def dot(a, b, da=1, db=0):
    return lax.dot_general(a, b, (((da,), (db,)), ((), ())), preferred_element_type=F32)


def halves(v):
    high = v.astype(BF16)
    return high, (v - high.astype(F32)).astype(BF16)


def dot3(a, b, da=1, db=0):
    ah, al = halves(a)
    bh, bl = halves(b)
    return dot(ah, bh, da, db) + (dot(ah, bl, da, db) + dot(al, bh, da, db))


def column_sums(v):
    high, low = halves(v)
    ones = jnp.ones((8, v.shape[1]), BF16)
    return (dot(ones, high, 1, 1) + dot(ones, low, 1, 1))[:1]


def as_column(row):
    return jnp.transpose(jnp.broadcast_to(row, (8, row.shape[1])))[:, :1]


def expand(table, base, width):
    rows = table.shape[0]
    lane = lax.broadcasted_iota(jnp.int32, (rows, LANES), 1)
    parts = []
    for pair in range(width // LANES):
        first = jnp.broadcast_to(table[:, base + 2 * pair : base + 2 * pair + 1], (rows, LANES))
        second = jnp.broadcast_to(table[:, base + 2 * pair + 1 : base + 2 * pair + 2], (rows, LANES))
        parts.append(jnp.where(lane < HEAD_DIM, first, second))
    return jnp.concatenate(parts, axis=1)


def head_matrix(width):
    channel = lax.broadcasted_iota(jnp.int32, (width, LANES), 0)
    head = lax.broadcasted_iota(jnp.int32, (width, LANES), 1)
    return ((channel >> 6) == head).astype(BF16)


def head_sums(v):
    high, low = halves(v)
    matrix = head_matrix(v.shape[1])
    return dot(high, matrix) + dot(low, matrix)


def triangle(upper):
    row = lax.broadcasted_iota(jnp.int32, (CHUNK, CHUNK), 0)
    col = lax.broadcasted_iota(jnp.int32, (CHUNK, CHUNK), 1)
    return ((col >= row) if upper else (col <= row)).astype(F32)


def silu_parts(pre):
    gate = jax.nn.sigmoid(pre)
    return pre * gate, gate * (1.0 + pre * (1.0 - gate))


def project_kernel(
    idx, starts, hid, halo, tail, gain, wi, wp, ws, conv_i, conv_p, bias_i, bias_p, sbias, dlog,
    low, in_i, in_p, pre_i, pre_p, aux, halo_low, halo_i, halo_p, sloc, pkl, fin, wide_i, wide_p, state, decay,
):
    step = pl.program_id(0)
    edge = tail.shape[0]
    width = wi.shape[1]

    @pl.when(step == 0)
    def _():
        state[...] = jnp.zeros_like(state)
        decay[...] = jnp.ones_like(decay)

    before = jnp.where(step == 0, tail[...].astype(F32), halo[...].astype(F32))
    rows = jnp.concatenate([before, hid[...].astype(F32)], axis=0)
    scale = lax.rsqrt(jnp.mean(rows * rows, axis=1, keepdims=True) + EPSILON)
    lowered = (rows * scale * gain[...]).astype(BF16)
    own = lowered[edge:]
    low[...] = own
    inner = dot(lowered, wi[...]).astype(BF16)
    pair = dot(lowered, wp[...]).astype(BF16)
    in_i[...] = inner[edge:]
    in_p[...] = pair[edge:]
    wide_i[...] = inner.astype(F32)
    wide_p[...] = pair.astype(F32)

    @pl.when(step == 0)
    def _():
        halo_low[...] = lowered[:edge]
        halo_i[...] = inner[:edge]
        halo_p[...] = pair[:edge]

    base = idx[1] + step * BLOCK
    pos = (base + lax.broadcasted_iota(jnp.int32, (BLOCK, LANES), 0)).astype(F32)
    begun = starts[...] <= pos
    start = jnp.max(jnp.where(begun, starts[...], -1.0), axis=1, keepdims=True)
    end = jnp.min(jnp.where(begun, FAR, starts[...]), axis=1, keepdims=True)
    within = pos[:, :1] - start
    keep = [(within >= float(3 - k)).astype(F32) for k in range(3)]

    def convolve(wide, weight, bias):
        total = bias[...] + wide[edge : edge + BLOCK] * weight[3:4]
        for k in range(3):
            total = total + wide[edge - 3 + k : edge - 3 + k + BLOCK] * weight[k : k + 1] * keep[k]
        return total

    conv_inner = convolve(wide_i, conv_i, bias_i)
    conv_pair = convolve(wide_p, conv_p, bias_p)
    pre_i[...] = conv_inner
    pre_p[...] = conv_pair
    values = conv_inner * jax.nn.sigmoid(conv_inner)
    maps = conv_pair[:, :LANES]
    maps = maps * jax.nn.sigmoid(maps)

    raw = dot(own, ws[...]) + sbias[...]
    dt = jnp.maximum(raw, 0.0) + jnp.log1p(jnp.exp(-jnp.abs(raw)))
    rate = jax.nn.sigmoid(raw)
    logs = -dt * jnp.exp(dlog[...])
    lane = lax.broadcasted_iota(jnp.int32, (CHUNK, LANES), 1)
    lower = triangle(False)
    for c in range(BLOCK // CHUNK):
        at = slice(c * CHUNK, (c + 1) * CHUNK)
        cum = jnp.dot(lower, logs[at], precision=HIGHEST, preferred_element_type=F32)
        last = cum[CHUNK - 1 :]
        first = (base + c * CHUNK).astype(F32)
        inflow = jnp.exp(cum) * (start[at] <= first - 1.0).astype(F32)
        outflow = jnp.exp(last - cum) * (end[at] > first + (CHUNK - 1.0)).astype(F32)
        table = jnp.where(lane < CUM, dt[at], pltpu.roll(cum, CUM, 1))
        table = jnp.where(lane < INFLOW, table, pltpu.roll(inflow, INFLOW, 1))
        table = jnp.where(lane < TAIL, table, pltpu.roll(outflow, TAIL, 1))
        table = jnp.where(lane < RATE, table, pltpu.roll(rate[at], RATE, 1))
        table = jnp.where(lane < START, table, jnp.where(lane < END, start[at], end[at]))
        aux[at, :] = table
        scaled = values[at] * expand(table, DT, width) * expand(table, TAIL, width)
        added = dot3(maps[at], scaled, 0, 0)
        kept = expand(jnp.broadcast_to(inflow[CHUNK - 1 :], (8, LANES)), 0, width)
        sloc[c] = state[...]
        pkl[c] = decay[...]
        state[...] = state[...] * kept[:1] + added
        decay[...] = decay[...] * kept
    fin[:CHUNK] = state[...]
    fin[CHUNK:] = decay[...]


def masks(table, first, transposed):
    row = lax.broadcasted_iota(jnp.int32, (CHUNK, CHUNK), 0)
    col = lax.broadcasted_iota(jnp.int32, (CHUNK, CHUNK), 1)
    at = (first + col).astype(F32)
    if transposed:
        return (col >= row) & (at < table[:, END : END + 1])
    return (col <= row) & (at >= table[:, START : START + 1])


def head_split(v, pair):
    lane = lax.broadcasted_iota(jnp.int32, (v.shape[0], LANES), 1)
    part = v[:, pair * LANES : (pair + 1) * LANES]
    return jnp.concatenate(
        [jnp.where(lane < HEAD_DIM, part, 0.0), jnp.where(lane < HEAD_DIM, 0.0, part)], axis=0
    ).astype(BF16)


def intra_kernel(idx, low, wg, pre_i, pre_p, aux, skip, gate, mixed):
    width = wg.shape[1]
    gate[...] = dot(low[...], wg[...])
    base = idx[1] + pl.program_id(0) * BLOCK
    maps, _ = silu_parts(pre_p[...])
    values, _ = silu_parts(pre_i[...])
    for c in range(BLOCK // CHUNK):
        at = slice(c * CHUNK, (c + 1) * CHUNK)
        table = aux[at, :]
        rows = jnp.transpose(table)
        joined = masks(table, base + c * CHUNK, False)
        scores = dot(maps[at, LANES:].astype(BF16), maps[at, :LANES].astype(BF16), 1, 1)
        scaled = values[at] * expand(table, DT, width)
        parts = []
        for pair in range(width // LANES):
            weights = []
            for h in (2 * pair, 2 * pair + 1):
                gap = table[:, CUM + h : CUM + h + 1] - rows[CUM + h : CUM + h + 1, :]
                weights.append((scores * jnp.exp(jnp.where(joined, gap, -1e30))).astype(BF16))
            parts.append(dot(jnp.concatenate(weights, axis=1), head_split(scaled, pair)))
        mixed[at, :] = jnp.concatenate(parts, axis=1) + values[at] * skip[...]


def mix_kernel(pre_c, aux, sloc, pkl, sin, local, gate, mixer, states, square):
    width = local.shape[1]
    reads, _ = silu_parts(pre_c[...])
    for c in range(BLOCK // CHUNK):
        at = slice(c * CHUNK, (c + 1) * CHUNK)
        state = sloc[c] + pkl[c, :1] * sin[...]
        states[c] = state
        mixer[at, :] = local[at, :] + expand(aux[at, :], INFLOW, width) * dot3(reads[at], state)
    act, _ = silu_parts(gate[...])
    gated = mixer[...] * act
    square[...] = column_sums(gated * gated)


def gate_scale(square, total):
    return as_column(lax.rsqrt(square / total + EPSILON))


def core_bit():
    return lax.rem(lax.axis_index("head"), 2)


def core_peer():
    return lax.axis_index("head") + 1 - 2 * core_bit()


def enter(peers):
    barrier = pltpu.get_barrier_semaphore()
    for peer in peers:
        pl.semaphore_signal(barrier, inc=1, device_id=peer, device_id_type=pl.DeviceIdType.MESH)
    pl.semaphore_wait(barrier, len(peers))


def to_peer(src, dst, sends, lands, slot):
    return pltpu.make_async_remote_copy(
        src_ref=src, dst_ref=dst, send_sem=sends.at[slot], recv_sem=lands.at[slot],
        device_id={"head": core_peer()}, device_id_type=pl.DeviceIdType.MESH,
    )


def add_halves(part, mine, away, land, send_sem, land_sem):
    step = pl.program_id(0)
    half = pl.num_programs(0) // 2

    def copy(slot):
        return to_peer(away.at[slot], land.at[slot], send_sem, land_sem, slot)

    @pl.when(step < half)
    def _():
        away[step] = part.astype(away.dtype)
        copy(step).start()

    @pl.when(step >= half)
    def _():
        copy(step - half).wait_recv()
        mine[...] = (part + land[step - half].astype(F32)).astype(mine.dtype)

    @pl.when(step == 2 * half - 1)
    def _():
        def drain(slot, carry):
            copy(slot).wait_send()
            return carry

        lax.fori_loop(0, half, drain, 0)


def branch_kernel(mixer, gate, square, gain, wo, mine, away, land, send_sem, land_sem, *, total):
    @pl.when(pl.program_id(0) == 0)
    def _():
        enter([{"head": core_peer()}])

    act, _ = silu_parts(gate[...])
    gated = mixer[...] * act
    normed = (gated * gate_scale(square[...], total) * gain[...]).astype(BF16)
    add_halves(dot(normed, wo[...]), mine, away, land, send_sem, land_sem)


def both_cores(buffers, wholes, sems):
    step = pl.program_id(0)
    half = pl.num_programs(0)
    local, send, land = sems

    def copies(k, slot):
        rows = pl.ds(pl.multiple_of((core_bit() * half + slot) * BLOCK, BLOCK), BLOCK)
        here = pltpu.make_async_copy(buffers[k].at[slot], wholes[k].at[rows], local.at[k * half + slot])
        there = to_peer(buffers[k].at[slot], wholes[k].at[rows], send, land, k * half + slot)
        return here, there

    for k in range(len(wholes)):
        for copy in copies(k, step):
            copy.start()

    @pl.when(step == half - 1)
    def _():
        for k in range(len(wholes)):

            def drain(slot, carry, k=k):
                here, there = copies(k, slot)
                here.wait()
                there.wait()
                return carry

            lax.fori_loop(0, half, drain, 0)


def loss_kernel(factor, hid, teacher, valid, mine, other, out, d_branch, d_out, error, out_block, grad_block, *sems):
    step = pl.program_id(0)

    @pl.when(step == 0)
    def _():
        error[...] = jnp.zeros_like(error)
        enter([{"head": core_peer()}])

    outf = hid[...].astype(F32) + (mine[...].astype(F32) + other[...].astype(F32))
    term = outf - teacher[...].astype(F32)
    masked = as_column(valid[...].astype(F32)) * term
    error[...] += jnp.sum(masked * term, axis=0, keepdims=True)
    grad = masked * factor[0]
    d_out[...] = grad
    out_block[step] = outf.astype(BF16)
    grad_block[step] = grad.astype(BF16)
    both_cores([out_block, grad_block], [out, d_branch], sems)


def branch_back_kernel(d_branch, mixer, gate, square, gain, wo, weighted, cross, g_gain, g_wo, *, total):
    step = pl.program_id(0)

    @pl.when(step == 0)
    def _():
        g_gain[...] = jnp.zeros_like(g_gain)
        g_wo[...] = jnp.zeros_like(g_wo)

    act, _ = silu_parts(gate[...])
    gated = mixer[...] * act
    scaled = gated * gate_scale(square[...], total)
    normed = (scaled * gain[...]).astype(BF16)
    g_wo[...] += dot(normed, d_branch[...], 0, 0)
    d_normed = dot(d_branch[...], wo[...], 1, 1)
    g_gain[...] += jnp.sum(d_normed * scaled, axis=0, keepdims=True)
    grad = d_normed * gain[...]
    weighted[...] = grad
    cross[...] = column_sums(grad * gated)


def gate_back_kernel(
    weighted, mixer, gate, square, cross, pre_c, aux, d_mixer, d_gate, gloc, pkl, fin, state, decay, *, total
):
    @pl.when(pl.program_id(0) == 0)
    def _():
        state[...] = jnp.zeros_like(state)
        decay[...] = jnp.ones_like(decay)

    width = mixer.shape[1]
    act, slope = silu_parts(gate[...])
    gated = mixer[...] * act
    row = lax.rsqrt(square[...] / total + EPSILON)
    scale = as_column(row)
    pull = as_column(row * row * row * cross[...] / total)
    d_gated = scale * weighted[...] - gated * pull
    dy = d_gated * act
    d_mixer[...] = dy
    d_gate[...] = (d_gated * mixer[...] * slope).astype(BF16)
    reads, _ = silu_parts(pre_c[...])
    for c in reversed(range(BLOCK // CHUNK)):
        at = slice(c * CHUNK, (c + 1) * CHUNK)
        inflow = expand(aux[at, :], INFLOW, width)
        gloc[c] = state[...]
        pkl[c] = decay[...]
        kept = inflow[CHUNK - 1 :]
        state[...] = state[...] * kept + dot3(reads[at], dy[at] * inflow, 0, 0)
        decay[...] = decay[...] * kept
    fin[:CHUNK] = state[...]
    fin[CHUNK:] = decay[...]


def intra_back_kernel(idx, d_mixer, pre_i, pre_p, aux, low, d_gate, d_scaled, d_maps, g_wg):
    @pl.when(pl.program_id(0) == 0)
    def _():
        g_wg[...] = jnp.zeros_like(g_wg)

    g_wg[...] += dot(low[...], d_gate[...], 0, 0)
    width = d_mixer.shape[1]
    base = idx[1] + pl.program_id(0) * BLOCK
    maps, _ = silu_parts(pre_p[...])
    values, _ = silu_parts(pre_i[...])
    for c in range(BLOCK // CHUNK):
        at = slice(c * CHUNK, (c + 1) * CHUNK)
        table = aux[at, :]
        rows = jnp.transpose(table)
        joined = masks(table, base + c * CHUNK, True)
        keys = maps[at, :LANES].astype(BF16)
        reads = maps[at, LANES:].astype(BF16)
        scores = dot(keys, reads, 1, 1)
        scaled = (values[at] * expand(table, DT, width)).astype(BF16)
        grads = d_mixer[at, :]
        d_scores = jnp.zeros((CHUNK, CHUNK), F32)
        parts = []
        for pair in range(width // LANES):
            split = head_split(grads, pair)
            d_weights = dot(scaled[:, pair * LANES : (pair + 1) * LANES], split, 1, 1)
            weights = []
            for side in range(2):
                h = 2 * pair + side
                gap = rows[CUM + h : CUM + h + 1, :] - table[:, CUM + h : CUM + h + 1]
                factor = jnp.exp(jnp.where(joined, gap, -1e30))
                weights.append((scores * factor).astype(BF16))
                d_scores = d_scores + factor * d_weights[:, side * CHUNK : (side + 1) * CHUNK]
            parts.append(dot(jnp.concatenate(weights, axis=1), split))
        d_scaled[at, :] = jnp.concatenate(parts, axis=1)
        low_scores = d_scores.astype(BF16)
        d_maps[at, :] = jnp.concatenate([dot(low_scores, reads), dot(low_scores, keys, 0, 0)], axis=1)


def conv_back(grad, within, inputs, edge_inputs, weight, shifted, first, last, acc):
    rows = grad.shape[0]

    @pl.when(first)
    def _():
        for ref in shifted:
            ref[...] = jnp.zeros_like(ref)

    total = grad * weight[3:4]
    edge = jnp.zeros((8, grad.shape[1]), F32)
    acc[3:4] += jnp.sum(grad * inputs, axis=0, keepdims=True)
    acc[4:5] += jnp.sum(grad, axis=0, keepdims=True)
    for k, ref in enumerate(shifted):
        ref[8 : 8 + rows] = grad * (within >= float(3 - k)).astype(F32)
        moved = ref[3 - k : 3 - k + 8 + rows]
        total = total + moved[8:] * weight[k : k + 1]
        edge = edge + moved[:8] * weight[k : k + 1]
        outer = jnp.where(last, edge_inputs, 0.0) * moved[:8]
        acc[k : k + 1] += jnp.sum(moved[8:] * inputs, axis=0, keepdims=True) + jnp.sum(outer, axis=0, keepdims=True)
        ref[8 + rows :] = ref[8:16]
    return total, edge


def device_copy(src, dst, sems, slot, to):
    return pltpu.make_async_remote_copy(
        src_ref=src, dst_ref=dst, send_sem=sems[0].at[slot], recv_sem=sems[1].at[slot],
        device_id=to, device_id_type=pl.DeviceIdType.MESH,
    )


def loop(start, stop, body):
    def run(d, carry):
        body(d)
        return carry

    lax.fori_loop(start, stop, run, 0)


def rows_at(ref, index, size):
    return ref.at[pl.ds(pl.multiple_of(index * size, size), size)]


class SeqSum:
    def __init__(self, source, first, land1, second, land2, done, sems):
        self.source, self.first, self.land1, self.second, self.land2, self.done = source, first, land1, second, land2, done
        self.sems = [sems[i : i + 2] for i in range(0, 8, 2)]
        self.wire = first.dtype
        self.members = land2.shape[0]
        self.piece = first.shape[0] // self.members
        me = lax.axis_index("seq")
        self.side, self.place = lax.rem(me, 2), me // 2
        self.partner = {"seq": me + 1 - 2 * self.side}

    def half(self, ref, side):
        return rows_at(ref, side, self.members * self.piece)

    def member(self, d):
        return lax.rem(self.place + d, self.members)

    def to_member(self, d):
        return {"seq": 2 * self.member(d) + self.side}

    def halve(self):
        return device_copy(self.first, self.land1, self.sems[0], 0, self.partner)

    def scatter(self, d):
        src = rows_at(self.second, self.member(d), self.piece)
        return device_copy(src, self.land2.at[d], self.sems[1], d, self.to_member(d))

    def part(self, place):
        return rows_at(self.done, self.side * self.members + place, self.piece)

    def gather(self, d):
        ref = self.part(self.place)
        return device_copy(ref, ref, self.sems[2], d, self.to_member(d))

    def gathered(self, d):
        ref = self.part(lax.rem(self.place + self.members - d, self.members))
        return device_copy(ref, ref, self.sems[2], d, self.partner)

    def widen(self, side):
        ref = self.half(self.done, side)
        return device_copy(ref, ref, self.sems[3], 0, self.partner)

    def begin(self):
        self.first[...] = self.half(self.source, 1 - self.side)[...].astype(self.wire)
        self.halve().start()

    def pass_on(self):
        self.halve().wait_recv()
        self.second[...] = (self.half(self.source, self.side)[...] + self.land1[...].astype(F32)).astype(self.wire)
        loop(1, self.members, lambda d: self.scatter(d).start())

    def finish(self):
        own = rows_at(self.source, self.side * self.members + self.place, self.piece)[...]
        own = own + rows_at(self.land1, self.place, self.piece)[...].astype(F32)

        def add(d, total):
            self.scatter(d).wait_recv()
            return total + self.land2[d].astype(F32)

        self.part(self.place)[...] = lax.fori_loop(1, self.members, add, own).astype(self.wire)
        loop(1, self.members, lambda d: self.gather(d).start())

    def collect(self):
        loop(1, self.members, lambda d: self.gathered(d).wait_recv())
        self.widen(self.side).start()

    def store(self, out):
        self.half(out, self.side)[...] = self.half(self.done, self.side)[...].astype(F32)
        self.widen(1 - self.side).wait_recv()
        self.half(out, 1 - self.side)[...] = self.half(self.done, 1 - self.side)[...].astype(F32)

    def drain(self):
        self.halve().wait_send()
        self.widen(self.side).wait_send()

        def both(d):
            self.scatter(d).wait_send()
            self.gather(d).wait_send()

        loop(1, self.members, both)

    @staticmethod
    def scratch(rows, lanes, wire, size):
        members = size // 2
        half = pltpu.VMEM((members * rows, lanes), wire)
        dma = pltpu.SemaphoreType.DMA
        return [half, half, half, pltpu.VMEM((members, rows, lanes), wire), pltpu.VMEM((2 * members * rows, lanes), wire)] + [
            dma((1,)), dma((1,)), dma((members,)), dma((members,)), dma((members,)), dma((members,)), dma((1,)), dma((1,)),
        ]


SUM_REFS = 13


class HeadSum:
    def __init__(self, source, out, fold1, half, fold2, quarter, sems):
        self.source, self.out, self.fold1, self.held, self.fold2, self.quarter = source, out, fold1, half, fold2, quarter
        self.sems = [sems[i : i + 2] for i in range(0, 8, 2)]
        self.rows = source.shape[0]
        head = lax.axis_index("head")
        self.core, self.plane = lax.rem(head, 2), head // 2
        self.beside, self.across = {"head": head + 1 - 2 * self.core}, {"head": head + 2 - 4 * self.plane}

    def fold_core(self):
        return device_copy(rows_at(self.source, 1 - self.core, self.rows // 2), self.fold1, self.sems[0], 0, self.beside)

    def fold_plane(self):
        return device_copy(rows_at(self.held, 1 - self.plane, self.rows // 4), self.fold2, self.sems[1], 0, self.across)

    def spread_plane(self, plane):
        ref = rows_at(self.out, 2 * self.core + plane, self.rows // 4)
        return device_copy(ref, ref, self.sems[2], 0, self.across)

    def spread_core(self, core):
        ref = rows_at(self.out, core, self.rows // 2)
        return device_copy(ref, ref, self.sems[3], 0, self.beside)

    def fold(self):
        self.fold_core().wait_recv()
        self.held[...] = rows_at(self.source, self.core, self.rows // 2)[...] + self.fold1[...]
        self.fold_plane().start()

    def settle(self):
        self.fold_plane().wait_recv()
        self.quarter[...] = jnp.zeros_like(self.quarter)
        self.quarter[: self.rows // 4] = rows_at(self.held, self.plane, self.rows // 4)[...] + self.fold2[...]

    def spread(self, total):
        rows_at(self.out, 2 * self.core + self.plane, self.rows // 4)[...] = total[: self.rows // 4]
        self.spread_plane(self.plane).start()

    def spread_more(self):
        self.spread_plane(1 - self.plane).wait_recv()
        self.spread_core(self.core).start()

    def finish(self):
        self.spread_core(1 - self.core).wait_recv()
        self.fold_core().wait_send()
        self.fold_plane().wait_send()
        self.spread_plane(self.plane).wait_send()
        self.spread_core(self.core).wait_send()

    @staticmethod
    def scratch(rows, lanes, padded_rows):
        dma = pltpu.SemaphoreType.DMA
        shapes = [(rows // 2, lanes), (rows // 2, lanes), (rows // 4, lanes), (padded_rows, lanes)]
        return [pltpu.VMEM(shape, F32) for shape in shapes] + [dma((1,))] * 8


HEAD_REFS = 12


def finale_kernel(
    d_scaled, d_maps, pre_i, pre_p, in_i, in_p, halo_low, halo_i, halo_p, aux, gloc, pkl, gin, states, d_mixer, mixer, skip, dlog,
    conv_i, conv_p, low, d_gate, wg, wi, ws, wp, hid, d_out, gain, error, g_wo, g_wg, g_gain,
    grad_all, sums, out_wo, out_wg, out_wi, out_pack, out_wp, out_small,
    shift_i0, shift_i1, shift_i2, shift_p0, shift_p1, shift_p2, small, small_p, heads,
    parts, land, mine, other, row, row_land, g_wi, g_ws, pack, g_wp, pair_small, sum_small, sum_wp, spread_wp, spread_small,
    grad_own, grad_other, edge, edge_core, edge_plane, edge_ahead,
    core_send, core_land, x_send, x_land, edge_send, edge_land, grad_send, grad_land, row_send, row_arrive, *more,
):
    shifted = (shift_i0, shift_i1, shift_i2, shift_p0, shift_p1, shift_p2)
    step = pl.program_id(0)
    blocks = pl.num_programs(0)
    half = blocks // 2
    first, last = step == 0, step == blocks - 1
    seq, devices = lax.axis_index("seq"), lax.axis_size("seq")
    head, core = lax.axis_index("head"), core_bit()
    width = wi.shape[1]
    model = low.shape[1]
    behind, ahead = lax.rem(seq + devices - 1, devices), lax.rem(seq + 1, devices)
    group = 2 * devices
    me = 2 * seq + core
    beside, across = {"head": core_peer()}, {"head": lax.rem(head + 2, 4)}
    summing = len(more) > 0

    more = list(more)

    def take(number):
        taken = more[:number]
        del more[:number]
        return taken

    seq_sums, wide = [], []
    if summing:
        head_parts = []
        for source, out in ((g_wp, spread_wp), (pair_small, spread_small)):
            refs = take(HEAD_REFS)
            head_parts.append(HeadSum(source, out, *refs[:4], refs[4:]))
        for source in (g_wo, g_wg, g_wi, pack, head_parts[0].quarter, head_parts[1].quarter):
            refs = take(SUM_REFS)
            seq_sums.append(SeqSum(source, *refs[:5], refs[5:]))
        s_wo, s_wg, s_wi, s_pack, s_wp, s_small = seq_sums
        wide = list(zip(head_parts, (s_wp, s_small), (sum_wp, sum_small)))

    def device(distance):
        to = lax.rem(me + distance, group)
        return {"seq": to // 2, "head": head - core + lax.rem(to, 2)}

    def hand(distance):
        return device_copy(row, row_land.at[me], (row_send, row_arrive), distance, device(distance))

    def edge_copy(slot, landing, to):
        return device_copy(edge.at[slot], landing, (edge_send, edge_land), slot, to)

    def core_copy(slot):
        return device_copy(parts.at[slot], land.at[slot], (core_send, core_land), slot, beside)

    def x_copy(slot):
        return device_copy(mine.at[slot], other.at[slot], (x_send, x_land), slot, across)

    def grad_copy(slot):
        return device_copy(grad_own.at[slot], grad_other.at[slot], (grad_send, grad_land), slot, beside)

    @pl.when(first)
    def _():
        barrier = pltpu.get_barrier_semaphore()

        def greet(to):
            pl.semaphore_signal(barrier, inc=1, device_id=to, device_id_type=pl.DeviceIdType.MESH)

        loop(1, group, lambda d: greet(device(d)))
        greet(across)
        for ref in (g_wi, g_ws, pack, g_wp, pair_small, small, small_p, heads):
            ref[...] = jnp.zeros_like(ref)
        row[:1] = jnp.zeros_like(row[:1])
        row[1:] = error[...]
        pl.semaphore_wait(barrier, group)
        if summing:
            s_wo.begin()
            s_wg.begin()

    base = seq * (blocks * BLOCK) + (blocks - 1 - step) * BLOCK
    maps, slope_p = silu_parts(pre_p[...])
    values, slope = silu_parts(pre_i[...])
    dy = d_mixer[...]
    upper = triangle(True)
    lane = lax.broadcasted_iota(jnp.int32, (CHUNK, LANES), 1)
    grown = jnp.exp(dlog[...])
    pieces, pieces_p, pieces_s = [], [], []
    for c in range(BLOCK // CHUNK):
        at = slice(c * CHUNK, (c + 1) * CHUNK)
        table = aux[at, :]
        sizes = expand(table, DT, width)
        inflow = expand(table, INFLOW, width)
        outflow = expand(table, TAIL, width)
        keys, reads = maps[at, :LANES], maps[at, LANES:]
        scaled = values[at] * sizes
        grad_state = gloc[c] + pkl[c, :1] * gin[...]
        state = states[c]
        passed = outflow * dot3(keys, grad_state)
        total = d_scaled[at, :] + passed
        d_reads = d_maps[at, LANES:] + dot3(dy[at] * inflow, state, 1, 1)
        d_keys = d_maps[at, :LANES] + dot3(scaled * outflow, grad_state, 1, 1)
        pieces_p.append(jnp.concatenate([d_keys, d_reads], axis=1))
        plain = mixer[at, :] - skip[...] * values[at]
        d_cum = head_sums(dy[at] * plain - scaled * total)
        carried = jnp.sum(grad_state * state, axis=0, keepdims=True) * inflow[CHUNK - 1 :]
        carried = carried + jnp.sum(scaled * passed, axis=0, keepdims=True)
        after = head_sums(jnp.broadcast_to(carried, (8, width)))[:1]
        d_logs = jnp.dot(upper, d_cum, precision=HIGHEST, preferred_element_type=F32) + after
        d_raw = (head_sums(total * values[at]) - grown * d_logs) * pltpu.roll(table, LANES - RATE, 1)
        d_raw = jnp.where(lane < 8, d_raw, 0.0)
        pieces_s.append(d_raw.astype(BF16))
        d_decay = jnp.where(lane < 8, -d_logs * table * grown, 0.0)
        heads[0:1] += jnp.sum(d_raw, axis=0, keepdims=True)
        heads[1:2] += jnp.sum(d_decay, axis=0, keepdims=True)
        pieces.append(total * sizes + dy[at] * skip[...])
    small[5:6] += jnp.sum(dy * values, axis=0, keepdims=True)
    grad = jnp.concatenate(pieces, axis=0) * slope
    pos = (base + lax.broadcasted_iota(jnp.int32, (BLOCK, 1), 0)).astype(F32)
    within = pos - aux[:, START : START + 1]
    whole, outer = conv_back(
        grad, within, in_i[...].astype(F32), halo_i[8:].astype(F32), conv_i, shifted[:3], first, last, small
    )
    grad_p = jnp.concatenate(pieces_p, axis=0) * slope_p
    whole_p, outer_p = conv_back(
        grad_p, within, in_p[...].astype(F32), halo_p[8:].astype(F32), conv_p, shifted[3:], first, last, small_p
    )

    inner = whole.astype(BF16)
    d_step = jnp.concatenate(pieces_s, axis=0)
    part = dot(d_gate[...], wg[...], 1, 1) + dot(inner, wi[...], 1, 1) + dot(d_step, ws[...], 1, 1)
    high, rest = halves(whole_p)
    part = part + (dot(high, wp[...], 1, 1) + dot(rest, wp[...], 1, 1))
    upper = (step < half).astype(jnp.int32)
    slot = half - 1 - lax.rem(step, half)
    own = upper == core

    def settle(at):
        core_copy(at).wait_recv()
        mine[at] = (parts[at].astype(F32) + land[at].astype(F32)).astype(BF16)
        x_copy(at).start()

    @pl.when((step > 0) & ((step - 1 < half).astype(jnp.int32) == core))
    def _():
        settle(half - 1 - lax.rem(step - 1, half))

    @pl.when((step >= half) & (core == 0))
    def _():
        core_copy(slot).wait_send()

    parts[slot] = part.astype(parts.dtype)

    @pl.when(jnp.logical_not(own))
    def _():
        core_copy(slot).start()

    g_ws[...] += dot(d_step, low[...], 0, 0)[:8]
    g_wp[...] += dot(low[...], high, 0, 0) + dot(low[...], rest, 0, 0)
    g_wi[:model] += dot(low[...], inner, 0, 0)

    def norm_back(at):
        x_copy(at).wait_recv()
        block_rows = pl.ds(at * BLOCK, BLOCK)
        d_low = mine[at].astype(F32) + other[at].astype(F32)
        if at == half - 1:
            edge_copy(2, edge_ahead, {"seq": behind}).wait_recv()
            there = ((core == 1) & (seq < devices - 1)).astype(F32)
            d_low = jnp.concatenate([d_low[: BLOCK - 8], d_low[BLOCK - 8 :] + there * edge_ahead[...]], axis=0)
        rows = hid[block_rows, :].astype(F32)
        scale = lax.rsqrt(jnp.mean(rows * rows, axis=1, keepdims=True) + EPSILON)
        row[:1] += jnp.sum(d_low * rows * scale, axis=0, keepdims=True)
        scaled = d_low * gain[...]
        pull = jnp.mean(scaled * rows, axis=1, keepdims=True) * (scale * scale * scale)
        block = (d_out[block_rows, :] + scale * scaled - rows * pull).astype(BF16)
        grad_own[at] = block
        grad_copy(at).start()
        rows_at(grad_all, core * half + at, BLOCK)[...] = block

    if summing:

        @pl.when(step == half)
        def _():
            s_wo.pass_on()

        @pl.when(step == blocks - 2)
        def _():
            s_wg.pass_on()

    @pl.when(last)
    def _():
        before = jnp.concatenate([jnp.zeros_like(outer), outer], axis=0).astype(BF16)
        g_wi[:model] += dot(halo_low[...], before, 0, 0)
        before_p = jnp.concatenate([jnp.zeros_like(outer_p), outer_p], axis=0)
        high_p, rest_p = halves(before_p)
        g_wp[...] += dot(halo_low[...], high_p, 0, 0) + dot(halo_low[...], rest_p, 0, 0)
        edge_part = dot(before, wi[...], 1, 1) + (dot(high_p, wp[...], 1, 1) + dot(rest_p, wp[...], 1, 1))
        edge[0] = edge_part[8:]
        edge_copy(0, edge_core, beside).start()
        pack[:6] = small[:6]
        pack[6:7] = g_gain[...]
        pack[8:16] = g_ws[:, :width]
        pack[16:24] = g_ws[:, width:]
        pack[24:32, : heads.shape[1]] = heads[...]
        pair_small[:8] = small_p[...]
        if summing:
            for h_sum, _, _ in wide:
                h_sum.fold_core().start()
            s_wi.begin()
            s_pack.begin()

        @pl.when(core == 0)
        def _():
            settle(0)

        if summing:
            for h_sum, _, _ in wide:
                h_sum.fold()
        edge_copy(0, edge_core, beside).wait_recv()
        edge[1] = edge[0] + edge_core[...]
        edge_copy(1, edge_plane, across).start()
        if summing:
            s_wo.finish()
            s_wi.pass_on()
            s_wg.finish()
            s_pack.pass_on()
        edge_copy(1, edge_plane, across).wait_recv()
        edge[2] = edge[1] + edge_plane[...]
        edge_copy(2, edge_ahead, {"seq": behind}).start()
        for h_sum, s_sum, _ in wide:
            h_sum.settle()
            s_sum.begin()
        norm_back(2)
        norm_back(1)
        if summing:
            s_wo.collect()
            s_wi.finish()
            s_pack.finish()
        for _, s_sum, _ in wide:
            s_sum.pass_on()
        norm_back(0)
        norm_back(3)
        loop(1, group, lambda d: hand(d).start())
        if summing:
            s_wg.collect()
            for _, s_sum, _ in wide:
                s_sum.finish()
            s_wo.store(out_wo)
            for _, s_sum, _ in wide:
                s_sum.collect()
            s_wi.collect()
            s_pack.collect()
            for h_sum, s_sum, total in wide:
                s_sum.store(total)
                h_sum.spread(total)
            s_wg.store(out_wg)
            for h_sum, _, _ in wide:
                h_sum.spread_more()
            s_wi.store(out_wi)
            s_pack.store(out_pack)
            for (h_sum, _, _), out in zip(wide, (out_wp, out_small)):
                h_sum.finish()
                out[...] = h_sum.out[...]
            for s_sum in seq_sums:
                s_sum.drain()
        else:
            for out, ref in (
                (out_wo, g_wo), (out_wg, g_wg), (out_wi, g_wi), (out_pack, pack), (out_wp, g_wp), (out_small, pair_small),
            ):
                out[...] = ref[...]
        row_land[me] = row[...]
        loop(1, group, lambda d: hand(d).wait())
        sums[...] = lax.fori_loop(1, group, lambda d, total: total + row_land[d], row_land[0])
        for at, to in enumerate((beside, across, {"seq": behind})):
            edge_copy(at, edge_core, to).wait_send()

        @pl.when(core == 1)
        def _():
            loop(0, half, lambda at: core_copy(at).wait_send())

        def drain(at):
            x_copy(at).wait_send()
            grad_copy(at).wait()
            rows_at(grad_all, (1 - core) * half + at, BLOCK)[...] = grad_other[at]

        loop(0, half, drain)


def call(kernel, grid, ins, outs, scratch=(), prefetch=0, flops=0, moved=0, collective=None, vmem=14):
    def spec(shape, block, index):
        if block is None:
            return pl.BlockSpec(shape, lambda *_: (0,) * len(shape))
        if isinstance(block, str):
            return pl.BlockSpec(memory_space={"smem": pltpu.SMEM, "vmem": pltpu.VMEM, "any": pl.ANY}[block])
        return pl.BlockSpec(block, index)

    scalars = [a for a, *_ in ins[:prefetch]]
    arrays = ins[prefetch:]
    extra = {} if collective is None else {"collective_id": collective, "has_side_effects": True}
    return pl.pallas_call(
        kernel,
        grid_spec=pltpu.PrefetchScalarGridSpec(
            num_scalar_prefetch=prefetch,
            grid=(grid,),
            in_specs=[spec(a.shape, block, index) for a, block, index in arrays],
            out_specs=[spec(shape, block, index) for shape, _, block, index in outs],
            scratch_shapes=list(scratch),
        ),
        out_shape=[jax.ShapeDtypeStruct(shape, dtype) for shape, dtype, _, _ in outs],
        compiler_params=pltpu.CompilerParams(
            dimension_semantics=("arbitrary",), vmem_limit_bytes=vmem << 20, **extra
        ),
        cost_estimate=pl.CostEstimate(flops=int(flops), bytes_accessed=int(moved), transcendentals=0),
    )(*scalars, *[a for a, *_ in arrays])


def swap(value, axis, bit):
    route = [(i, i ^ bit) for i in range(lax.axis_size(axis))]
    return jax.tree.map(lambda v: lax.ppermute(v, axis, route), value)


def shifted(value, axis, distance):
    devices = range(lax.axis_size(axis))
    route = [(i - distance, i) for i in devices if i - distance in devices]
    return lax.ppermute(value, axis, route)


def bits(axis):
    size = lax.axis_size(axis)
    return [1 << b for b in range(size.bit_length() - 1)]


def total_over(value, axis):
    for bit in bits(axis):
        value = value + swap(value, axis, bit)
    return value


def carried(total, axis, backward):
    mine = lax.axis_index(axis)

    def join(early, late):
        decay = late[CHUNK : CHUNK + 1]
        return jnp.concatenate([late[:CHUNK] + decay * early[:CHUNK], late[CHUNK:] * early[CHUNK:]])

    reached = jnp.concatenate([jnp.zeros_like(total[:CHUNK]), jnp.ones_like(total[CHUNK:])])
    for bit in bits(axis):
        other = swap(total, axis, bit)
        later = ((mine & bit) == 0) if backward else ((mine & bit) != 0)
        reached = jnp.where(later, join(other, reached), reached)
        total = jnp.where(later, join(other, total), join(total, other))
    return reached[:CHUNK]


def padded(row, lanes=LANES):
    return jnp.zeros((1, lanes), F32).at[0, : row.shape[0]].set(row)


def shards(
    hidden, teacher, doc_starts, valid_mask, norm_gain, w_gate, w_inner, w_pair, w_step, conv_inner, bias_inner,
    conv_pair, bias_pair, step_bias, decay_log, skip_gain, gate_gain, w_output,
):
    rows, model = hidden.shape
    width = w_inner.shape[1]
    pair_width = w_pair.shape[1]
    heads = step_bias.shape[0]
    blocks, chunks = rows // BLOCK, rows // CHUNK
    per = BLOCK // CHUNK
    half = blocks // 2
    inner_total = float(width * lax.axis_size("head"))
    core = lax.axis_index("head") & 1
    offset = lax.axis_index("seq") * rows
    idx = jnp.stack([core, offset]).astype(jnp.int32)
    edge_rows = 16

    starts = jnp.full((1, LANES), FAR, F32).at[0, : doc_starts.shape[0]].set(doc_starts.astype(F32))
    ws = jnp.zeros((model, LANES), BF16).at[:, :heads].set(w_step)
    sbias, dlog = padded(step_bias), padded(decay_log)
    skip = jnp.repeat(skip_gain, HEAD_DIM)[None, :]
    gain, out_gain = norm_gain[None, :], gate_gain[None, :]
    conv_i, conv_p = conv_inner.astype(F32), conv_pair.astype(F32)
    bias_i, bias_p = bias_inner.astype(F32)[None, :], bias_pair.astype(F32)[None, :]
    valid = valid_mask[None, :]

    tail = shifted(hidden[rows - edge_rows :], "seq", 1)
    count = total_over(jnp.full((8, LANES), jnp.sum(valid_mask.astype(F32))), "seq")[0, 0]
    factor = (rows * lax.axis_size("seq")) / count

    def by(w, column=0):
        return (BLOCK, w), lambda i, *_: (i, column)

    def back(w, column=0):
        return (BLOCK, w), lambda i, *_: (blocks - 1 - i, column)

    row = ((1, BLOCK), lambda i, *_: (0, i))
    row_back = ((1, BLOCK), lambda i, *_: (0, blocks - 1 - i))
    grid3 = lambda n: ((per, n, width), lambda i, *_: (i, 0, 0))
    back3 = lambda n: ((per, n, width), lambda i, *_: (blocks - 1 - i, 0, 0))
    whole = (None, None)

    def send_order(w):
        return (BLOCK, w), lambda i: (lax.rem(i + half * (1 - core_bit()), blocks), 0)

    send_row = ((1, BLOCK), lambda i: (0, lax.rem(i + half * (1 - core_bit()), blocks)))
    half_own = lambda w: ((BLOCK, w), lambda i: (i + half * core_bit(), 0))
    tail_half = lambda w: ((BLOCK, w), lambda i: (jnp.maximum(i - half, 0), 0))
    dma = pltpu.SemaphoreType.DMA
    swap_scratch = [pltpu.VMEM((half, BLOCK, model), F32)] * 2 + [dma((half,))] * 2

    halo_block = ((edge_rows, model), lambda i, *_: (jnp.maximum(i * (BLOCK // edge_rows) - 1, 0), 0))
    (low, in_i, in_p, pre_i, pre_p, aux, halo_low, halo_i, halo_p, sloc, pkl, fin) = call(
        project_kernel,
        blocks,
        [
            (idx, None, None), (starts, *whole), (hidden, *by(model)), (hidden, *halo_block), (tail, *whole),
            (gain, *whole), (w_inner, *whole), (w_pair, *whole), (ws, *whole), (conv_i, *whole), (conv_p, *whole),
            (bias_i, *whole), (bias_p, *whole), (sbias, *whole), (dlog, *whole),
        ],
        [
            ((rows, model), BF16, *by(model)), ((rows, width), BF16, *by(width)), ((rows, pair_width), BF16, *by(pair_width)),
            ((rows, width), F32, *by(width)), ((rows, pair_width), F32, *by(pair_width)), ((rows, LANES), F32, *by(LANES)),
            ((edge_rows, model), BF16, *whole), ((edge_rows, width), BF16, *whole), ((edge_rows, pair_width), BF16, *whole),
            ((chunks, CHUNK, width), F32, *grid3(CHUNK)), ((chunks, 8, width), F32, *grid3(8)),
            ((CHUNK + 8, width), F32, *whole),
        ],
        [
            pltpu.VMEM((BLOCK + edge_rows, width), F32), pltpu.VMEM((BLOCK + edge_rows, pair_width), F32),
            pltpu.VMEM((CHUNK, width), F32), pltpu.VMEM((8, width), F32),
        ],
        prefetch=1, flops=3e9, moved=2e7,
    )
    state_in = carried(fin, "seq", False)
    gate, local = call(
        intra_kernel,
        blocks,
        [
            (idx, None, None), (low, *by(model)), (w_gate, *whole), (pre_i, *by(width)), (pre_p, *by(pair_width)),
            (aux, *by(LANES)), (skip, *whole),
        ],
        [((rows, width), F32, *by(width)), ((rows, width), F32, *by(width))],
        prefetch=1, flops=4e9, moved=2e7,
    )
    mixer, states, square = call(
        mix_kernel,
        blocks,
        [
            (pre_p, *by(LANES, 1)), (aux, *by(LANES)), (sloc, *grid3(CHUNK)), (pkl, *grid3(8)), (state_in, *whole),
            (local, *by(width)), (gate, *by(width)),
        ],
        [((rows, width), F32, *by(width)), ((chunks, CHUNK, width), F32, *grid3(CHUNK)), ((1, rows), F32, *row)],
        flops=1e9, moved=2e7,
    )
    square = total_over(square, "head")
    (mine,) = call(
        partial(branch_kernel, total=inner_total),
        blocks,
        [
            (mixer, *send_order(width)), (gate, *send_order(width)), (square, *send_row), (out_gain, *whole), (w_output, *whole),
        ],
        [((rows // 2, model), BF16, *tail_half(model))],
        swap_scratch,
        flops=1.2e9, moved=1e7, collective=2,
    )
    other = swap(mine, "head", 2)
    output, d_branch, d_out, error = call(
        loss_kernel,
        half,
        [
            (factor.reshape(1), "smem", None), (hidden, *half_own(model)), (teacher, *half_own(model)),
            (valid, (1, BLOCK), lambda i: (0, i + half * core_bit())), (mine, *by(model)), (other, *by(model)),
        ],
        [
            ((rows, model), BF16, "any", None), ((rows, model), BF16, "any", None),
            ((rows // 2, model), F32, *by(model)), ((1, model), F32, *whole),
        ],
        [pltpu.VMEM((half, BLOCK, model), BF16)] * 2 + [dma((2 * half,))] * 3,
        flops=1e8, moved=1.5e7, collective=3,
    )
    weighted, cross, g_gain, g_wo = call(
        partial(branch_back_kernel, total=inner_total),
        blocks,
        [
            (d_branch, *by(model)), (mixer, *by(width)), (gate, *by(width)), (square, *row), (out_gain, *whole),
            (w_output, *whole),
        ],
        [
            ((rows, width), F32, *by(width)), ((1, rows), F32, *row), ((1, width), F32, *whole),
            ((width, model), F32, *whole),
        ],
        flops=2.4e9, moved=1.5e7,
    )
    cross = total_over(cross, "head")
    d_mixer, d_gate, gloc, pkb, fin_back = call(
        partial(gate_back_kernel, total=inner_total),
        blocks,
        [
            (weighted, *back(width)), (mixer, *back(width)), (gate, *back(width)), (square, *row_back), (cross, *row_back),
            (pre_p, *back(LANES, 1)), (aux, *back(LANES)),
        ],
        [
            ((rows, width), F32, *back(width)), ((rows, width), BF16, *back(width)),
            ((chunks, CHUNK, width), F32, *back3(CHUNK)), ((chunks, 8, width), F32, *back3(8)), ((CHUNK + 8, width), F32, *whole),
        ],
        [pltpu.VMEM((CHUNK, width), F32), pltpu.VMEM((8, width), F32)],
        flops=1e9, moved=2e7,
    )
    grad_in = carried(fin_back, "seq", True)
    d_scaled, d_maps, g_wg = call(
        intra_back_kernel,
        blocks,
        [
            (idx, None, None), (d_mixer, *by(width)), (pre_i, *by(width)), (pre_p, *by(pair_width)), (aux, *by(LANES)),
            (low, *by(model)), (d_gate, *by(width)),
        ],
        [((rows, width), F32, *by(width)), ((rows, pair_width), F32, *by(pair_width)), ((model, width), F32, *whole)],
        prefetch=1, flops=6e9, moved=2e7,
    )
    size = lax.axis_size("seq")
    summing = size <= 8

    def piece(total_rows, tile):
        return -(-total_rows // (size * tile)) * tile

    r_wo, r_w, r_pack, r_wp, r_small = piece(width, 16), piece(model, 16), 8, piece(model // 4, 8), 8
    vmem = ("vmem", None)
    core_wire = F32 if summing else BF16
    once = lambda w: ((rows // 2, w), lambda i: (core_bit(), 0))
    sum_shapes = [(r_wo, model, BF16), (r_w, width, BF16), (r_w, width, BF16), (r_pack, width, F32), (r_wp, pair_width, F32),
                  (r_small, pair_width, F32)]
    n_wo, n_w, n_pack = (r_wo * size, r_w * size, r_pack * size) if summing else (width, model, 64)
    scratch = [pltpu.VMEM((BLOCK + 16, width), F32)] * 3 + [pltpu.VMEM((BLOCK + 16, pair_width), F32)] * 3 + [
        pltpu.VMEM((8, width), F32), pltpu.VMEM((8, pair_width), F32), pltpu.VMEM((8, LANES), F32),
        pltpu.VMEM((half, BLOCK, model), core_wire), pltpu.VMEM((half, BLOCK, model), core_wire),
        pltpu.VMEM((half, BLOCK, model), BF16), pltpu.VMEM((half, BLOCK, model), BF16),
        pltpu.VMEM((2, model), F32), pltpu.VMEM((2 * size, 2, model), F32),
        pltpu.VMEM((n_w, width), F32), pltpu.VMEM((8, model), F32), pltpu.VMEM((n_pack, width), F32),
        pltpu.VMEM((model, pair_width), F32), pltpu.VMEM((32, pair_width), F32),
        pltpu.VMEM((r_small * size, pair_width), F32), pltpu.VMEM((r_wp * size, pair_width), F32),
        pltpu.VMEM((model, pair_width), F32), pltpu.VMEM((32, pair_width), F32),
        pltpu.VMEM((half, BLOCK, model), BF16), pltpu.VMEM((half, BLOCK, model), BF16),
        pltpu.VMEM((3, 8, model), F32), pltpu.VMEM((8, model), F32), pltpu.VMEM((8, model), F32), pltpu.VMEM((8, model), F32),
        dma((half,)), dma((half,)), dma((half,)), dma((half,)), dma((3,)), dma((3,)), dma((half,)), dma((half,)),
        dma((2 * size,)), dma((2 * size,)),
    ]
    if summing:
        scratch += HeadSum.scratch(model, pair_width, r_wp * size) + HeadSum.scratch(32, pair_width, r_small * size)
        for r, lanes, wire in sum_shapes:
            scratch += SeqSum.scratch(r, lanes, wire, size)
    grad_hidden, sums, g_wo, g_wg, g_wi, pack, g_wp, small_p = call(
        finale_kernel,
        blocks,
        [
            (d_scaled, *back(width)), (d_maps, *back(pair_width)), (pre_i, *back(width)), (pre_p, *back(pair_width)),
            (in_i, *back(width)), (in_p, *back(pair_width)), (halo_low, *whole), (halo_i, *whole), (halo_p, *whole),
            (aux, *back(LANES)), (gloc, *back3(CHUNK)), (pkb, *back3(8)), (grad_in, *whole), (states, *back3(CHUNK)),
            (d_mixer, *back(width)), (mixer, *back(width)), (skip, *whole), (dlog, *whole), (conv_i, *whole), (conv_p, *whole),
            (low, *back(model)), (d_gate, *back(width)), (w_gate, *whole), (w_inner, *whole), (ws, *whole), (w_pair, *whole),
            (hidden, *once(model)), (d_out, *vmem), (gain, *whole), (error, *whole), (g_wo, *vmem), (g_wg, *vmem),
            (g_gain, *whole),
        ],
        [
            ((rows, model), BF16, *vmem), ((2, model), F32, *vmem), ((n_wo, model), F32, *vmem),
            ((n_w, width), F32, *vmem), ((n_w, width), F32, *vmem), ((n_pack, width), F32, *vmem),
            ((model, pair_width), F32, *vmem), ((32, pair_width), F32, *vmem),
        ],
        scratch,
        flops=9e9, moved=8e7, collective=4, vmem=58,
    )
    if not summing:
        g_wo, g_wg, g_wi, pack = lax.psum((g_wo, g_wg, g_wi, pack), "seq")
        g_wp, small_p = lax.psum((g_wp, small_p), ("seq", "head"))
    by_head, g_ws = pack[:8], jnp.concatenate([pack[8:16], pack[16:24]], axis=1)[:heads].T
    pair_small, head_small = small_p[:8], pack[24:32, :LANES]
    loss = jnp.sum(sums[1]) / (count * model)
    return (
        output, loss, grad_hidden, sums[0], g_wg, g_wi, g_wp, g_ws, by_head[:4], by_head[4], pair_small[:4], pair_small[4],
        head_small[0, :heads], head_small[1, :heads], jnp.sum(by_head[5].reshape(heads, HEAD_DIM), axis=1), by_head[6], g_wo,
    )


def solution(mesh):
    seq, head, wide = P("seq", None), P("head"), P(None, "head")
    in_specs = (
        seq, seq, P(), P("seq"), P(), wide, wide, P(), wide, wide, head, P(), P(), head, head, head, head, P("head", None),
    )
    out_specs = (
        seq, P(), seq, P(), wide, wide, P(), wide, wide, head, P(), P(), head, head, head, head, P("head", None),
    )
    return jax.shard_map(shards, mesh=mesh, in_specs=in_specs, out_specs=out_specs, check_vma=False)
```

```python
from functools import partial

import jax
import jax.numpy as jnp
from jax import lax
from jax.experimental import pallas as pl
from jax.experimental.pallas import tpu as pltpu
from jax.sharding import PartitionSpec as P

EPSILON = 1e-05
CHUNK = 128
BLOCK = 256
HEAD_DIM = 64
LANES = 128
FAR = float(1 << 24)
F32 = jnp.float32
BF16 = jnp.bfloat16
HIGHEST = lax.Precision.HIGHEST

DT, CUM, INFLOW, TAIL, RATE, START, END = 0, 8, 16, 24, 32, 40, 41


def dot(a, b, da=1, db=0):
    return lax.dot_general(a, b, (((da,), (db,)), ((), ())), preferred_element_type=F32)


def halves(v):
    high = v.astype(BF16)
    return high, (v - high.astype(F32)).astype(BF16)


def dot3(a, b, da=1, db=0):
    ah, al = halves(a)
    bh, bl = halves(b)
    return dot(ah, bh, da, db) + (dot(ah, bl, da, db) + dot(al, bh, da, db))


def column_sums(v):
    folded = v[:, :LANES]
    for at in range(LANES, v.shape[1], LANES):
        folded = folded + v[:, at : at + LANES]
    return jnp.sum(jnp.transpose(folded), axis=0, keepdims=True)


def as_column(row, width=LANES):
    column = jnp.transpose(jnp.broadcast_to(row, (LANES, row.shape[1])))
    return jnp.concatenate([column] * (width // LANES), axis=1)


def expand(table, base, width):
    rows = table.shape[0]
    lane = lax.broadcasted_iota(jnp.int32, (rows, LANES), 1)
    parts = []
    for pair in range(width // LANES):
        first = jnp.broadcast_to(table[:, base + 2 * pair : base + 2 * pair + 1], (rows, LANES))
        second = jnp.broadcast_to(table[:, base + 2 * pair + 1 : base + 2 * pair + 2], (rows, LANES))
        parts.append(jnp.where(lane < HEAD_DIM, first, second))
    return jnp.concatenate(parts, axis=1)


def head_matrix(width):
    channel = lax.broadcasted_iota(jnp.int32, (width, LANES), 0)
    head = lax.broadcasted_iota(jnp.int32, (width, LANES), 1)
    return ((channel >> 6) == head).astype(BF16)


def head_sums(v):
    high, low = halves(v)
    matrix = head_matrix(v.shape[1])
    return dot(high, matrix) + dot(low, matrix)


def triangle(upper):
    row = lax.broadcasted_iota(jnp.int32, (CHUNK, CHUNK), 0)
    col = lax.broadcasted_iota(jnp.int32, (CHUNK, CHUNK), 1)
    return ((col >= row) if upper else (col <= row)).astype(F32)


def silu_parts(pre):
    gate = jax.nn.sigmoid(pre)
    return pre * gate, gate * (1.0 + pre * (1.0 - gate))


def project_kernel(
    idx, given, valid, hid, halo, tail, gain, wi, wp, ws, conv_i, conv_p, bias_i, bias_p,
    low, low_t, in_i, in_p, pre_i, pre_p, aux, halo_low, halo_i, halo_p, sloc, pkl, fin, wide_i, wide_p, state, decay, counted,
):
    step = pl.program_id(0)
    edge = tail.shape[0]
    width = wi.shape[1]

    @pl.when(step == 0)
    def _():
        state[...] = jnp.zeros_like(state)
        decay[...] = jnp.ones_like(decay)
        counted[...] = jnp.zeros_like(counted)

    counted[...] += jnp.sum(valid[...].astype(F32), axis=1, keepdims=True)
    before = jnp.where(step == 0, tail[...].astype(F32), halo[...].astype(F32))
    rows = jnp.concatenate([before, hid[...].astype(F32)], axis=0)
    scale = lax.rsqrt(jnp.mean(rows * rows, axis=1, keepdims=True) + EPSILON)
    lowered = (rows * scale * gain[...]).astype(BF16)
    own = lowered[edge:]
    low[...] = own
    low_t[...] = jnp.transpose(own)
    inner = dot(lowered, wi[...]).astype(BF16)
    pair = dot(lowered, wp[...]).astype(BF16)
    in_i[...] = inner[edge:]
    in_p[...] = pair[edge:]
    wide_i[...] = inner.astype(F32)
    wide_p[...] = pair.astype(F32)

    @pl.when(step == 0)
    def _():
        halo_low[...] = lowered[:edge]
        halo_i[...] = inner[:edge]
        halo_p[...] = pair[:edge]

    base = idx[1] + step * BLOCK
    pos = (base + lax.broadcasted_iota(jnp.int32, (BLOCK, LANES), 0)).astype(F32)
    starts = given[3:4]
    begun = starts <= pos
    start = jnp.max(jnp.where(begun, starts, -1.0), axis=1, keepdims=True)
    end = jnp.min(jnp.where(begun, FAR, starts), axis=1, keepdims=True)
    within = pos[:, :1] - start
    keep = [(within >= float(3 - k)).astype(F32) for k in range(3)]

    def convolve(wide, weight, bias):
        taps = weight[...].astype(F32)
        total = bias[...].astype(F32) + wide[edge : edge + BLOCK] * taps[3:4]
        for k in range(3):
            total = total + wide[edge - 3 + k : edge - 3 + k + BLOCK] * taps[k : k + 1] * keep[k]
        return total

    conv_inner = convolve(wide_i, conv_i, bias_i)
    conv_pair = convolve(wide_p, conv_p, bias_p)
    pre_i[...] = conv_inner
    pre_p[...] = conv_pair
    values = conv_inner * jax.nn.sigmoid(conv_inner)
    maps = conv_pair[:, :LANES]
    maps = maps * jax.nn.sigmoid(maps)

    raw = dot(own, ws[...]) + given[0:1]
    dt = jnp.maximum(raw, 0.0) + jnp.log1p(jnp.exp(-jnp.abs(raw)))
    rate = jax.nn.sigmoid(raw)
    logs = -dt * jnp.exp(given[1:2])
    lane = lax.broadcasted_iota(jnp.int32, (CHUNK, LANES), 1)
    lower = triangle(False)
    for c in range(BLOCK // CHUNK):
        at = slice(c * CHUNK, (c + 1) * CHUNK)
        cum = jnp.dot(lower, logs[at], precision=HIGHEST, preferred_element_type=F32)
        last = cum[CHUNK - 1 :]
        first = (base + c * CHUNK).astype(F32)
        inflow = jnp.exp(cum) * (start[at] <= first - 1.0).astype(F32)
        outflow = jnp.exp(last - cum) * (end[at] > first + (CHUNK - 1.0)).astype(F32)
        table = jnp.where(lane < CUM, dt[at], pltpu.roll(cum, CUM, 1))
        table = jnp.where(lane < INFLOW, table, pltpu.roll(inflow, INFLOW, 1))
        table = jnp.where(lane < TAIL, table, pltpu.roll(outflow, TAIL, 1))
        table = jnp.where(lane < RATE, table, pltpu.roll(rate[at], RATE, 1))
        table = jnp.where(lane < START, table, jnp.where(lane < END, start[at], end[at]))
        aux[at, :] = table
        scaled = values[at] * expand(table, DT, width) * expand(table, TAIL, width)
        added = dot3(maps[at], scaled, 0, 0)
        kept = expand(jnp.broadcast_to(inflow[CHUNK - 1 :], (8, LANES)), 0, width)
        sloc[c] = state[...]
        pkl[c] = decay[...]
        state[...] = state[...] * kept[:1] + added
        decay[...] = decay[...] * kept
    fin[:CHUNK] = state[...]
    fin[CHUNK:] = jnp.concatenate([decay[:7], jnp.broadcast_to(counted[...], (1, width))], axis=0)


def masks(table, first, transposed):
    row = lax.broadcasted_iota(jnp.int32, (CHUNK, CHUNK), 0)
    col = lax.broadcasted_iota(jnp.int32, (CHUNK, CHUNK), 1)
    at = (first + col).astype(F32)
    if transposed:
        return (col >= row) & (at < table[:, END : END + 1])
    return (col <= row) & (at >= table[:, START : START + 1])


def head_split(v, pair):
    lane = lax.broadcasted_iota(jnp.int32, (v.shape[0], LANES), 1)
    part = v[:, pair * LANES : (pair + 1) * LANES]
    return jnp.concatenate(
        [jnp.where(lane < HEAD_DIM, part, 0.0), jnp.where(lane < HEAD_DIM, 0.0, part)], axis=0
    ).astype(BF16)


def intra_kernel(idx, low, wg, pre_i, pre_p, aux, given, gate, mixed):
    width = wg.shape[1]
    skip = expand(given[...], 0, width)[2:3]
    gate[...] = dot(low[...], wg[...])
    base = idx[1] + pl.program_id(0) * BLOCK
    maps, _ = silu_parts(pre_p[...])
    values, _ = silu_parts(pre_i[...])
    for c in range(BLOCK // CHUNK):
        at = slice(c * CHUNK, (c + 1) * CHUNK)
        table = aux[at, :]
        rows = jnp.transpose(table)
        joined = masks(table, base + c * CHUNK, False)
        scores = dot(maps[at, LANES:].astype(BF16), maps[at, :LANES].astype(BF16), 1, 1)
        scaled = values[at] * expand(table, DT, width)
        parts = []
        for pair in range(width // LANES):
            weights = []
            for h in (2 * pair, 2 * pair + 1):
                gap = table[:, CUM + h : CUM + h + 1] - rows[CUM + h : CUM + h + 1, :]
                weights.append((scores * jnp.exp(jnp.where(joined, gap, -1e30))).astype(BF16))
            parts.append(dot(jnp.concatenate(weights, axis=1), head_split(scaled, pair)))
        mixed[at, :] = jnp.concatenate(parts, axis=1) + values[at] * skip


def core_bit():
    return lax.rem(lax.axis_index("head"), 2)


def core_peer():
    return lax.axis_index("head") + 1 - 2 * core_bit()


def mid_kernel(
    factor, pre_c, aux, sloc, pkl, sin, local, gate, gain, wo, hid, teacher, valid,
    states, d_mixer, d_gate, gloc, pkb, fin, out, d_out, error, g_gain, g_wo,
    mix, squares, square_land, crosses, cross_land, scales, parts, land, mine, other, d_branch, out_block, weighted, keeps,
    state, wo_t, square_send, square_got, cross_send, cross_got, core_send, core_land, x_send, x_land, grad_send, grad_land,
    out_local, out_send, out_land, *, total,
):
    step = pl.program_id(0)
    half = mine.shape[0]
    blocks = 2 * half
    width = local.shape[1]
    head, core = lax.axis_index("head"), core_bit()
    beside, across = {"head": core_peer()}, {"head": lax.rem(head + 2, 4)}

    def to_head(distance):
        return {"head": lax.rem(head + distance, 4)}

    def square_copy(block, d):
        return device_copy(squares.at[block], square_land.at[d, block], (square_send, square_got), 4 * block + d, to_head(d))

    def cross_copy(block, d):
        return device_copy(crosses.at[block], cross_land.at[d, block], (cross_send, cross_got), 4 * block + d, to_head(d))

    def core_copy(slot):
        return device_copy(parts.at[slot], land.at[slot], (core_send, core_land), slot, beside)

    def x_copy(slot):
        return device_copy(mine.at[slot], other.at[slot], (x_send, x_land), slot, across)

    def grad_copy(block):
        return device_copy(d_branch.at[block], d_branch.at[block], (grad_send, grad_land), block, beside)

    def out_copies(slot):
        rows = rows_at(out, core * half + slot, BLOCK)
        here = pltpu.make_async_copy(out_block.at[slot], rows, out_local.at[slot])
        return here, device_copy(out_block.at[slot], rows, (out_send, out_land), slot, beside)

    def gate_rows(block):
        return gate[pl.ds(pl.multiple_of(block * BLOCK, BLOCK), BLOCK), :]

    def settle(slot):
        core_copy(slot).wait_recv()
        mine[slot] = (parts[slot] + land[slot]).astype(BF16)
        x_copy(slot).start()

    @pl.when(step == 0)
    def _():
        barrier = pltpu.get_barrier_semaphore()

        def greet(d):
            pl.semaphore_signal(barrier, inc=1, device_id=to_head(d), device_id_type=pl.DeviceIdType.MESH)

        loop(1, 4, greet)
        for ref in (error, g_gain, g_wo):
            ref[...] = jnp.zeros_like(ref)
        wo_t[...] = jnp.transpose(wo[...])
        pl.semaphore_wait(barrier, 3)

    @pl.when(step < blocks)
    def _():
        reads, _ = silu_parts(pre_c[...])
        for c in range(BLOCK // CHUNK):
            at = slice(c * CHUNK, (c + 1) * CHUNK)
            now = sloc[c] + pkl[c, :1] * sin[...]
            states[c] = now
            mix[step, at, :] = local[at, :] + expand(aux[at, :], INFLOW, width) * dot3(reads[at], now)
        act, _ = silu_parts(gate_rows(step))
        gated = mix[step] * act
        squares[step] = column_sums(gated * gated)
        loop(1, 4, lambda d: square_copy(step, d).start())

    @pl.when((step > blocks) & (step <= 2 * blocks) & ((step - blocks - 1) // half == core))
    def _():
        settle(lax.rem(step - blocks - 1, half))

    @pl.when((step >= blocks) & (step < 2 * blocks))
    def _():
        block = step - blocks
        slot = lax.rem(block, half)
        own = block // half == core

        def add(d, sum_row):
            square_copy(block, d).wait_recv()
            return sum_row + square_land[d, block]

        row = lax.rsqrt(lax.fori_loop(1, 4, add, squares[block]) / total + EPSILON)
        scales[block] = row
        act, _ = silu_parts(gate_rows(block))
        normed = (mix[block] * act * as_column(row, width) * gain[...]).astype(BF16)

        @pl.when(own & (core == 1))
        def _():
            core_copy(slot).wait_send()

        parts[slot] = dot(normed, wo[...])

        @pl.when(jnp.logical_not(own))
        def _():
            core_copy(slot).start()

    @pl.when((step >= 2 * blocks) & (step < 3 * blocks))
    def _():
        block = step - 2 * blocks
        slot = lax.rem(block, half)
        own = block // half == core

        @pl.when(own)
        def _():
            x_copy(slot).wait_recv()
            at = pl.ds(pl.multiple_of(slot * BLOCK, BLOCK), BLOCK)
            outf = hid[at, :].astype(F32) + (mine[slot].astype(F32) + other[slot].astype(F32))
            term = outf - teacher[at, :].astype(F32)
            masked = as_column(valid[...].astype(F32), term.shape[1]) * term
            error[...] += jnp.sum(masked * term, axis=0, keepdims=True)
            grad = masked * factor[0]
            d_out[...] = grad
            d_branch[block] = grad.astype(BF16)
            grad_copy(block).start()
            out_block[slot] = outf.astype(BF16)
            for copy in out_copies(slot):
                copy.start()

        @pl.when(jnp.logical_not(own))
        def _():
            grad_copy(block).wait_recv()

        act, _ = silu_parts(gate_rows(block))
        gated = mix[block] * act
        scaled = gated * as_column(scales[block], width)
        normed = (scaled * gain[...]).astype(BF16)
        grads = d_branch[block]
        g_wo[...] += dot(normed, grads, 0, 0)
        d_normed = dot(grads, wo_t[...])
        g_gain[...] += jnp.sum(d_normed * scaled, axis=0, keepdims=True)
        pulled = d_normed * gain[...]
        weighted[lax.rem(block, 2)] = pulled
        crosses[block] = column_sums(pulled * gated)
        loop(1, 4, lambda d: cross_copy(block, d).start())

    @pl.when(step > 2 * blocks)
    def _():
        block = step - 2 * blocks - 1

        def add(d, sum_row):
            cross_copy(block, d).wait_recv()
            return sum_row + cross_land[d, block]

        cross = lax.fori_loop(1, 4, add, crosses[block])
        act, slope = silu_parts(gate_rows(block))
        gated = mix[block] * act
        row = scales[block]
        pull = as_column(row * row * row * cross / total, width)
        d_gated = as_column(row, width) * weighted[lax.rem(block, 2)] - gated * pull
        dy = d_gated * act
        d_mixer[...] = dy
        d_gate[...] = (d_gated * mix[block] * slope).astype(BF16)
        reads, _ = silu_parts(pre_c[...])
        for c in range(BLOCK // CHUNK):
            at = slice(c * CHUNK, (c + 1) * CHUNK)
            inflow = expand(aux[at, :], INFLOW, width)
            keeps[block * (BLOCK // CHUNK) + c] = jnp.broadcast_to(inflow[CHUNK - 1 :], (8, width))
            gloc[block * (BLOCK // CHUNK) + c] = dot3(reads[at], dy[at] * inflow, 0, 0)

    @pl.when(step == 3 * blocks)
    def _():
        state[...] = jnp.zeros_like(state)
        chunks = gloc.shape[0]

        def back(i, decay):
            c = chunks - 1 - i
            added = gloc[c]
            gloc[c] = state[...]
            pkb[c] = decay
            state[...] = state[...] * keeps[c, :1] + added
            return decay * keeps[c]

        decay = lax.fori_loop(0, chunks, back, jnp.ones((8, width), F32))
        fin[:CHUNK] = state[...]
        fin[CHUNK:] = decay

        def drain(block):
            def both(d):
                square_copy(block, d).wait_send()
                cross_copy(block, d).wait_send()

            loop(1, 4, both)

            @pl.when(block // half == core)
            def _():
                grad_copy(block).wait_send()

        loop(0, blocks, drain)

        @pl.when(core == 0)
        def _():
            loop(0, half, lambda slot: core_copy(slot).wait_send())

        def finish(slot):
            x_copy(slot).wait_send()
            here, there = out_copies(slot)
            here.wait()
            there.wait()

        loop(0, half, finish)


def intra_back_kernel(idx, d_mixer, pre_i, pre_p, aux, low_t, d_gate, d_scaled, d_maps, g_wg):
    @pl.when(pl.program_id(0) == 0)
    def _():
        g_wg[...] = jnp.zeros_like(g_wg)

    g_wg[...] += dot(low_t[...], d_gate[...])
    width = d_mixer.shape[1]
    base = idx[1] + pl.program_id(0) * BLOCK
    maps, _ = silu_parts(pre_p[...])
    values, _ = silu_parts(pre_i[...])
    for c in range(BLOCK // CHUNK):
        at = slice(c * CHUNK, (c + 1) * CHUNK)
        table = aux[at, :]
        rows = jnp.transpose(table)
        joined = masks(table, base + c * CHUNK, True)
        keys = maps[at, :LANES].astype(BF16)
        reads = maps[at, LANES:].astype(BF16)
        scores = dot(keys, reads, 1, 1)
        scaled = (values[at] * expand(table, DT, width)).astype(BF16)
        grads = d_mixer[at, :]
        d_scores = jnp.zeros((CHUNK, CHUNK), F32)
        parts = []
        for pair in range(width // LANES):
            split = head_split(grads, pair)
            d_weights = dot(scaled[:, pair * LANES : (pair + 1) * LANES], split, 1, 1)
            weights = []
            for side in range(2):
                h = 2 * pair + side
                gap = rows[CUM + h : CUM + h + 1, :] - table[:, CUM + h : CUM + h + 1]
                factor = jnp.exp(jnp.where(joined, gap, -1e30))
                weights.append((scores * factor).astype(BF16))
                d_scores = d_scores + factor * d_weights[:, side * CHUNK : (side + 1) * CHUNK]
            parts.append(dot(jnp.concatenate(weights, axis=1), split))
        d_scaled[at, :] = jnp.concatenate(parts, axis=1)
        low_scores = d_scores.astype(BF16)
        d_maps[at, :] = jnp.concatenate([dot(low_scores, reads), dot(low_scores, keys, 0, 0)], axis=1)


def conv_back(grad, within, inputs, edge_inputs, weight, shifted, first, last, acc):
    rows = grad.shape[0]

    @pl.when(first)
    def _():
        for ref in shifted:
            ref[...] = jnp.zeros_like(ref)

    weight = weight[...].astype(F32)
    total = grad * weight[3:4]
    edge = jnp.zeros((8, grad.shape[1]), F32)
    acc[3:4] += jnp.sum(grad * inputs, axis=0, keepdims=True)
    acc[4:5] += jnp.sum(grad, axis=0, keepdims=True)
    for k, ref in enumerate(shifted):
        ref[8 : 8 + rows] = grad * (within >= float(3 - k)).astype(F32)
        moved = ref[3 - k : 3 - k + 8 + rows]
        total = total + moved[8:] * weight[k : k + 1]
        edge = edge + moved[:8] * weight[k : k + 1]
        outer = jnp.where(last, edge_inputs, 0.0) * moved[:8]
        acc[k : k + 1] += jnp.sum(moved[8:] * inputs, axis=0, keepdims=True) + jnp.sum(outer, axis=0, keepdims=True)
        ref[8 + rows :] = ref[8:16]
    return total, edge


def device_copy(src, dst, sems, slot, to):
    return pltpu.make_async_remote_copy(
        src_ref=src, dst_ref=dst, send_sem=sems[0].at[slot], recv_sem=sems[1].at[slot],
        device_id=to, device_id_type=pl.DeviceIdType.MESH,
    )


def loop(start, stop, body):
    def run(d, carry):
        body(d)
        return carry

    lax.fori_loop(start, stop, run, 0)


def rows_at(ref, index, size):
    return ref.at[pl.ds(pl.multiple_of(index * size, size), size)]


class SeqSum:
    def __init__(self, source, first, land1, second, land2, done, sems):
        self.source, self.first, self.land1, self.second, self.land2, self.done = source, first, land1, second, land2, done
        self.sems = [sems[i : i + 2] for i in range(0, 8, 2)]
        self.wire = first.dtype
        self.members = land2.shape[0]
        self.piece = first.shape[0] // self.members
        me = lax.axis_index("seq")
        self.side, self.place = lax.rem(me, 2), me // 2
        self.partner = {"seq": me + 1 - 2 * self.side}

    def half(self, ref, side):
        return rows_at(ref, side, self.members * self.piece)

    def member(self, d):
        return lax.rem(self.place + d, self.members)

    def to_member(self, d):
        return {"seq": 2 * self.member(d) + self.side}

    def halve(self):
        return device_copy(self.first, self.land1, self.sems[0], 0, self.partner)

    def scatter(self, d):
        src = rows_at(self.second, self.member(d), self.piece)
        return device_copy(src, self.land2.at[d], self.sems[1], d, self.to_member(d))

    def part(self, place):
        return rows_at(self.done, self.side * self.members + place, self.piece)

    def gather(self, d):
        ref = self.part(self.place)
        return device_copy(ref, ref, self.sems[2], d, self.to_member(d))

    def gathered(self, d):
        ref = self.part(lax.rem(self.place + self.members - d, self.members))
        return device_copy(ref, ref, self.sems[2], d, self.partner)

    def widen(self, side):
        ref = self.half(self.done, side)
        return device_copy(ref, ref, self.sems[3], 0, self.partner)

    def begin(self):
        self.first[...] = self.half(self.source, 1 - self.side)[...].astype(self.wire)
        self.halve().start()

    def pass_on(self):
        self.halve().wait_recv()
        self.second[...] = (self.half(self.source, self.side)[...] + self.land1[...].astype(F32)).astype(self.wire)
        loop(1, self.members, lambda d: self.scatter(d).start())

    def finish(self):
        own = rows_at(self.source, self.side * self.members + self.place, self.piece)[...]
        own = own + rows_at(self.land1, self.place, self.piece)[...].astype(F32)

        def add(d, total):
            self.scatter(d).wait_recv()
            return total + self.land2[d].astype(F32)

        self.part(self.place)[...] = lax.fori_loop(1, self.members, add, own).astype(self.wire)
        loop(1, self.members, lambda d: self.gather(d).start())

    def collect(self):
        loop(1, self.members, lambda d: self.gathered(d).wait_recv())
        self.widen(self.side).start()

    def store(self, out):
        self.half(out, self.side)[...] = self.half(self.done, self.side)[...].astype(F32)
        self.widen(1 - self.side).wait_recv()
        self.half(out, 1 - self.side)[...] = self.half(self.done, 1 - self.side)[...].astype(F32)

    def drain(self):
        self.halve().wait_send()
        self.widen(self.side).wait_send()

        def both(d):
            self.scatter(d).wait_send()
            self.gather(d).wait_send()

        loop(1, self.members, both)

    @staticmethod
    def scratch(rows, lanes, wire, size):
        members = size // 2
        half = pltpu.VMEM((members * rows, lanes), wire)
        dma = pltpu.SemaphoreType.DMA
        return [half, half, half, pltpu.VMEM((members, rows, lanes), wire), pltpu.VMEM((2 * members * rows, lanes), wire)] + [
            dma((1,)), dma((1,)), dma((members,)), dma((members,)), dma((members,)), dma((members,)), dma((1,)), dma((1,)),
        ]


SUM_REFS = 13


class HeadSum:
    def __init__(self, source, out, fold1, half, fold2, quarter, sems):
        self.source, self.out, self.fold1, self.held, self.fold2, self.quarter = source, out, fold1, half, fold2, quarter
        self.sems = [sems[i : i + 2] for i in range(0, 8, 2)]
        self.rows = source.shape[0]
        head = lax.axis_index("head")
        self.core, self.plane = lax.rem(head, 2), head // 2
        self.beside, self.across = {"head": head + 1 - 2 * self.core}, {"head": head + 2 - 4 * self.plane}

    def fold_core(self):
        return device_copy(rows_at(self.source, 1 - self.core, self.rows // 2), self.fold1, self.sems[0], 0, self.beside)

    def fold_plane(self):
        return device_copy(rows_at(self.held, 1 - self.plane, self.rows // 4), self.fold2, self.sems[1], 0, self.across)

    def spread_plane(self, plane):
        ref = rows_at(self.out, 2 * self.core + plane, self.rows // 4)
        return device_copy(ref, ref, self.sems[2], 0, self.across)

    def spread_core(self, core):
        ref = rows_at(self.out, core, self.rows // 2)
        return device_copy(ref, ref, self.sems[3], 0, self.beside)

    def fold(self):
        self.fold_core().wait_recv()
        self.held[...] = rows_at(self.source, self.core, self.rows // 2)[...] + self.fold1[...]
        self.fold_plane().start()

    def settle(self):
        self.fold_plane().wait_recv()
        self.quarter[...] = jnp.zeros_like(self.quarter)
        self.quarter[: self.rows // 4] = rows_at(self.held, self.plane, self.rows // 4)[...] + self.fold2[...]

    def spread(self, total):
        rows_at(self.out, 2 * self.core + self.plane, self.rows // 4)[...] = total[: self.rows // 4]
        self.spread_plane(self.plane).start()

    def spread_more(self):
        self.spread_plane(1 - self.plane).wait_recv()
        self.spread_core(self.core).start()

    def finish(self):
        self.spread_core(1 - self.core).wait_recv()
        self.fold_core().wait_send()
        self.fold_plane().wait_send()
        self.spread_plane(self.plane).wait_send()
        self.spread_core(self.core).wait_send()

    @staticmethod
    def scratch(rows, lanes, padded_rows):
        dma = pltpu.SemaphoreType.DMA
        shapes = [(rows // 2, lanes), (rows // 2, lanes), (rows // 4, lanes), (padded_rows, lanes)]
        return [pltpu.VMEM(shape, F32) for shape in shapes] + [dma((1,))] * 8


HEAD_REFS = 12


def finale_kernel(
    d_scaled, d_maps, pre_i, pre_p, in_i, in_p, halo_low, halo_i, halo_p, aux, gloc, pkl, gin, states, d_mixer, mixer, given,
    conv_i, conv_p, low_t, d_gate, wg, wi, ws, wp, hid, d_out, gain, error, g_wo, g_wg, g_gain, factor,
    grad_all, out_norm, out_loss, out_wo, out_wg, out_wi, out_wp, out_ws, out_conv_i, out_bias_i, out_conv_p, out_bias_p,
    out_sbias, out_dlog, out_skip, out_gain,
    shift_i0, shift_i1, shift_i2, shift_p0, shift_p1, shift_p2, small, small_p, heads,
    parts, land, mine, other, row, row_land, g_wi, g_ws, pack, g_wp, pair_small, sum_small, sum_wp, sum_pack, spread_wp, spread_small,
    grad_own, grad_other, wg_t, wi_t, ws_t, wp_t, edge, edge_core, edge_plane, edge_ahead,
    core_send, core_land, x_send, x_land, edge_send, edge_land, grad_send, grad_land, row_send, row_arrive, *more,
):
    shifted = (shift_i0, shift_i1, shift_i2, shift_p0, shift_p1, shift_p2)
    step = pl.program_id(0)
    blocks = pl.num_programs(0)
    half = blocks // 2
    first, last = step == 0, step == blocks - 1
    seq, devices = lax.axis_index("seq"), lax.axis_size("seq")
    head, core = lax.axis_index("head"), core_bit()
    width = wi.shape[1]
    model = low_t.shape[0]
    behind, ahead = lax.rem(seq + devices - 1, devices), lax.rem(seq + 1, devices)
    group = 2 * devices
    me = 2 * seq + core
    beside, across = {"head": core_peer()}, {"head": lax.rem(head + 2, 4)}
    summing = len(more) > 0

    more = list(more)

    def take(number):
        taken = more[:number]
        del more[:number]
        return taken

    seq_sums, wide = [], []
    if summing:
        head_parts = []
        for source, out in ((g_wp, spread_wp), (pair_small, spread_small)):
            refs = take(HEAD_REFS)
            head_parts.append(HeadSum(source, out, *refs[:4], refs[4:]))
        third = model // 3
        thirds = [g_wi.at[pl.ds(i * third, third)] for i in range(3)]
        outs_wi = [out_wi.at[pl.ds(i * third, third)] for i in range(3)]
        for source in (g_wo, g_wg, *thirds, pack, head_parts[0].quarter, head_parts[1].quarter):
            refs = take(SUM_REFS)
            seq_sums.append(SeqSum(source, *refs[:5], refs[5:]))
        s_wo, s_wg, *s_wi, s_pack, s_wp, s_small = seq_sums
        wide = list(zip(head_parts, (s_wp, s_small), (sum_wp, sum_small)))

    def device(distance):
        to = lax.rem(me + distance, group)
        return {"seq": to // 2, "head": head - core + lax.rem(to, 2)}

    def hand(distance):
        return device_copy(row, row_land.at[me], (row_send, row_arrive), distance, device(distance))

    def edge_copy(slot, landing, to):
        return device_copy(edge.at[slot], landing, (edge_send, edge_land), slot, to)

    def core_copy(slot):
        return device_copy(parts.at[slot], land.at[slot], (core_send, core_land), slot, beside)

    def x_copy(slot):
        return device_copy(mine.at[slot], other.at[slot], (x_send, x_land), slot, across)

    def grad_copy(slot):
        return device_copy(grad_own.at[slot], grad_other.at[slot], (grad_send, grad_land), slot, beside)

    @pl.when(first)
    def _():
        barrier = pltpu.get_barrier_semaphore()

        def greet(to):
            pl.semaphore_signal(barrier, inc=1, device_id=to, device_id_type=pl.DeviceIdType.MESH)

        loop(1, group, lambda d: greet(device(d)))
        greet(across)
        for ref in (g_wi, g_ws, pack, g_wp, pair_small, small, small_p, heads):
            ref[...] = jnp.zeros_like(ref)
        row[:1] = jnp.zeros_like(row[:1])
        row[1:] = error[...]
        for ref, weight in ((wg_t, wg), (wi_t, wi), (ws_t, ws), (wp_t, wp)):
            ref[...] = jnp.transpose(weight[...])
        pl.semaphore_wait(barrier, group)
        if summing:
            s_wo.begin()
            s_wg.begin()

    base = seq * (blocks * BLOCK) + (blocks - 1 - step) * BLOCK
    maps, slope_p = silu_parts(pre_p[...])
    values, slope = silu_parts(pre_i[...])
    dy = d_mixer[...]
    upper = triangle(True)
    lane = lax.broadcasted_iota(jnp.int32, (CHUNK, LANES), 1)
    grown = jnp.exp(given[1:2])
    skip = expand(given[...], 0, width)[2:3]
    pieces, pieces_p, pieces_s = [], [], []
    for c in range(BLOCK // CHUNK):
        at = slice(c * CHUNK, (c + 1) * CHUNK)
        table = aux[at, :]
        sizes = expand(table, DT, width)
        inflow = expand(table, INFLOW, width)
        outflow = expand(table, TAIL, width)
        keys, reads = maps[at, :LANES], maps[at, LANES:]
        scaled = values[at] * sizes
        grad_state = gloc[c] + pkl[c, :1] * gin[...]
        state = states[c]
        passed = outflow * dot3(keys, grad_state)
        total = d_scaled[at, :] + passed
        d_reads = d_maps[at, LANES:] + dot3(dy[at] * inflow, state, 1, 1)
        d_keys = d_maps[at, :LANES] + dot3(scaled * outflow, grad_state, 1, 1)
        pieces_p.append(jnp.concatenate([d_keys, d_reads], axis=1))
        plain = mixer[at, :] - skip * values[at]
        d_cum = head_sums(dy[at] * plain - scaled * total)
        carried = jnp.sum(grad_state * state, axis=0, keepdims=True) * inflow[CHUNK - 1 :]
        carried = carried + jnp.sum(scaled * passed, axis=0, keepdims=True)
        after = head_sums(jnp.broadcast_to(carried, (8, width)))[:1]
        d_logs = jnp.dot(upper, d_cum, precision=HIGHEST, preferred_element_type=F32) + after
        d_raw = (head_sums(total * values[at]) - grown * d_logs) * pltpu.roll(table, LANES - RATE, 1)
        d_raw = jnp.where(lane < 8, d_raw, 0.0)
        pieces_s.append(d_raw.astype(BF16))
        d_decay = jnp.where(lane < 8, -d_logs * table * grown, 0.0)
        heads[0:1] += jnp.sum(d_raw, axis=0, keepdims=True)
        heads[1:2] += jnp.sum(d_decay, axis=0, keepdims=True)
        pieces.append(total * sizes + dy[at] * skip)
    small[5:6] += jnp.sum(dy * values, axis=0, keepdims=True)
    grad = jnp.concatenate(pieces, axis=0) * slope
    pos = (base + lax.broadcasted_iota(jnp.int32, (BLOCK, 1), 0)).astype(F32)
    within = pos - aux[:, START : START + 1]
    whole, outer = conv_back(
        grad, within, in_i[...].astype(F32), halo_i[8:].astype(F32), conv_i, shifted[:3], first, last, small
    )
    grad_p = jnp.concatenate(pieces_p, axis=0) * slope_p
    whole_p, outer_p = conv_back(
        grad_p, within, in_p[...].astype(F32), halo_p[8:].astype(F32), conv_p, shifted[3:], first, last, small_p
    )

    inner = whole.astype(BF16)
    d_step = jnp.concatenate(pieces_s, axis=0)
    part = dot(d_gate[...], wg_t[...]) + dot(inner, wi_t[...]) + dot(d_step, ws_t[...])
    high, rest = halves(whole_p)
    part = part + (dot(high, wp_t[...]) + dot(rest, wp_t[...]))
    upper = (step < half).astype(jnp.int32)
    slot = half - 1 - lax.rem(step, half)
    own = upper == core

    def settle(at):
        core_copy(at).wait_recv()
        mine[at] = (parts[at].astype(F32) + land[at].astype(F32)).astype(BF16)
        x_copy(at).start()

    @pl.when((step > 0) & ((step - 1 < half).astype(jnp.int32) == core))
    def _():
        settle(half - 1 - lax.rem(step - 1, half))

    @pl.when((step >= half) & (core == 0))
    def _():
        core_copy(slot).wait_send()

    parts[slot] = part.astype(parts.dtype)

    @pl.when(jnp.logical_not(own))
    def _():
        core_copy(slot).start()

    g_ws[...] += dot(low_t[...], d_step)
    g_wp[...] += dot(low_t[...], high) + dot(low_t[...], rest)
    g_wi[:model] += dot(low_t[...], inner)

    def norm_back(at):
        x_copy(at).wait_recv()
        block_rows = pl.ds(at * BLOCK, BLOCK)
        d_low = mine[at].astype(F32) + other[at].astype(F32)
        if at == half - 1:
            edge_copy(2, edge_ahead, {"seq": behind}).wait_recv()
            there = ((core == 1) & (seq < devices - 1)).astype(F32)
            d_low = jnp.concatenate([d_low[: BLOCK - 8], d_low[BLOCK - 8 :] + there * edge_ahead[...]], axis=0)
        rows = hid[block_rows, :].astype(F32)
        scale = lax.rsqrt(jnp.mean(rows * rows, axis=1, keepdims=True) + EPSILON)
        row[:1] += jnp.sum(d_low * rows * scale, axis=0, keepdims=True)
        scaled = d_low * gain[...]
        pull = jnp.mean(scaled * rows, axis=1, keepdims=True) * (scale * scale * scale)
        block = (d_out[block_rows, :] + scale * scaled - rows * pull).astype(BF16)
        grad_own[at] = block
        grad_copy(at).start()
        rows_at(grad_all, core * half + at, BLOCK)[...] = block

    if summing:

        moves = (s_wo.pass_on, s_wg.pass_on, s_wo.finish, s_wg.finish, s_wo.collect)
        for number, move in enumerate(moves):

            @pl.when(step == number + 2)
            def _(move=move):
                move()

    @pl.when(last)
    def _():
        before = jnp.concatenate([jnp.zeros_like(outer), outer], axis=0).astype(BF16)
        g_wi[:model] += dot(halo_low[...], before, 0, 0)
        before_p = jnp.concatenate([jnp.zeros_like(outer_p), outer_p], axis=0)
        high_p, rest_p = halves(before_p)
        g_wp[...] += dot(halo_low[...], high_p, 0, 0) + dot(halo_low[...], rest_p, 0, 0)
        edge_part = dot(before, wi_t[...]) + (dot(high_p, wp_t[...]) + dot(rest_p, wp_t[...]))
        edge[0] = edge_part[8:]
        edge_copy(0, edge_core, beside).start()
        pack[:6] = small[:6]
        pack[6:7] = g_gain[...]
        step_rows = jnp.transpose(g_ws[...])[:8]
        pack[8:16] = step_rows[:, :width]
        pack[16:24] = step_rows[:, width:]
        pack[24:32, : heads.shape[1]] = heads[...]
        pair_small[:8] = small_p[...]
        if summing:
            for h_sum, _, _ in wide:
                h_sum.fold_core().start()
            s_wi[0].begin()
            s_wi[1].begin()

        @pl.when(core == 0)
        def _():
            settle(0)

        if summing:
            for h_sum, _, _ in wide:
                h_sum.fold()
            s_wi[2].begin()
            s_pack.begin()
        edge_copy(0, edge_core, beside).wait_recv()
        edge[1] = edge[0] + edge_core[...]
        edge_copy(1, edge_plane, across).start()
        if summing:
            s_wg.collect()
            s_wi[0].pass_on()
            s_wi[1].pass_on()
        edge_copy(1, edge_plane, across).wait_recv()
        edge[2] = edge[1] + edge_plane[...]
        edge_copy(2, edge_ahead, {"seq": behind}).start()
        for h_sum, s_sum, _ in wide:
            h_sum.settle()
            s_sum.begin()
        norm_back(2)
        norm_back(1)
        if summing:
            s_wi[2].pass_on()
            s_pack.pass_on()
            s_wi[0].finish()
        for _, s_sum, _ in wide:
            s_sum.pass_on()
        norm_back(0)
        norm_back(3)
        loop(1, group, lambda d: hand(d).start())
        if summing:
            s_wi[1].finish()
            s_wi[2].finish()
            s_pack.finish()
            for _, s_sum, _ in wide:
                s_sum.finish()
            s_wi[0].collect()
            s_wo.store(out_wo)
            s_wi[1].collect()
            s_wi[2].collect()
            for _, s_sum, _ in wide:
                s_sum.collect()
            s_pack.collect()
            s_wg.store(out_wg)
            for h_sum, s_sum, total in wide:
                s_sum.store(total)
                h_sum.spread(total)
            for s_sum, out in zip(s_wi, outs_wi):
                s_sum.store(out)
            for h_sum, _, _ in wide:
                h_sum.spread_more()
            s_pack.store(sum_pack)
            for h_sum, _, _ in wide:
                h_sum.finish()
            out_wp[...] = spread_wp[...]
            totals, pair_totals = sum_pack[:32], spread_small[:8]
            for s_sum in seq_sums:
                s_sum.drain()
        else:
            for out, ref in ((out_wo, g_wo), (out_wg, g_wg), (out_wi, g_wi), (out_wp, g_wp)):
                out[...] = ref[...]
            totals, pair_totals = pack[:32], pair_small[:8]
        heads_here = out_sbias.shape[1]
        out_conv_i[...] = totals[:4]
        out_bias_i[...] = totals[4:5]
        out_skip[...] = head_sums(totals[:8])[5:6, :heads_here]
        out_gain[...] = totals[6:7]
        out_ws[...] = jnp.transpose(jnp.concatenate([totals[8:16], totals[16:24]], axis=1))[:, :heads_here]
        out_sbias[...] = totals[24:25, :heads_here]
        out_dlog[...] = totals[25:26, :heads_here]
        out_conv_p[...] = pair_totals[:4]
        out_bias_p[...] = pair_totals[4:5]
        row_land[me] = row[...]
        loop(1, group, lambda d: hand(d).wait())
        both_rows = lax.fori_loop(1, group, lambda d, total: total + row_land[d], row_land[0])
        out_norm[...] = both_rows[:1]
        per_token = factor[0] / (group * half * BLOCK * model)
        out_loss[...] = jnp.sum(both_rows[1:], axis=1, keepdims=True) * per_token
        for at, to in enumerate((beside, across, {"seq": behind})):
            edge_copy(at, edge_core, to).wait_send()

        @pl.when(core == 1)
        def _():
            loop(0, half, lambda at: core_copy(at).wait_send())

        def drain(at):
            x_copy(at).wait_send()
            grad_copy(at).wait()
            rows_at(grad_all, (1 - core) * half + at, BLOCK)[...] = grad_other[at]

        loop(0, half, drain)


def call(kernel, grid, ins, outs, scratch=(), prefetch=0, flops=0, moved=0, collective=None, vmem=14):
    def spec(shape, block, index):
        if block is None:
            return pl.BlockSpec(shape, lambda *_: (0,) * len(shape))
        if isinstance(block, str):
            return pl.BlockSpec(memory_space={"smem": pltpu.SMEM, "vmem": pltpu.VMEM, "any": pl.ANY}[block])
        return pl.BlockSpec(block, index)

    scalars = [a for a, *_ in ins[:prefetch]]
    arrays = ins[prefetch:]
    extra = {} if collective is None else {"collective_id": collective, "has_side_effects": True}
    return pl.pallas_call(
        kernel,
        grid_spec=pltpu.PrefetchScalarGridSpec(
            num_scalar_prefetch=prefetch,
            grid=(grid,),
            in_specs=[spec(a.shape, block, index) for a, block, index in arrays],
            out_specs=[spec(shape, block, index) for shape, _, block, index in outs],
            scratch_shapes=list(scratch),
        ),
        out_shape=[jax.ShapeDtypeStruct(shape, dtype) for shape, dtype, _, _ in outs],
        compiler_params=pltpu.CompilerParams(
            dimension_semantics=("arbitrary",), vmem_limit_bytes=vmem << 20, **extra
        ),
        cost_estimate=pl.CostEstimate(flops=int(flops), bytes_accessed=int(moved), transcendentals=0),
    )(*scalars, *[a for a, *_ in arrays])


def swap(value, axis, bit):
    route = [(i, i ^ bit) for i in range(lax.axis_size(axis))]
    return jax.tree.map(lambda v: lax.ppermute(v, axis, route), value)


def shifted(value, axis, distance):
    devices = range(lax.axis_size(axis))
    route = [(i - distance, i) for i in devices if i - distance in devices]
    return lax.ppermute(value, axis, route)


def bits(axis):
    size = lax.axis_size(axis)
    return [1 << b for b in range(size.bit_length() - 1)]


def total_over(value, axis):
    for bit in bits(axis):
        value = value + swap(value, axis, bit)
    return value


def carried(total, axis, backward):
    mine = lax.axis_index(axis)
    decays = slice(CHUNK, total.shape[0] - 1)

    def join(early, late):
        decay = late[CHUNK : CHUNK + 1]
        return jnp.concatenate([
            late[:CHUNK] + decay * early[:CHUNK], late[decays] * early[decays], late[-1:] + early[-1:],
        ])

    reached = jnp.concatenate([jnp.zeros_like(total[:CHUNK]), jnp.ones_like(total[CHUNK:])])
    for bit in bits(axis):
        other = swap(total, axis, bit)
        later = ((mine & bit) == 0) if backward else ((mine & bit) != 0)
        reached = jnp.where(later, join(other, reached), reached)
        total = jnp.where(later, join(other, total), join(total, other))
    return reached[:CHUNK], total[-1, 0]


def shards(
    hidden, teacher, doc_starts, valid_mask, norm_gain, w_gate, w_inner, w_pair, w_step, conv_inner, bias_inner,
    conv_pair, bias_pair, step_bias, decay_log, skip_gain, gate_gain, w_output,
):
    rows, model = hidden.shape
    width = w_inner.shape[1]
    pair_width = w_pair.shape[1]
    heads = step_bias.shape[0]
    blocks, chunks = rows // BLOCK, rows // CHUNK
    per = BLOCK // CHUNK
    half = blocks // 2
    inner_total = float(width * lax.axis_size("head"))
    core = lax.axis_index("head") & 1
    offset = lax.axis_index("seq") * rows
    idx = jnp.stack([core, offset]).astype(jnp.int32)
    edge_rows = 16

    given = jnp.stack([
        jnp.pad(step_bias, (0, LANES - heads)), jnp.pad(decay_log, (0, LANES - heads)), jnp.pad(skip_gain, (0, LANES - heads)),
        jnp.pad(doc_starts.astype(F32), (0, LANES - doc_starts.shape[0]), constant_values=FAR),
        *[jnp.zeros((LANES,), F32)] * 4,
    ])
    ws = jnp.pad(w_step, ((0, 0), (0, LANES - heads)))
    gain, out_gain = norm_gain[None, :], gate_gain[None, :]
    bias_i, bias_p = bias_inner[None, :], bias_pair[None, :]
    valid = valid_mask[None, :]

    tail = shifted(hidden[rows - edge_rows :], "seq", 1)

    def by(w, column=0):
        return (BLOCK, w), lambda i, *_: (i, column)

    def back(w, column=0):
        return (BLOCK, w), lambda i, *_: (blocks - 1 - i, column)

    grid3 = lambda n: ((per, n, width), lambda i, *_: (i, 0, 0))
    back3 = lambda n: ((per, n, width), lambda i, *_: (blocks - 1 - i, 0, 0))
    whole = (None, None)

    dma = pltpu.SemaphoreType.DMA

    halo_block = ((edge_rows, model), lambda i, *_: (jnp.maximum(i * (BLOCK // edge_rows) - 1, 0), 0))
    (low, low_t, in_i, in_p, pre_i, pre_p, aux, halo_low, halo_i, halo_p, sloc, pkl, fin) = call(
        project_kernel,
        blocks,
        [
            (idx, None, None), (given, *whole), (valid, (1, BLOCK), lambda i, *_: (0, i)), (hidden, *by(model)), (hidden, *halo_block), (tail, *whole),
            (gain, *whole), (w_inner, *whole), (w_pair, *whole), (ws, *whole), (conv_inner, *whole), (conv_pair, *whole),
            (bias_i, *whole), (bias_p, *whole),
        ],
        [
            ((rows, model), BF16, *by(model)), ((model, rows), BF16, (model, BLOCK), lambda i, *_: (0, i)),
            ((rows, width), BF16, *by(width)), ((rows, pair_width), BF16, *by(pair_width)),
            ((rows, width), F32, *by(width)), ((rows, pair_width), F32, *by(pair_width)), ((rows, LANES), F32, *by(LANES)),
            ((edge_rows, model), BF16, *whole), ((edge_rows, width), BF16, *whole), ((edge_rows, pair_width), BF16, *whole),
            ((chunks, CHUNK, width), F32, *grid3(CHUNK)), ((chunks, 8, width), F32, *grid3(8)),
            ((CHUNK + 8, width), F32, *whole),
        ],
        [
            pltpu.VMEM((BLOCK + edge_rows, width), F32), pltpu.VMEM((BLOCK + edge_rows, pair_width), F32),
            pltpu.VMEM((CHUNK, width), F32), pltpu.VMEM((8, width), F32), pltpu.VMEM((1, 1), F32),
        ],
        prefetch=1, flops=3e9, moved=2e7,
    )
    state_in, count = carried(fin, "seq", False)
    factor = (rows * lax.axis_size("seq")) / count
    gate, local = call(
        intra_kernel,
        blocks,
        [
            (idx, None, None), (low, *by(model)), (w_gate, *whole), (pre_i, *by(width)), (pre_p, *by(pair_width)),
            (aux, *by(LANES)), (given, *whole),
        ],
        [((rows, width), F32, *by(width)), ((rows, width), F32, *by(width))],
        prefetch=1, flops=4e9, moved=2e7,
    )
    size = lax.axis_size("seq")
    vmem = ("vmem", None)
    once = lambda w: ((rows // 2, w), lambda i: (core_bit(), 0))
    first_or_last = lambda i: jnp.where(i < blocks, i, jnp.clip(i - 2 * blocks - 1, 0, blocks - 1))
    early = lambda i: jnp.minimum(i, blocks - 1)
    late = lambda i: jnp.clip(i - 2 * blocks - 1, 0, blocks - 1)
    own_slot = lambda i: jnp.clip(i - 2 * blocks - half * core_bit(), 0, half - 1)
    early3 = lambda n: ((per, n, width), lambda i: (early(i), 0, 0))
    states, d_mixer, d_gate, gloc, pkb, fin_back, output, d_out, error, g_gain, g_wo, mixer = call(
        partial(mid_kernel, total=inner_total),
        3 * blocks + 1,
        [
            (factor.reshape(1), "smem", None), (pre_p, (BLOCK, LANES), lambda i: (first_or_last(i), 1)),
            (aux, (BLOCK, LANES), lambda i: (first_or_last(i), 0)), (sloc, *early3(CHUNK)), (pkl, *early3(8)), (state_in, *whole),
            (local, (BLOCK, width), lambda i: (early(i), 0)), (gate, *vmem), (out_gain, *whole), (w_output, *whole),
            (hidden, *once(model)), (teacher, *once(model)),
            (valid, (1, BLOCK), lambda i: (0, own_slot(i) + half * core_bit())),
        ],
        [
            ((chunks, CHUNK, width), F32, *early3(CHUNK)), ((rows, width), F32, (BLOCK, width), lambda i: (late(i), 0)),
            ((rows, width), BF16, (BLOCK, width), lambda i: (late(i), 0)), ((chunks, CHUNK, width), F32, *vmem),
            ((chunks, 8, width), F32, *vmem), ((CHUNK + 8, width), F32, *vmem), ((rows, model), BF16, "any", None),
            ((rows // 2, model), F32, (BLOCK, model), lambda i: (own_slot(i), 0)), ((1, model), F32, *whole),
            ((1, width), F32, *whole), ((width, model), F32, *whole), ((blocks, BLOCK, width), F32, *vmem),
        ],
        [
            pltpu.VMEM((blocks, 1, BLOCK), F32), pltpu.VMEM((4, blocks, 1, BLOCK), F32),
            pltpu.VMEM((blocks, 1, BLOCK), F32), pltpu.VMEM((4, blocks, 1, BLOCK), F32), pltpu.VMEM((blocks, 1, BLOCK), F32),
            pltpu.VMEM((half, BLOCK, model), F32), pltpu.VMEM((half, BLOCK, model), F32),
            pltpu.VMEM((half, BLOCK, model), BF16), pltpu.VMEM((half, BLOCK, model), BF16),
            pltpu.VMEM((blocks, BLOCK, model), BF16), pltpu.VMEM((half, BLOCK, model), BF16),
            pltpu.VMEM((2, BLOCK, width), F32), pltpu.VMEM((chunks, 8, width), F32), pltpu.VMEM((CHUNK, width), F32),
            pltpu.VMEM((model, width), BF16), dma((4 * blocks,)), dma((4 * blocks,)), dma((4 * blocks,)), dma((4 * blocks,)), dma((half,)), dma((half,)),
            dma((half,)), dma((half,)), dma((blocks,)), dma((blocks,)), dma((half,)), dma((half,)), dma((half,)),
        ],
        flops=6e9, moved=6e7, collective=2, vmem=44,
    )
    mixer = mixer.reshape(rows, width)
    grad_in, _ = carried(fin_back, "seq", True)
    d_scaled, d_maps, g_wg = call(
        intra_back_kernel,
        blocks,
        [
            (idx, None, None), (d_mixer, *by(width)), (pre_i, *by(width)), (pre_p, *by(pair_width)), (aux, *by(LANES)),
            (low_t, (model, BLOCK), lambda i, *_: (0, i)), (d_gate, *by(width)),
        ],
        [((rows, width), F32, *by(width)), ((rows, pair_width), F32, *by(pair_width)), ((model, width), F32, *whole)],
        prefetch=1, flops=6e9, moved=2e7,
    )
    summing = size <= 8

    def piece(total_rows, tile):
        return -(-total_rows // (size * tile)) * tile

    r_wo, r_w, r_pack, r_wp, r_small = piece(width, 16), piece(model, 16), 8, piece(model // 4, 8), 8
    core_wire = F32 if summing else BF16
    sum_shapes = [(r_wo, model, BF16), (r_w, width, BF16), *[(piece(model // 3, 16), width, BF16)] * 3, (r_pack, width, F32), (r_wp, pair_width, F32),
                  (r_small, pair_width, F32)]
    n_wo, n_w, n_pack = (r_wo * size, r_w * size, r_pack * size) if summing else (width, model, 64)
    scratch = [pltpu.VMEM((BLOCK + 16, width), F32)] * 3 + [pltpu.VMEM((BLOCK + 16, pair_width), F32)] * 3 + [
        pltpu.VMEM((8, width), F32), pltpu.VMEM((8, pair_width), F32), pltpu.VMEM((8, LANES), F32),
        pltpu.VMEM((half, BLOCK, model), core_wire), pltpu.VMEM((half, BLOCK, model), core_wire),
        pltpu.VMEM((half, BLOCK, model), BF16), pltpu.VMEM((half, BLOCK, model), BF16),
        pltpu.VMEM((2, model), F32), pltpu.VMEM((2 * size, 2, model), F32),
        pltpu.VMEM((n_w, width), F32), pltpu.VMEM((model, LANES), F32), pltpu.VMEM((n_pack, width), F32),
        pltpu.VMEM((model, pair_width), F32), pltpu.VMEM((32, pair_width), F32),
        pltpu.VMEM((r_small * size, pair_width), F32), pltpu.VMEM((r_wp * size, pair_width), F32),
        pltpu.VMEM((n_pack, width), F32), pltpu.VMEM((model, pair_width), F32), pltpu.VMEM((32, pair_width), F32),
        pltpu.VMEM((half, BLOCK, model), BF16), pltpu.VMEM((half, BLOCK, model), BF16),
        pltpu.VMEM((width, model), BF16), pltpu.VMEM((width, model), BF16), pltpu.VMEM((LANES, model), BF16),
        pltpu.VMEM((pair_width, model), BF16),
        pltpu.VMEM((3, 8, model), F32), pltpu.VMEM((8, model), F32), pltpu.VMEM((8, model), F32), pltpu.VMEM((8, model), F32),
        dma((half,)), dma((half,)), dma((half,)), dma((half,)), dma((3,)), dma((3,)), dma((half,)), dma((half,)),
        dma((2 * size,)), dma((2 * size,)),
    ]
    if summing:
        scratch += HeadSum.scratch(model, pair_width, r_wp * size) + HeadSum.scratch(32, pair_width, r_small * size)
        for r, lanes, wire in sum_shapes:
            scratch += SeqSum.scratch(r, lanes, wire, size)
    grad_hidden, g_norm, loss, *grads, g_wp, g_ws, g_ci, g_bi, g_cp, g_bp, g_sb, g_dl, g_skip, g_gain = call(
        finale_kernel,
        blocks,
        [
            (d_scaled, *back(width)), (d_maps, *back(pair_width)), (pre_i, *back(width)), (pre_p, *back(pair_width)),
            (in_i, *back(width)), (in_p, *back(pair_width)), (halo_low, *whole), (halo_i, *whole), (halo_p, *whole),
            (aux, *back(LANES)), (gloc, *back3(CHUNK)), (pkb, *back3(8)), (grad_in, *whole), (states, *back3(CHUNK)),
            (d_mixer, *back(width)), (mixer, *back(width)), (given, *whole), (conv_inner, *whole), (conv_pair, *whole),
            (low_t, (model, BLOCK), lambda i, *_: (0, blocks - 1 - i)), (d_gate, *back(width)), (w_gate, *whole), (w_inner, *whole), (ws, *whole), (w_pair, *whole),
            (hidden, *once(model)), (d_out, *vmem), (gain, *whole), (error, *whole), (g_wo, *vmem), (g_wg, *vmem),
            (g_gain, *whole), (factor.reshape(1), "smem", None),
        ],
        [
            ((rows, model), BF16, *vmem), ((1, model), F32, *vmem), ((1, 1), F32, *vmem), ((n_wo, model), F32, *vmem),
            ((n_w, width), F32, *vmem), ((n_w, width), F32, *vmem), ((model, pair_width), F32, *vmem),
            ((model, heads), F32, *vmem), ((4, width), F32, *vmem), ((1, width), F32, *vmem), ((4, pair_width), F32, *vmem),
            ((1, pair_width), F32, *vmem), ((1, heads), F32, *vmem), ((1, heads), F32, *vmem), ((1, heads), F32, *vmem),
            ((1, width), F32, *vmem),
        ],
        scratch,
        flops=9e9, moved=8e7, collective=4, vmem=58,
    )
    if not summing:
        *grads, g_ws, g_ci, g_bi, g_sb, g_dl, g_skip, g_gain = lax.psum(
            (*grads, g_ws, g_ci, g_bi, g_sb, g_dl, g_skip, g_gain), "seq"
        )
        g_wp, g_cp, g_bp = lax.psum((g_wp, g_cp, g_bp), ("seq", "head"))
    g_wo, g_wg, g_wi = grads
    return (
        output, loss.reshape(()), grad_hidden, g_norm.reshape(-1), g_wg, g_wi, g_wp, g_ws, g_ci, g_bi.reshape(-1), g_cp,
        g_bp.reshape(-1), g_sb.reshape(-1), g_dl.reshape(-1), g_skip.reshape(-1), g_gain.reshape(-1), g_wo,
    )


def solution(mesh):
    seq, head, wide = P("seq", None), P("head"), P(None, "head")
    in_specs = (
        seq, seq, P(), P("seq"), P(), wide, wide, P(), wide, wide, head, P(), P(), head, head, head, head, P("head", None),
    )
    out_specs = (
        seq, P(), seq, P(), wide, wide, P(), wide, wide, head, P(), P(), head, head, head, head, P("head", None),
    )
    return jax.shard_map(shards, mesh=mesh, in_specs=in_specs, out_specs=out_specs, check_vma=False)
```

```python
from functools import partial

import jax
import jax.numpy as jnp
from jax import lax
from jax.experimental import pallas as pl
from jax.experimental.pallas import tpu as pltpu
from jax.sharding import PartitionSpec as P

EPSILON = 1e-05
CHUNK = 128
BLOCK = 256
HEAD_DIM = 64
LANES = 128
FAR = float(1 << 24)
F32 = jnp.float32
BF16 = jnp.bfloat16

DT, CUM, INFLOW, TAIL, RATE, START, END = 0, 8, 16, 24, 32, 40, 41


def dot(a, b, da=1, db=0):
    return lax.dot_general(a, b, (((da,), (db,)), ((), ())), preferred_element_type=F32)


def halves(v):
    high = v.astype(BF16)
    return high, (v - high.astype(F32)).astype(BF16)


def dot3(a, b, da=1, db=0):
    ah, al = halves(a)
    bh, bl = halves(b)
    return dot(ah, bh, da, db) + (dot(ah, bl, da, db) + dot(al, bh, da, db))


def column_sums(v):
    folded = v[:, :LANES]
    for at in range(LANES, v.shape[1], LANES):
        folded = folded + v[:, at : at + LANES]
    return jnp.sum(jnp.transpose(folded), axis=0, keepdims=True)


def as_column(row, width=LANES):
    column = jnp.transpose(jnp.broadcast_to(row, (LANES, row.shape[1])))
    return jnp.concatenate([column] * (width // LANES), axis=1)


def expand(table, base, width):
    rows = table.shape[0]
    lane = lax.broadcasted_iota(jnp.int32, (rows, LANES), 1)
    parts = []
    for pair in range(width // LANES):
        first = jnp.broadcast_to(table[:, base + 2 * pair : base + 2 * pair + 1], (rows, LANES))
        second = jnp.broadcast_to(table[:, base + 2 * pair + 1 : base + 2 * pair + 2], (rows, LANES))
        parts.append(jnp.where(lane < HEAD_DIM, first, second))
    return jnp.concatenate(parts, axis=1)


def triangle_sums(ones, v):
    high, rest = halves(v)
    low = (v - high.astype(F32) - rest.astype(F32)).astype(BF16)
    sums = dot(ones, jnp.concatenate([high, rest, low], axis=1))
    return sums[:, :LANES] + (sums[:, LANES : 2 * LANES] + sums[:, 2 * LANES :])


def head_matrix(width):
    channel = lax.broadcasted_iota(jnp.int32, (width, LANES), 0)
    head = lax.broadcasted_iota(jnp.int32, (width, LANES), 1)
    return ((channel >> 6) == head).astype(BF16)


def head_sums(v):
    high, low = halves(v)
    matrix = head_matrix(v.shape[1])
    return dot(high, matrix) + dot(low, matrix)


def triangle(upper):
    row = lax.broadcasted_iota(jnp.int32, (CHUNK, CHUNK), 0)
    col = lax.broadcasted_iota(jnp.int32, (CHUNK, CHUNK), 1)
    return ((col >= row) if upper else (col <= row)).astype(BF16)


def silu_parts(pre):
    gate = jax.nn.sigmoid(pre)
    return pre * gate, gate * (1.0 + pre * (1.0 - gate))


def project_kernel(
    idx, given, valid, hid, halo, tail, gain, wi, wp, ws, conv_i, conv_p, bias_i, bias_p,
    low, low_t, in_i, in_p, pre_i, pre_p, aux, halo_low, halo_i, halo_p, sloc, pkl, fin, wide_i, wide_p, state, decay, counted,
):
    step = pl.program_id(0)
    edge = tail.shape[0]
    width = wi.shape[1]

    @pl.when(step == 0)
    def _():
        state[...] = jnp.zeros_like(state)
        decay[...] = jnp.ones_like(decay)
        counted[...] = jnp.zeros_like(counted)

    counted[...] += jnp.sum(valid[...].astype(F32), axis=1, keepdims=True)
    before = jnp.where(step == 0, tail[...].astype(F32), halo[...].astype(F32))
    rows = jnp.concatenate([before, hid[...].astype(F32)], axis=0)
    scale = lax.rsqrt(jnp.mean(rows * rows, axis=1, keepdims=True) + EPSILON)
    lowered = (rows * scale * gain[...]).astype(BF16)
    own = lowered[edge:]
    low[...] = own
    low_t[...] = jnp.transpose(own)
    inner = dot(lowered, wi[...]).astype(BF16)
    pair = dot(lowered, wp[...]).astype(BF16)
    in_i[...] = inner[edge:]
    in_p[...] = pair[edge:]
    wide_i[...] = inner.astype(F32)
    wide_p[...] = pair.astype(F32)

    @pl.when(step == 0)
    def _():
        halo_low[...] = lowered[:edge]
        halo_i[...] = inner[:edge]
        halo_p[...] = pair[:edge]

    base = idx[1] + step * BLOCK
    pos = (base + lax.broadcasted_iota(jnp.int32, (BLOCK, LANES), 0)).astype(F32)
    starts = given[3:4]
    begun = starts <= pos
    start = jnp.max(jnp.where(begun, starts, -1.0), axis=1, keepdims=True)
    end = jnp.min(jnp.where(begun, FAR, starts), axis=1, keepdims=True)
    within = pos[:, :1] - start
    keep = [(within >= float(3 - k)).astype(F32) for k in range(3)]

    def convolve(wide, weight, bias):
        taps = weight[...].astype(F32)
        total = bias[...].astype(F32) + wide[edge : edge + BLOCK] * taps[3:4]
        for k in range(3):
            total = total + wide[edge - 3 + k : edge - 3 + k + BLOCK] * taps[k : k + 1] * keep[k]
        return total

    conv_inner = convolve(wide_i, conv_i, bias_i)
    conv_pair = convolve(wide_p, conv_p, bias_p)
    pre_i[...] = conv_inner
    pre_p[...] = conv_pair
    values = conv_inner * jax.nn.sigmoid(conv_inner)
    maps = conv_pair[:, :LANES]
    maps = maps * jax.nn.sigmoid(maps)

    raw = dot(own, ws[...]) + given[0:1]
    dt = jnp.maximum(raw, 0.0) + jnp.log1p(jnp.exp(-jnp.abs(raw)))
    rate = jax.nn.sigmoid(raw)
    logs = -dt * jnp.exp(given[1:2])
    lane = lax.broadcasted_iota(jnp.int32, (CHUNK, LANES), 1)
    lower = triangle(False)
    for c in range(BLOCK // CHUNK):
        at = slice(c * CHUNK, (c + 1) * CHUNK)
        cum = triangle_sums(lower, logs[at])
        last = cum[CHUNK - 1 :]
        first = (base + c * CHUNK).astype(F32)
        inflow = jnp.exp(cum) * (start[at] <= first - 1.0).astype(F32)
        outflow = jnp.exp(last - cum) * (end[at] > first + (CHUNK - 1.0)).astype(F32)
        table = jnp.where(lane < CUM, dt[at], pltpu.roll(cum, CUM, 1))
        table = jnp.where(lane < INFLOW, table, pltpu.roll(inflow, INFLOW, 1))
        table = jnp.where(lane < TAIL, table, pltpu.roll(outflow, TAIL, 1))
        table = jnp.where(lane < RATE, table, pltpu.roll(rate[at], RATE, 1))
        table = jnp.where(lane < START, table, jnp.where(lane < END, start[at], end[at]))
        aux[at, :] = table
        scaled = values[at] * expand(dt[at] * outflow, 0, width)
        added = dot3(maps[at], scaled, 0, 0)
        kept = expand(jnp.broadcast_to(inflow[CHUNK - 1 :], (8, LANES)), 0, width)
        sloc[c] = state[...]
        pkl[c] = decay[...]
        state[...] = state[...] * kept[:1] + added
        decay[...] = decay[...] * kept
    fin[:CHUNK] = state[...]
    fin[CHUNK:] = jnp.concatenate([decay[:7], jnp.broadcast_to(counted[...], (1, width))], axis=0)


def masks(table, first, transposed):
    row = lax.broadcasted_iota(jnp.int32, (CHUNK, CHUNK), 0)
    col = lax.broadcasted_iota(jnp.int32, (CHUNK, CHUNK), 1)
    at = (first + col).astype(F32)
    if transposed:
        return (col >= row) & (at < table[:, END : END + 1])
    return (col <= row) & (at >= table[:, START : START + 1])


def head_split(v, pair):
    lane = lax.broadcasted_iota(jnp.int32, (v.shape[0], LANES), 1)
    part = v[:, pair * LANES : (pair + 1) * LANES]
    return jnp.concatenate(
        [jnp.where(lane < HEAD_DIM, part, 0.0), jnp.where(lane < HEAD_DIM, 0.0, part)], axis=0
    ).astype(BF16)


def intra_kernel(idx, low, wg, pre_i, pre_p, aux, given, gate, mixed):
    width = wg.shape[1]
    skip = expand(given[...], 0, width)[2:3]
    gate[...] = dot(low[...], wg[...])
    base = idx[1] + pl.program_id(0) * BLOCK
    maps, _ = silu_parts(pre_p[...])
    values, _ = silu_parts(pre_i[...])
    for c in range(BLOCK // CHUNK):
        at = slice(c * CHUNK, (c + 1) * CHUNK)
        table = aux[at, :]
        rows = jnp.transpose(table)
        joined = masks(table, base + c * CHUNK, False)
        scores = dot(maps[at, LANES:].astype(BF16), maps[at, :LANES].astype(BF16), 1, 1)
        scaled = values[at] * expand(table, DT, width)
        parts = []
        for pair in range(width // LANES):
            weights = []
            for h in (2 * pair, 2 * pair + 1):
                gap = table[:, CUM + h : CUM + h + 1] - rows[CUM + h : CUM + h + 1, :]
                weights.append((scores * jnp.exp(jnp.where(joined, gap, -1e30))).astype(BF16))
            parts.append(dot(jnp.concatenate(weights, axis=1), head_split(scaled, pair)))
        mixed[at, :] = jnp.concatenate(parts, axis=1) + values[at] * skip


def core_bit():
    return lax.rem(lax.axis_index("head"), 2)


def core_peer():
    return lax.axis_index("head") + 1 - 2 * core_bit()


def mid_kernel(
    factor, pre_c, aux, sloc, pkl, sin, local, gate, gain, wo, hid, teacher, valid,
    states, d_mixer, d_gate, gloc, pkb, fin, out, d_out, error, g_gain, g_wo,
    mix, squares, square_land, crosses, cross_land, scales, parts, land, mine, other, d_branch, out_block, weighted, keeps,
    state, wo_t, square_send, square_got, cross_send, cross_got, core_send, core_land, x_send, x_land, grad_send, grad_land,
    out_local, out_send, out_land, *, total,
):
    step = pl.program_id(0)
    half = mine.shape[0]
    blocks = 2 * half
    width = local.shape[1]
    head, core = lax.axis_index("head"), core_bit()
    beside, across = {"head": core_peer()}, {"head": lax.rem(head + 2, 4)}

    def to_head(distance):
        return {"head": lax.rem(head + distance, 4)}

    def square_copy(block, d):
        return device_copy(squares.at[block], square_land.at[d, block], (square_send, square_got), 4 * block + d, to_head(d))

    def cross_copy(block, d):
        return device_copy(crosses.at[block], cross_land.at[d, block], (cross_send, cross_got), 4 * block + d, to_head(d))

    def core_copy(slot):
        return device_copy(parts.at[slot], land.at[slot], (core_send, core_land), slot, beside)

    def x_copy(slot):
        return device_copy(mine.at[slot], other.at[slot], (x_send, x_land), slot, across)

    def grad_copy(block):
        return device_copy(d_branch.at[block], d_branch.at[block], (grad_send, grad_land), block, beside)

    def out_copies(slot):
        rows = rows_at(out, core * half + slot, BLOCK)
        here = pltpu.make_async_copy(out_block.at[slot], rows, out_local.at[slot])
        return here, device_copy(out_block.at[slot], rows, (out_send, out_land), slot, beside)

    def gate_rows(block):
        return gate[pl.ds(pl.multiple_of(block * BLOCK, BLOCK), BLOCK), :]

    def settle(slot):
        core_copy(slot).wait_recv()
        mine[slot] = (parts[slot] + land[slot]).astype(BF16)
        x_copy(slot).start()

    @pl.when(step == 0)
    def _():
        barrier = pltpu.get_barrier_semaphore()

        def greet(d):
            pl.semaphore_signal(barrier, inc=1, device_id=to_head(d), device_id_type=pl.DeviceIdType.MESH)

        loop(1, 4, greet)
        for ref in (error, g_gain, g_wo):
            ref[...] = jnp.zeros_like(ref)
        wo_t[...] = jnp.transpose(wo[...])
        pl.semaphore_wait(barrier, 3)

    @pl.when(step < blocks)
    def _():
        reads, _ = silu_parts(pre_c[...])
        for c in range(BLOCK // CHUNK):
            at = slice(c * CHUNK, (c + 1) * CHUNK)
            now = sloc[c] + pkl[c, :1] * sin[...]
            states[c] = now
            mix[step, at, :] = local[at, :] + expand(aux[at, :], INFLOW, width) * dot3(reads[at], now)
        act, _ = silu_parts(gate_rows(step))
        gated = mix[step] * act
        squares[step] = column_sums(gated * gated)
        loop(1, 4, lambda d: square_copy(step, d).start())

    @pl.when((step > blocks) & (step <= 2 * blocks) & ((step - blocks - 1) // half == core))
    def _():
        settle(lax.rem(step - blocks - 1, half))

    @pl.when((step >= blocks) & (step < 2 * blocks))
    def _():
        block = step - blocks
        slot = lax.rem(block, half)
        own = block // half == core

        def add(d, sum_row):
            square_copy(block, d).wait_recv()
            return sum_row + square_land[d, block]

        row = lax.rsqrt(lax.fori_loop(1, 4, add, squares[block]) / total + EPSILON)
        scales[block] = row
        act, _ = silu_parts(gate_rows(block))
        normed = (mix[block] * act * as_column(row, width) * gain[...]).astype(BF16)

        @pl.when(own & (core == 1))
        def _():
            core_copy(slot).wait_send()

        parts[slot] = dot(normed, wo[...])

        @pl.when(jnp.logical_not(own))
        def _():
            core_copy(slot).start()

    @pl.when((step >= 2 * blocks) & (step < 3 * blocks))
    def _():
        block = step - 2 * blocks
        slot = lax.rem(block, half)
        own = block // half == core

        @pl.when(own)
        def _():
            x_copy(slot).wait_recv()
            at = pl.ds(pl.multiple_of(slot * BLOCK, BLOCK), BLOCK)
            outf = hid[at, :].astype(F32) + (mine[slot].astype(F32) + other[slot].astype(F32))
            term = outf - teacher[at, :].astype(F32)
            masked = as_column(valid[...].astype(F32), term.shape[1]) * term
            error[...] += jnp.sum(masked * term, axis=0, keepdims=True)
            grad = masked * factor[0]
            d_out[...] = grad
            d_branch[block] = grad.astype(BF16)
            grad_copy(block).start()
            out_block[slot] = outf.astype(BF16)
            for copy in out_copies(slot):
                copy.start()

        @pl.when(jnp.logical_not(own))
        def _():
            grad_copy(block).wait_recv()

        act, _ = silu_parts(gate_rows(block))
        gated = mix[block] * act
        scaled = gated * as_column(scales[block], width)
        normed = (scaled * gain[...]).astype(BF16)
        grads = d_branch[block]
        g_wo[...] += dot(normed, grads, 0, 0)
        d_normed = dot(grads, wo_t[...])
        g_gain[...] += jnp.sum(d_normed * scaled, axis=0, keepdims=True)
        pulled = d_normed * gain[...]
        weighted[lax.rem(block, 2)] = pulled
        crosses[block] = column_sums(pulled * gated)
        loop(1, 4, lambda d: cross_copy(block, d).start())

    @pl.when(step > 2 * blocks)
    def _():
        block = step - 2 * blocks - 1

        def add(d, sum_row):
            cross_copy(block, d).wait_recv()
            return sum_row + cross_land[d, block]

        cross = lax.fori_loop(1, 4, add, crosses[block])
        act, slope = silu_parts(gate_rows(block))
        gated = mix[block] * act
        row = scales[block]
        pull = as_column(row * row * row * cross / total, width)
        d_gated = as_column(row, width) * weighted[lax.rem(block, 2)] - gated * pull
        dy = d_gated * act
        d_mixer[...] = dy
        d_gate[...] = (d_gated * mix[block] * slope).astype(BF16)
        reads, _ = silu_parts(pre_c[...])
        for c in range(BLOCK // CHUNK):
            at = slice(c * CHUNK, (c + 1) * CHUNK)
            inflow = expand(aux[at, :], INFLOW, width)
            keeps[block * (BLOCK // CHUNK) + c] = jnp.broadcast_to(inflow[CHUNK - 1 :], (8, width))
            gloc[block * (BLOCK // CHUNK) + c] = dot3(reads[at], dy[at] * inflow, 0, 0)

    @pl.when(step == 3 * blocks)
    def _():
        state[...] = jnp.zeros_like(state)
        chunks = gloc.shape[0]

        def back(i, decay):
            c = chunks - 1 - i
            added = gloc[c]
            gloc[c] = state[...]
            pkb[c] = decay
            state[...] = state[...] * keeps[c, :1] + added
            return decay * keeps[c]

        decay = lax.fori_loop(0, chunks, back, jnp.ones((8, width), F32))
        fin[:CHUNK] = state[...]
        fin[CHUNK:] = decay

        def drain(block):
            def both(d):
                square_copy(block, d).wait_send()
                cross_copy(block, d).wait_send()

            loop(1, 4, both)

            @pl.when(block // half == core)
            def _():
                grad_copy(block).wait_send()

        loop(0, blocks, drain)

        @pl.when(core == 0)
        def _():
            loop(0, half, lambda slot: core_copy(slot).wait_send())

        def finish(slot):
            x_copy(slot).wait_send()
            here, there = out_copies(slot)
            here.wait()
            there.wait()

        loop(0, half, finish)


def intra_back_kernel(idx, d_mixer, pre_i, pre_p, aux, low_t, d_gate, d_scaled, d_maps, g_wg):
    @pl.when(pl.program_id(0) == 0)
    def _():
        g_wg[...] = jnp.zeros_like(g_wg)

    g_wg[...] += dot(low_t[...], d_gate[...])
    width = d_mixer.shape[1]
    base = idx[1] + pl.program_id(0) * BLOCK
    maps, _ = silu_parts(pre_p[...])
    values, _ = silu_parts(pre_i[...])
    for c in range(BLOCK // CHUNK):
        at = slice(c * CHUNK, (c + 1) * CHUNK)
        table = aux[at, :]
        rows = jnp.transpose(table)
        joined = masks(table, base + c * CHUNK, True)
        keys = maps[at, :LANES].astype(BF16)
        reads = maps[at, LANES:].astype(BF16)
        scores = dot(keys, reads, 1, 1)
        scaled = (values[at] * expand(table, DT, width)).astype(BF16)
        grads = d_mixer[at, :]
        d_scores = jnp.zeros((CHUNK, CHUNK), F32)
        parts = []
        for pair in range(width // LANES):
            split = head_split(grads, pair)
            d_weights = dot(scaled[:, pair * LANES : (pair + 1) * LANES], split, 1, 1)
            weights = []
            for side in range(2):
                h = 2 * pair + side
                gap = rows[CUM + h : CUM + h + 1, :] - table[:, CUM + h : CUM + h + 1]
                factor = jnp.exp(jnp.where(joined, gap, -1e30))
                weights.append((scores * factor).astype(BF16))
                d_scores = d_scores + factor * d_weights[:, side * CHUNK : (side + 1) * CHUNK]
            parts.append(dot(jnp.concatenate(weights, axis=1), split))
        d_scaled[at, :] = jnp.concatenate(parts, axis=1)
        low_scores = d_scores.astype(BF16)
        d_maps[at, :] = jnp.concatenate([dot(low_scores, reads), dot(low_scores, keys, 0, 0)], axis=1)


def conv_back(grad, within, inputs, edge_inputs, weight, shifted, first, last, acc):
    rows = grad.shape[0]

    @pl.when(first)
    def _():
        for ref in shifted:
            ref[...] = jnp.zeros_like(ref)

    weight = weight[...].astype(F32)
    total = grad * weight[3:4]
    edge = jnp.zeros((8, grad.shape[1]), F32)
    acc[3:4] += jnp.sum(grad * inputs, axis=0, keepdims=True)
    acc[4:5] += jnp.sum(grad, axis=0, keepdims=True)
    for k, ref in enumerate(shifted):
        ref[8 : 8 + rows] = grad * (within >= float(3 - k)).astype(F32)
        moved = ref[3 - k : 3 - k + 8 + rows]
        total = total + moved[8:] * weight[k : k + 1]
        edge = edge + moved[:8] * weight[k : k + 1]
        outer = jnp.where(last, edge_inputs, 0.0) * moved[:8]
        acc[k : k + 1] += jnp.sum(moved[8:] * inputs, axis=0, keepdims=True) + jnp.sum(outer, axis=0, keepdims=True)
        ref[8 + rows :] = ref[8:16]
    return total, edge


def device_copy(src, dst, sems, slot, to):
    return pltpu.make_async_remote_copy(
        src_ref=src, dst_ref=dst, send_sem=sems[0].at[slot], recv_sem=sems[1].at[slot],
        device_id=to, device_id_type=pl.DeviceIdType.MESH,
    )


def loop(start, stop, body):
    def run(d, carry):
        body(d)
        return carry

    lax.fori_loop(start, stop, run, 0)


def rows_at(ref, index, size):
    return ref.at[pl.ds(pl.multiple_of(index * size, size), size)]


class SeqSum:
    def __init__(self, source, first, land1, second, land2, done, sems):
        self.source, self.first, self.land1, self.second, self.land2, self.done = source, first, land1, second, land2, done
        self.sems = [sems[i : i + 2] for i in range(0, 8, 2)]
        self.wire = first.dtype
        self.members = land2.shape[0]
        self.piece = first.shape[0] // self.members
        me = lax.axis_index("seq")
        self.side, self.place = lax.rem(me, 2), me // 2
        self.partner = {"seq": me + 1 - 2 * self.side}

    def half(self, ref, side):
        return rows_at(ref, side, self.members * self.piece)

    def member(self, d):
        return lax.rem(self.place + d, self.members)

    def to_member(self, d):
        return {"seq": 2 * self.member(d) + self.side}

    def halve(self):
        return device_copy(self.first, self.land1, self.sems[0], 0, self.partner)

    def scatter(self, d):
        src = rows_at(self.second, self.member(d), self.piece)
        return device_copy(src, self.land2.at[d], self.sems[1], d, self.to_member(d))

    def part(self, place):
        return rows_at(self.done, self.side * self.members + place, self.piece)

    def gather(self, d):
        ref = self.part(self.place)
        return device_copy(ref, ref, self.sems[2], d, self.to_member(d))

    def gathered(self, d):
        ref = self.part(lax.rem(self.place + self.members - d, self.members))
        return device_copy(ref, ref, self.sems[2], d, self.partner)

    def widen(self, side):
        ref = self.half(self.done, side)
        return device_copy(ref, ref, self.sems[3], 0, self.partner)

    def begin(self):
        self.first[...] = self.half(self.source, 1 - self.side)[...].astype(self.wire)
        self.halve().start()

    def pass_on(self):
        self.halve().wait_recv()
        self.second[...] = (self.half(self.source, self.side)[...] + self.land1[...].astype(F32)).astype(self.wire)
        loop(1, self.members, lambda d: self.scatter(d).start())

    def finish(self):
        own = rows_at(self.source, self.side * self.members + self.place, self.piece)[...]
        own = own + rows_at(self.land1, self.place, self.piece)[...].astype(F32)

        def add(d, total):
            self.scatter(d).wait_recv()
            return total + self.land2[d].astype(F32)

        self.part(self.place)[...] = lax.fori_loop(1, self.members, add, own).astype(self.wire)
        loop(1, self.members, lambda d: self.gather(d).start())

    def collect(self):
        loop(1, self.members, lambda d: self.gathered(d).wait_recv())
        self.widen(self.side).start()

    def store(self, out):
        self.half(out, self.side)[...] = self.half(self.done, self.side)[...].astype(F32)
        self.widen(1 - self.side).wait_recv()
        self.half(out, 1 - self.side)[...] = self.half(self.done, 1 - self.side)[...].astype(F32)

    def drain(self):
        self.halve().wait_send()
        self.widen(self.side).wait_send()

        def both(d):
            self.scatter(d).wait_send()
            self.gather(d).wait_send()

        loop(1, self.members, both)

    @staticmethod
    def scratch(rows, lanes, wire, size):
        members = size // 2
        half = pltpu.VMEM((members * rows, lanes), wire)
        dma = pltpu.SemaphoreType.DMA
        return [half, half, half, pltpu.VMEM((members, rows, lanes), wire), pltpu.VMEM((2 * members * rows, lanes), wire)] + [
            dma((1,)), dma((1,)), dma((members,)), dma((members,)), dma((members,)), dma((members,)), dma((1,)), dma((1,)),
        ]


SUM_REFS = 13


class HeadSum:
    def __init__(self, source, out, fold1, half, fold2, quarter, sems):
        self.source, self.out, self.fold1, self.held, self.fold2, self.quarter = source, out, fold1, half, fold2, quarter
        self.sems = [sems[i : i + 2] for i in range(0, 8, 2)]
        self.rows = source.shape[0]
        head = lax.axis_index("head")
        self.core, self.plane = lax.rem(head, 2), head // 2
        self.beside, self.across = {"head": head + 1 - 2 * self.core}, {"head": head + 2 - 4 * self.plane}

    def fold_core(self):
        return device_copy(rows_at(self.source, 1 - self.core, self.rows // 2), self.fold1, self.sems[0], 0, self.beside)

    def fold_plane(self):
        return device_copy(rows_at(self.held, 1 - self.plane, self.rows // 4), self.fold2, self.sems[1], 0, self.across)

    def spread_plane(self, plane):
        ref = rows_at(self.out, 2 * self.core + plane, self.rows // 4)
        return device_copy(ref, ref, self.sems[2], 0, self.across)

    def spread_core(self, core):
        ref = rows_at(self.out, core, self.rows // 2)
        return device_copy(ref, ref, self.sems[3], 0, self.beside)

    def fold(self):
        self.fold_core().wait_recv()
        self.held[...] = rows_at(self.source, self.core, self.rows // 2)[...] + self.fold1[...]
        self.fold_plane().start()

    def settle(self):
        self.fold_plane().wait_recv()
        self.quarter[...] = jnp.zeros_like(self.quarter)
        self.quarter[: self.rows // 4] = rows_at(self.held, self.plane, self.rows // 4)[...] + self.fold2[...]

    def spread(self, total):
        rows_at(self.out, 2 * self.core + self.plane, self.rows // 4)[...] = total[: self.rows // 4]
        self.spread_plane(self.plane).start()

    def spread_more(self):
        self.spread_plane(1 - self.plane).wait_recv()
        self.spread_core(self.core).start()

    def finish(self):
        self.spread_core(1 - self.core).wait_recv()
        self.fold_core().wait_send()
        self.fold_plane().wait_send()
        self.spread_plane(self.plane).wait_send()
        self.spread_core(self.core).wait_send()

    @staticmethod
    def scratch(rows, lanes, padded_rows):
        dma = pltpu.SemaphoreType.DMA
        shapes = [(rows // 2, lanes), (rows // 2, lanes), (rows // 4, lanes), (padded_rows, lanes)]
        return [pltpu.VMEM(shape, F32) for shape in shapes] + [dma((1,))] * 8


HEAD_REFS = 12


def finale_kernel(
    d_scaled, d_maps, pre_i, pre_p, in_i, in_p, halo_low, halo_i, halo_p, aux, gloc, pkl, gin, states, d_mixer, mixer, given,
    conv_i, conv_p, low_t, d_gate, wg, wi, ws, wp, hid, d_out, gain, error, g_wo, g_wg, g_gain, factor,
    grad_all, out_norm, out_loss, out_wo, out_wg, out_wi, out_wp, out_ws, out_conv_i, out_bias_i, out_conv_p, out_bias_p,
    out_sbias, out_dlog, out_skip, out_gain,
    shift_i0, shift_i1, shift_i2, shift_p0, shift_p1, shift_p2, small, small_p, heads,
    parts, land, mine, other, row, row_land, g_wi, g_ws, pack, g_wp, pair_small, sum_small, sum_wp, sum_pack, spread_wp, spread_small,
    grad_own, grad_other, w_t, edge, edge_core, edge_plane, edge_ahead,
    core_send, core_land, x_send, x_land, edge_send, edge_land, grad_send, grad_land, row_send, row_arrive, *more,
):
    shifted = (shift_i0, shift_i1, shift_i2, shift_p0, shift_p1, shift_p2)
    step = pl.program_id(0)
    blocks = pl.num_programs(0)
    half = blocks // 2
    first, last = step == 0, step == blocks - 1
    seq, devices = lax.axis_index("seq"), lax.axis_size("seq")
    head, core = lax.axis_index("head"), core_bit()
    width = wi.shape[1]
    model = low_t.shape[0]
    behind, ahead = lax.rem(seq + devices - 1, devices), lax.rem(seq + 1, devices)
    group = 2 * devices
    me = 2 * seq + core
    beside, across = {"head": core_peer()}, {"head": lax.rem(head + 2, 4)}
    summing = len(more) > 0

    more = list(more)

    def take(number):
        taken = more[:number]
        del more[:number]
        return taken

    seq_sums, wide = [], []
    if summing:
        head_parts = []
        for source, out in ((g_wp, spread_wp), (pair_small, spread_small)):
            refs = take(HEAD_REFS)
            head_parts.append(HeadSum(source, out, *refs[:4], refs[4:]))
        third = model // 3
        thirds = [g_wi.at[pl.ds(i * third, third)] for i in range(3)]
        outs_wi = [out_wi.at[pl.ds(i * third, third)] for i in range(3)]
        for source in (g_wo, g_wg, *thirds, pack, head_parts[0].quarter, head_parts[1].quarter):
            refs = take(SUM_REFS)
            seq_sums.append(SeqSum(source, *refs[:5], refs[5:]))
        s_wo, s_wg, *s_wi, s_pack, s_wp, s_small = seq_sums
        wide = list(zip(head_parts, (s_wp, s_small), (sum_wp, sum_small)))

    def device(distance):
        to = lax.rem(me + distance, group)
        return {"seq": to // 2, "head": head - core + lax.rem(to, 2)}

    def hand(distance):
        return device_copy(row, row_land.at[me], (row_send, row_arrive), distance, device(distance))

    def edge_copy(slot, landing, to):
        return device_copy(edge.at[slot], landing, (edge_send, edge_land), slot, to)

    def core_copy(slot):
        return device_copy(parts.at[slot], land.at[slot], (core_send, core_land), slot, beside)

    def x_copy(slot):
        return device_copy(mine.at[slot], other.at[slot], (x_send, x_land), slot, across)

    def grad_copy(slot):
        return device_copy(grad_own.at[slot], grad_other.at[slot], (grad_send, grad_land), slot, beside)

    @pl.when(first)
    def _():
        barrier = pltpu.get_barrier_semaphore()

        def greet(to):
            pl.semaphore_signal(barrier, inc=1, device_id=to, device_id_type=pl.DeviceIdType.MESH)

        loop(1, group, lambda d: greet(device(d)))
        greet(across)
        for ref in (g_wi, g_ws, pack, g_wp, pair_small, small, small_p, heads):
            ref[...] = jnp.zeros_like(ref)
        row[:1] = jnp.zeros_like(row[:1])
        row[1:] = error[...]
        filled = 0
        for weight in (wg, wi, ws, wp, wp):
            w_t[filled : filled + weight.shape[1]] = jnp.transpose(weight[...])
            filled += weight.shape[1]
        pl.semaphore_wait(barrier, group)
        if summing:
            s_wo.begin()
            s_wg.begin()

    base = seq * (blocks * BLOCK) + (blocks - 1 - step) * BLOCK
    maps, slope_p = silu_parts(pre_p[...])
    values, slope = silu_parts(pre_i[...])
    dy = d_mixer[...]
    upper = triangle(True)
    lane = lax.broadcasted_iota(jnp.int32, (CHUNK, LANES), 1)
    grown = jnp.exp(given[1:2])
    skip = expand(given[...], 0, width)[2:3]
    pieces, pieces_p, pieces_s = [], [], []
    for c in range(BLOCK // CHUNK):
        at = slice(c * CHUNK, (c + 1) * CHUNK)
        table = aux[at, :]
        sizes = expand(table, DT, width)
        inflow = expand(table, INFLOW, width)
        outflow = expand(table, TAIL, width)
        keys, reads = maps[at, :LANES], maps[at, LANES:]
        scaled = values[at] * sizes
        grad_state = gloc[c] + pkl[c, :1] * gin[...]
        state = states[c]
        passed = outflow * dot3(keys, grad_state)
        total = d_scaled[at, :] + passed
        d_reads = d_maps[at, LANES:] + dot3(dy[at] * inflow, state, 1, 1)
        d_keys = d_maps[at, :LANES] + dot3(scaled * outflow, grad_state, 1, 1)
        pieces_p.append(jnp.concatenate([d_keys, d_reads], axis=1))
        plain = mixer[at, :] - skip * values[at]
        d_cum = head_sums(dy[at] * plain - scaled * total)
        carried = jnp.sum(grad_state * state, axis=0, keepdims=True) * inflow[CHUNK - 1 :]
        carried = carried + jnp.sum(scaled * passed, axis=0, keepdims=True)
        after = head_sums(jnp.broadcast_to(carried, (8, width)))[:1]
        d_logs = triangle_sums(upper, d_cum) + after
        d_raw = (head_sums(total * values[at]) - grown * d_logs) * pltpu.roll(table, LANES - RATE, 1)
        d_raw = jnp.where(lane < 8, d_raw, 0.0)
        pieces_s.append(d_raw.astype(BF16))
        d_decay = jnp.where(lane < 8, -d_logs * table * grown, 0.0)
        heads[0:1] += jnp.sum(d_raw, axis=0, keepdims=True)
        heads[1:2] += jnp.sum(d_decay, axis=0, keepdims=True)
        pieces.append(total * sizes + dy[at] * skip)
    small[5:6] += jnp.sum(dy * values, axis=0, keepdims=True)
    grad = jnp.concatenate(pieces, axis=0) * slope
    pos = (base + lax.broadcasted_iota(jnp.int32, (BLOCK, 1), 0)).astype(F32)
    within = pos - aux[:, START : START + 1]
    whole, outer = conv_back(
        grad, within, in_i[...].astype(F32), halo_i[8:].astype(F32), conv_i, shifted[:3], first, last, small
    )
    grad_p = jnp.concatenate(pieces_p, axis=0) * slope_p
    whole_p, outer_p = conv_back(
        grad_p, within, in_p[...].astype(F32), halo_p[8:].astype(F32), conv_p, shifted[3:], first, last, small_p
    )

    inner = whole.astype(BF16)
    d_step = jnp.concatenate(pieces_s, axis=0)
    high, rest = halves(whole_p)
    part = dot(jnp.concatenate([d_gate[...], inner, d_step, high, rest], axis=1), w_t[...])
    upper = (step < half).astype(jnp.int32)
    slot = half - 1 - lax.rem(step, half)
    own = upper == core

    def settle(at):
        core_copy(at).wait_recv()
        mine[at] = (parts[at].astype(F32) + land[at].astype(F32)).astype(BF16)
        x_copy(at).start()

    @pl.when((step > 0) & ((step - 1 < half).astype(jnp.int32) == core))
    def _():
        settle(half - 1 - lax.rem(step - 1, half))

    @pl.when((step >= half) & (core == 0))
    def _():
        core_copy(slot).wait_send()

    parts[slot] = part.astype(parts.dtype)

    @pl.when(jnp.logical_not(own))
    def _():
        core_copy(slot).start()

    products = dot(low_t[...], jnp.concatenate([inner, d_step, high, rest], axis=1))
    g_wi[:model] += products[:, :width]
    g_ws[...] += products[:, width : width + LANES]
    to_pair = products[:, width + LANES :]
    g_wp[...] += to_pair[:, : to_pair.shape[1] // 2] + to_pair[:, to_pair.shape[1] // 2 :]

    def norm_back(at):
        x_copy(at).wait_recv()
        block_rows = pl.ds(at * BLOCK, BLOCK)
        d_low = mine[at].astype(F32) + other[at].astype(F32)
        if at == half - 1:
            edge_copy(2, edge_ahead, {"seq": behind}).wait_recv()
            there = ((core == 1) & (seq < devices - 1)).astype(F32)
            d_low = jnp.concatenate([d_low[: BLOCK - 8], d_low[BLOCK - 8 :] + there * edge_ahead[...]], axis=0)
        rows = hid[block_rows, :].astype(F32)
        scale = lax.rsqrt(jnp.mean(rows * rows, axis=1, keepdims=True) + EPSILON)
        row[:1] += jnp.sum(d_low * rows * scale, axis=0, keepdims=True)
        scaled = d_low * gain[...]
        pull = jnp.mean(scaled * rows, axis=1, keepdims=True) * (scale * scale * scale)
        block = (d_out[block_rows, :] + scale * scaled - rows * pull).astype(BF16)
        grad_own[at] = block
        grad_copy(at).start()
        rows_at(grad_all, core * half + at, BLOCK)[...] = block

    if summing:

        moves = (s_wo.pass_on, s_wg.pass_on, s_wo.finish, s_wg.finish, s_wo.collect)
        for number, move in enumerate(moves):

            @pl.when(step == number + 2)
            def _(move=move):
                move()

    @pl.when(last)
    def _():
        before = jnp.concatenate([jnp.zeros_like(outer), outer], axis=0).astype(BF16)
        g_wi[:model] += dot(halo_low[...], before, 0, 0)
        before_p = jnp.concatenate([jnp.zeros_like(outer_p), outer_p], axis=0)
        high_p, rest_p = halves(before_p)
        g_wp[...] += dot(halo_low[...], high_p, 0, 0) + dot(halo_low[...], rest_p, 0, 0)
        edge_in = jnp.concatenate([before, jnp.zeros((16, LANES), BF16), high_p, rest_p], axis=1)
        edge_part = dot(edge_in, w_t[width:])
        edge[0] = edge_part[8:]
        edge_copy(0, edge_core, beside).start()
        pack[:6] = small[:6]
        pack[6:7] = g_gain[...]
        step_rows = jnp.transpose(g_ws[...])[:8]
        pack[8:16] = step_rows[:, :width]
        pack[16:24] = step_rows[:, width:]
        pack[24:32, : heads.shape[1]] = heads[...]
        pair_small[:8] = small_p[...]
        if summing:
            for h_sum, _, _ in wide:
                h_sum.fold_core().start()
            s_wi[0].begin()
            s_wi[1].begin()

        if summing:
            for h_sum, _, _ in wide:
                h_sum.fold()

        @pl.when(core == 0)
        def _():
            settle(0)

        if summing:
            s_wi[2].begin()
            s_pack.begin()
        edge_copy(0, edge_core, beside).wait_recv()
        edge[1] = edge[0] + edge_core[...]
        edge_copy(1, edge_plane, across).start()
        if summing:
            s_wg.collect()
            s_wi[0].pass_on()
            s_wi[1].pass_on()
        edge_copy(1, edge_plane, across).wait_recv()
        edge[2] = edge[1] + edge_plane[...]
        edge_copy(2, edge_ahead, {"seq": behind}).start()
        for h_sum, s_sum, _ in wide:
            h_sum.settle()
            s_sum.begin()
        norm_back(2)
        norm_back(1)
        if summing:
            s_wi[2].pass_on()
            s_pack.pass_on()
            s_wi[0].finish()
        for _, s_sum, _ in wide:
            s_sum.pass_on()
        norm_back(0)
        norm_back(3)
        loop(1, group, lambda d: hand(d).start())
        if summing:
            s_wi[1].finish()
            s_wi[2].finish()
            s_pack.finish()
            for _, s_sum, _ in wide:
                s_sum.finish()
            s_wi[0].collect()
            s_wo.store(out_wo)
            s_wi[1].collect()
            s_wi[2].collect()
            for _, s_sum, _ in wide:
                s_sum.collect()
            s_pack.collect()
            s_wg.store(out_wg)
            for h_sum, s_sum, total in wide:
                s_sum.store(total)
                h_sum.spread(total)
            for s_sum, out in zip(s_wi, outs_wi):
                s_sum.store(out)
            for h_sum, _, _ in wide:
                h_sum.spread_more()
            s_pack.store(sum_pack)
            for h_sum, _, _ in wide:
                h_sum.finish()
            out_wp[...] = spread_wp[...]
            totals, pair_totals = sum_pack[:32], spread_small[:8]
            for s_sum in seq_sums:
                s_sum.drain()
        else:
            for out, ref in ((out_wo, g_wo), (out_wg, g_wg), (out_wi, g_wi), (out_wp, g_wp)):
                out[...] = ref[...]
            totals, pair_totals = pack[:32], pair_small[:8]
        heads_here = out_sbias.shape[1]
        out_conv_i[...] = totals[:4]
        out_bias_i[...] = totals[4:5]
        out_skip[...] = head_sums(totals[:8])[5:6, :heads_here]
        out_gain[...] = totals[6:7]
        out_ws[...] = jnp.transpose(jnp.concatenate([totals[8:16], totals[16:24]], axis=1))[:, :heads_here]
        out_sbias[...] = totals[24:25, :heads_here]
        out_dlog[...] = totals[25:26, :heads_here]
        out_conv_p[...] = pair_totals[:4]
        out_bias_p[...] = pair_totals[4:5]
        row_land[me] = row[...]
        loop(1, group, lambda d: hand(d).wait())
        both_rows = lax.fori_loop(1, group, lambda d, total: total + row_land[d], row_land[0])
        out_norm[...] = both_rows[:1]
        per_token = factor[0] / (group * half * BLOCK * model)
        out_loss[...] = jnp.sum(both_rows[1:], axis=1, keepdims=True) * per_token
        for at, to in enumerate((beside, across, {"seq": behind})):
            edge_copy(at, edge_core, to).wait_send()

        @pl.when(core == 1)
        def _():
            loop(0, half, lambda at: core_copy(at).wait_send())

        def drain(at):
            x_copy(at).wait_send()
            grad_copy(at).wait()
            rows_at(grad_all, (1 - core) * half + at, BLOCK)[...] = grad_other[at]

        loop(0, half, drain)


def call(kernel, grid, ins, outs, scratch=(), prefetch=0, flops=0, moved=0, collective=None, vmem=14):
    def spec(shape, block, index, **single):
        if block is None:
            return pl.BlockSpec(shape, lambda *_: (0,) * len(shape), **single)
        if isinstance(block, str):
            return pl.BlockSpec(memory_space={"smem": pltpu.SMEM, "vmem": pltpu.VMEM, "any": pl.ANY}[block])
        return pl.BlockSpec(block, index)

    scalars = [a for a, *_ in ins[:prefetch]]
    arrays = ins[prefetch:]
    extra = {} if collective is None else {"collective_id": collective, "has_side_effects": True}
    return pl.pallas_call(
        kernel,
        grid_spec=pltpu.PrefetchScalarGridSpec(
            num_scalar_prefetch=prefetch,
            grid=(grid,),
            in_specs=[spec(a.shape, block, index, pipeline_mode=pl.Buffered(1)) for a, block, index in arrays],
            out_specs=[spec(shape, block, index) for shape, _, block, index in outs],
            scratch_shapes=list(scratch),
        ),
        out_shape=[jax.ShapeDtypeStruct(shape, dtype) for shape, dtype, _, _ in outs],
        compiler_params=pltpu.CompilerParams(
            dimension_semantics=("arbitrary",), vmem_limit_bytes=vmem << 20, **extra
        ),
        cost_estimate=pl.CostEstimate(flops=int(flops), bytes_accessed=int(moved), transcendentals=0),
    )(*scalars, *[a for a, *_ in arrays])


def swap(value, axis, bit):
    route = [(i, i ^ bit) for i in range(lax.axis_size(axis))]
    return jax.tree.map(lambda v: lax.ppermute(v, axis, route), value)


def shifted(value, axis, distance):
    devices = range(lax.axis_size(axis))
    route = [(i - distance, i) for i in devices if i - distance in devices]
    return lax.ppermute(value, axis, route)


def bits(axis):
    size = lax.axis_size(axis)
    return [1 << b for b in range(size.bit_length() - 1)]


def total_over(value, axis):
    for bit in bits(axis):
        value = value + swap(value, axis, bit)
    return value


def carried(total, axis, backward):
    mine = lax.axis_index(axis)
    decays = slice(CHUNK, total.shape[0] - 1)

    def join(early, late):
        decay = late[CHUNK : CHUNK + 1]
        return jnp.concatenate([
            late[:CHUNK] + decay * early[:CHUNK], late[decays] * early[decays], late[-1:] + early[-1:],
        ])

    reached = jnp.concatenate([jnp.zeros_like(total[:CHUNK]), jnp.ones_like(total[CHUNK:])])
    for bit in bits(axis):
        other = swap(total, axis, bit)
        later = ((mine & bit) == 0) if backward else ((mine & bit) != 0)
        reached = jnp.where(later, join(other, reached), reached)
        total = jnp.where(later, join(other, total), join(total, other))
    return reached[:CHUNK], total[-1, 0]


def shards(
    hidden, teacher, doc_starts, valid_mask, norm_gain, w_gate, w_inner, w_pair, w_step, conv_inner, bias_inner,
    conv_pair, bias_pair, step_bias, decay_log, skip_gain, gate_gain, w_output,
):
    rows, model = hidden.shape
    width = w_inner.shape[1]
    pair_width = w_pair.shape[1]
    heads = step_bias.shape[0]
    blocks, chunks = rows // BLOCK, rows // CHUNK
    per = BLOCK // CHUNK
    half = blocks // 2
    inner_total = float(width * lax.axis_size("head"))
    core = lax.axis_index("head") & 1
    offset = lax.axis_index("seq") * rows
    idx = jnp.stack([core, offset]).astype(jnp.int32)
    edge_rows = 16

    given = jnp.stack([
        jnp.pad(step_bias, (0, LANES - heads)), jnp.pad(decay_log, (0, LANES - heads)), jnp.pad(skip_gain, (0, LANES - heads)),
        jnp.pad(doc_starts.astype(F32), (0, LANES - doc_starts.shape[0]), constant_values=FAR),
        *[jnp.zeros((LANES,), F32)] * 4,
    ])
    ws = jnp.pad(w_step, ((0, 0), (0, LANES - heads)))
    gain, out_gain = norm_gain[None, :], gate_gain[None, :]
    bias_i, bias_p = bias_inner[None, :], bias_pair[None, :]
    valid = valid_mask[None, :]

    tail = shifted(hidden[rows - edge_rows :], "seq", 1)

    def by(w, column=0):
        return (BLOCK, w), lambda i, *_: (i, column)

    def back(w, column=0):
        return (BLOCK, w), lambda i, *_: (blocks - 1 - i, column)

    grid3 = lambda n: ((per, n, width), lambda i, *_: (i, 0, 0))
    back3 = lambda n: ((per, n, width), lambda i, *_: (blocks - 1 - i, 0, 0))
    whole = (None, None)

    dma = pltpu.SemaphoreType.DMA

    halo_block = ((edge_rows, model), lambda i, *_: (jnp.maximum(i * (BLOCK // edge_rows) - 1, 0), 0))
    (low, low_t, in_i, in_p, pre_i, pre_p, aux, halo_low, halo_i, halo_p, sloc, pkl, fin) = call(
        project_kernel,
        blocks,
        [
            (idx, None, None), (given, *whole), (valid, (1, BLOCK), lambda i, *_: (0, i)), (hidden, *by(model)), (hidden, *halo_block), (tail, *whole),
            (gain, *whole), (w_inner, *whole), (w_pair, *whole), (ws, *whole), (conv_inner, *whole), (conv_pair, *whole),
            (bias_i, *whole), (bias_p, *whole),
        ],
        [
            ((rows, model), BF16, *by(model)), ((model, rows), BF16, (model, BLOCK), lambda i, *_: (0, i)),
            ((rows, width), BF16, *by(width)), ((rows, pair_width), BF16, *by(pair_width)),
            ((rows, width), F32, *by(width)), ((rows, pair_width), F32, *by(pair_width)), ((rows, LANES), F32, *by(LANES)),
            ((edge_rows, model), BF16, *whole), ((edge_rows, width), BF16, *whole), ((edge_rows, pair_width), BF16, *whole),
            ((chunks, CHUNK, width), F32, *grid3(CHUNK)), ((chunks, 8, width), F32, *grid3(8)),
            ((CHUNK + 8, width), F32, *whole),
        ],
        [
            pltpu.VMEM((BLOCK + edge_rows, width), F32), pltpu.VMEM((BLOCK + edge_rows, pair_width), F32),
            pltpu.VMEM((CHUNK, width), F32), pltpu.VMEM((8, width), F32), pltpu.VMEM((1, 1), F32),
        ],
        prefetch=1, flops=3e9, moved=2e7,
    )
    state_in, count = carried(fin, "seq", False)
    factor = (rows * lax.axis_size("seq")) / count
    gate, local = call(
        intra_kernel,
        blocks,
        [
            (idx, None, None), (low, *by(model)), (w_gate, *whole), (pre_i, *by(width)), (pre_p, *by(pair_width)),
            (aux, *by(LANES)), (given, *whole),
        ],
        [((rows, width), F32, *by(width)), ((rows, width), F32, *by(width))],
        prefetch=1, flops=4e9, moved=2e7,
    )
    size = lax.axis_size("seq")
    vmem = ("vmem", None)
    once = lambda w: ((rows // 2, w), lambda i: (core_bit(), 0))
    first_or_last = lambda i: jnp.where(i < blocks, i, jnp.clip(i - 2 * blocks - 1, 0, blocks - 1))
    early = lambda i: jnp.minimum(i, blocks - 1)
    late = lambda i: jnp.clip(i - 2 * blocks - 1, 0, blocks - 1)
    own_slot = lambda i: jnp.clip(i - 2 * blocks - half * core_bit(), 0, half - 1)
    early3 = lambda n: ((per, n, width), lambda i: (early(i), 0, 0))
    states, d_mixer, d_gate, gloc, pkb, fin_back, output, d_out, error, g_gain, g_wo, mixer = call(
        partial(mid_kernel, total=inner_total),
        3 * blocks + 1,
        [
            (factor.reshape(1), "smem", None), (pre_p, (BLOCK, LANES), lambda i: (first_or_last(i), 1)),
            (aux, (BLOCK, LANES), lambda i: (first_or_last(i), 0)), (sloc, *early3(CHUNK)), (pkl, *early3(8)), (state_in, *whole),
            (local, (BLOCK, width), lambda i: (early(i), 0)), (gate, *vmem), (out_gain, *whole), (w_output, *whole),
            (hidden, *once(model)), (teacher, *once(model)),
            (valid, (1, BLOCK), lambda i: (0, own_slot(i) + half * core_bit())),
        ],
        [
            ((chunks, CHUNK, width), F32, *early3(CHUNK)), ((rows, width), F32, (BLOCK, width), lambda i: (late(i), 0)),
            ((rows, width), BF16, (BLOCK, width), lambda i: (late(i), 0)), ((chunks, CHUNK, width), F32, *vmem),
            ((chunks, 8, width), F32, *vmem), ((CHUNK + 8, width), F32, *vmem), ((rows, model), BF16, "any", None),
            ((rows // 2, model), F32, (BLOCK, model), lambda i: (own_slot(i), 0)), ((1, model), F32, *whole),
            ((1, width), F32, *whole), ((width, model), F32, *whole), ((blocks, BLOCK, width), F32, *vmem),
        ],
        [
            pltpu.VMEM((blocks, 1, BLOCK), F32), pltpu.VMEM((4, blocks, 1, BLOCK), F32),
            pltpu.VMEM((blocks, 1, BLOCK), F32), pltpu.VMEM((4, blocks, 1, BLOCK), F32), pltpu.VMEM((blocks, 1, BLOCK), F32),
            pltpu.VMEM((half, BLOCK, model), F32), pltpu.VMEM((half, BLOCK, model), F32),
            pltpu.VMEM((half, BLOCK, model), BF16), pltpu.VMEM((half, BLOCK, model), BF16),
            pltpu.VMEM((blocks, BLOCK, model), BF16), pltpu.VMEM((half, BLOCK, model), BF16),
            pltpu.VMEM((2, BLOCK, width), F32), pltpu.VMEM((chunks, 8, width), F32), pltpu.VMEM((CHUNK, width), F32),
            pltpu.VMEM((model, width), BF16), dma((4 * blocks,)), dma((4 * blocks,)), dma((4 * blocks,)), dma((4 * blocks,)), dma((half,)), dma((half,)),
            dma((half,)), dma((half,)), dma((blocks,)), dma((blocks,)), dma((half,)), dma((half,)), dma((half,)),
        ],
        flops=6e9, moved=6e7, collective=2, vmem=44,
    )
    mixer = mixer.reshape(rows, width)
    grad_in, _ = carried(fin_back, "seq", True)
    d_scaled, d_maps, g_wg = call(
        intra_back_kernel,
        blocks,
        [
            (idx, None, None), (d_mixer, *by(width)), (pre_i, *by(width)), (pre_p, *by(pair_width)), (aux, *by(LANES)),
            (low_t, (model, BLOCK), lambda i, *_: (0, i)), (d_gate, *by(width)),
        ],
        [((rows, width), F32, *by(width)), ((rows, pair_width), F32, *by(pair_width)), ((model, width), F32, *whole)],
        prefetch=1, flops=6e9, moved=2e7,
    )
    summing = size <= 8

    def piece(total_rows, tile):
        return -(-total_rows // (size * tile)) * tile

    r_wo, r_w, r_pack, r_wp, r_small = piece(width, 16), piece(model, 16), 8, piece(model // 4, 8), 8
    core_wire = F32 if summing else BF16
    sum_shapes = [(r_wo, model, BF16), (r_w, width, BF16), *[(piece(model // 3, 16), width, BF16)] * 3, (r_pack, width, F32), (r_wp, pair_width, F32),
                  (r_small, pair_width, F32)]
    n_wo, n_w, n_pack = (r_wo * size, r_w * size, r_pack * size) if summing else (width, model, 64)
    scratch = [pltpu.VMEM((BLOCK + 16, width), F32)] * 3 + [pltpu.VMEM((BLOCK + 16, pair_width), F32)] * 3 + [
        pltpu.VMEM((8, width), F32), pltpu.VMEM((8, pair_width), F32), pltpu.VMEM((8, LANES), F32),
        pltpu.VMEM((half, BLOCK, model), core_wire), pltpu.VMEM((half, BLOCK, model), core_wire),
        pltpu.VMEM((half, BLOCK, model), BF16), pltpu.VMEM((half, BLOCK, model), BF16),
        pltpu.VMEM((2, model), F32), pltpu.VMEM((2 * size, 2, model), F32),
        pltpu.VMEM((n_w, width), F32), pltpu.VMEM((model, LANES), F32), pltpu.VMEM((n_pack, width), F32),
        pltpu.VMEM((model, pair_width), F32), pltpu.VMEM((32, pair_width), F32),
        pltpu.VMEM((r_small * size, pair_width), F32), pltpu.VMEM((r_wp * size, pair_width), F32),
        pltpu.VMEM((n_pack, width), F32), pltpu.VMEM((model, pair_width), F32), pltpu.VMEM((32, pair_width), F32),
        pltpu.VMEM((half, BLOCK, model), BF16), pltpu.VMEM((half, BLOCK, model), BF16),
        pltpu.VMEM((2 * width + LANES + 2 * pair_width, model), BF16),
        pltpu.VMEM((3, 8, model), F32), pltpu.VMEM((8, model), F32), pltpu.VMEM((8, model), F32), pltpu.VMEM((8, model), F32),
        dma((half,)), dma((half,)), dma((half,)), dma((half,)), dma((3,)), dma((3,)), dma((half,)), dma((half,)),
        dma((2 * size,)), dma((2 * size,)),
    ]
    if summing:
        scratch += HeadSum.scratch(model, pair_width, r_wp * size) + HeadSum.scratch(32, pair_width, r_small * size)
        for r, lanes, wire in sum_shapes:
            scratch += SeqSum.scratch(r, lanes, wire, size)
    grad_hidden, g_norm, loss, *grads, g_wp, g_ws, g_ci, g_bi, g_cp, g_bp, g_sb, g_dl, g_skip, g_gain = call(
        finale_kernel,
        blocks,
        [
            (d_scaled, *back(width)), (d_maps, *back(pair_width)), (pre_i, *back(width)), (pre_p, *back(pair_width)),
            (in_i, *back(width)), (in_p, *back(pair_width)), (halo_low, *whole), (halo_i, *whole), (halo_p, *whole),
            (aux, *back(LANES)), (gloc, *back3(CHUNK)), (pkb, *back3(8)), (grad_in, *whole), (states, *back3(CHUNK)),
            (d_mixer, *back(width)), (mixer, *back(width)), (given, *whole), (conv_inner, *whole), (conv_pair, *whole),
            (low_t, (model, BLOCK), lambda i, *_: (0, blocks - 1 - i)), (d_gate, *back(width)), (w_gate, *whole), (w_inner, *whole), (ws, *whole), (w_pair, *whole),
            (hidden, *once(model)), (d_out, *vmem), (gain, *whole), (error, *whole), (g_wo, *vmem), (g_wg, *vmem),
            (g_gain, *whole), (factor.reshape(1), "smem", None),
        ],
        [
            ((rows, model), BF16, *vmem), ((1, model), F32, *vmem), ((1, 1), F32, *vmem), ((n_wo, model), F32, *vmem),
            ((n_w, width), F32, *vmem), ((n_w, width), F32, *vmem), ((model, pair_width), F32, *vmem),
            ((model, heads), F32, *vmem), ((4, width), F32, *vmem), ((1, width), F32, *vmem), ((4, pair_width), F32, *vmem),
            ((1, pair_width), F32, *vmem), ((1, heads), F32, *vmem), ((1, heads), F32, *vmem), ((1, heads), F32, *vmem),
            ((1, width), F32, *vmem),
        ],
        scratch,
        flops=9e9, moved=8e7, collective=4, vmem=58,
    )
    if not summing:
        *grads, g_ws, g_ci, g_bi, g_sb, g_dl, g_skip, g_gain = lax.psum(
            (*grads, g_ws, g_ci, g_bi, g_sb, g_dl, g_skip, g_gain), "seq"
        )
        g_wp, g_cp, g_bp = lax.psum((g_wp, g_cp, g_bp), ("seq", "head"))
    g_wo, g_wg, g_wi = grads
    return (
        output, loss.reshape(()), grad_hidden, g_norm.reshape(-1), g_wg, g_wi, g_wp, g_ws, g_ci, g_bi.reshape(-1), g_cp,
        g_bp.reshape(-1), g_sb.reshape(-1), g_dl.reshape(-1), g_skip.reshape(-1), g_gain.reshape(-1), g_wo,
    )


def solution(mesh):
    seq, head, wide = P("seq", None), P("head"), P(None, "head")
    in_specs = (
        seq, seq, P(), P("seq"), P(), wide, wide, P(), wide, wide, head, P(), P(), head, head, head, head, P("head", None),
    )
    out_specs = (
        seq, P(), seq, P(), wide, wide, P(), wide, wide, head, P(), P(), head, head, head, head, P("head", None),
    )
    return jax.shard_map(shards, mesh=mesh, in_specs=in_specs, out_specs=out_specs, check_vma=False)
```

```python
from functools import partial

import jax
import jax.numpy as jnp
from jax import lax
from jax.experimental import pallas as pl
from jax.experimental.pallas import tpu as pltpu
from jax.sharding import PartitionSpec as P

EPSILON = 1e-05
CHUNK = 128
BLOCK = 256
HEAD_DIM = 64
LANES = 128
FAR = float(1 << 24)
F32 = jnp.float32
BF16 = jnp.bfloat16

DT, CUM, INFLOW, TAIL, RATE, START, END = 0, 8, 16, 24, 32, 40, 41


def dot(a, b, da=1, db=0):
    return lax.dot_general(a, b, (((da,), (db,)), ((), ())), preferred_element_type=F32)


def halves(v):
    high = v.astype(BF16)
    return high, (v - high.astype(F32)).astype(BF16)


def dot3(a, b, da=1, db=0):
    ah, al = halves(a)
    bh, bl = halves(b)
    return dot(ah, bh, da, db) + (dot(ah, bl, da, db) + dot(al, bh, da, db))


def column_sums(v):
    folded = v[:, :LANES]
    for at in range(LANES, v.shape[1], LANES):
        folded = folded + v[:, at : at + LANES]
    return jnp.sum(jnp.transpose(folded), axis=0, keepdims=True)


def as_column(row, width=LANES):
    column = jnp.transpose(jnp.broadcast_to(row, (LANES, row.shape[1])))
    return jnp.concatenate([column] * (width // LANES), axis=1)


def expand(table, base, width):
    rows = table.shape[0]
    lane = lax.broadcasted_iota(jnp.int32, (rows, LANES), 1)
    parts = []
    for pair in range(width // LANES):
        first = jnp.broadcast_to(table[:, base + 2 * pair : base + 2 * pair + 1], (rows, LANES))
        second = jnp.broadcast_to(table[:, base + 2 * pair + 1 : base + 2 * pair + 2], (rows, LANES))
        parts.append(jnp.where(lane < HEAD_DIM, first, second))
    return jnp.concatenate(parts, axis=1)


def triangle_sums(ones, v):
    high, rest = halves(v)
    low = (v - high.astype(F32) - rest.astype(F32)).astype(BF16)
    sums = dot(ones, jnp.concatenate([high, rest, low], axis=1))
    return sums[:, :LANES] + (sums[:, LANES : 2 * LANES] + sums[:, 2 * LANES :])


def head_matrix(width):
    channel = lax.broadcasted_iota(jnp.int32, (width, LANES), 0)
    head = lax.broadcasted_iota(jnp.int32, (width, LANES), 1)
    return ((channel >> 6) == head).astype(BF16)


def head_sums(v):
    high, low = halves(v)
    matrix = head_matrix(v.shape[1])
    return dot(high, matrix) + dot(low, matrix)


def triangle(upper):
    row = lax.broadcasted_iota(jnp.int32, (CHUNK, CHUNK), 0)
    col = lax.broadcasted_iota(jnp.int32, (CHUNK, CHUNK), 1)
    return ((col >= row) if upper else (col <= row)).astype(BF16)


def silu_parts(pre):
    gate = jax.nn.sigmoid(pre)
    return pre * gate, gate * (1.0 + pre * (1.0 - gate))


def project_kernel(
    idx, given, valid, hid, halo, tail, gain, wi, wp, ws, conv_i, conv_p, bias_i, bias_p,
    low, low_t, in_i, in_p, pre_i, pre_p, aux, halo_low, halo_i, halo_p, sloc, pkl, fin, wide_i, wide_p, state, decay, counted,
):
    step = pl.program_id(0)
    edge = tail.shape[0]
    width = wi.shape[1]

    @pl.when(step == 0)
    def _():
        state[...] = jnp.zeros_like(state)
        decay[...] = jnp.ones_like(decay)
        counted[...] = jnp.zeros_like(counted)

    counted[...] += jnp.sum(valid[...].astype(F32), axis=1, keepdims=True)
    before = jnp.where(step == 0, tail[...].astype(F32), halo[...].astype(F32))
    rows = jnp.concatenate([before, hid[...].astype(F32)], axis=0)
    scale = lax.rsqrt(jnp.mean(rows * rows, axis=1, keepdims=True) + EPSILON)
    lowered = (rows * scale * gain[...]).astype(BF16)
    own = lowered[edge:]
    low[...] = own
    low_t[...] = jnp.transpose(own)
    inner = dot(lowered, wi[...]).astype(BF16)
    pair = dot(lowered, wp[...]).astype(BF16)
    in_i[...] = inner[edge:]
    in_p[...] = pair[edge:]
    wide_i[...] = inner.astype(F32)
    wide_p[...] = pair.astype(F32)

    @pl.when(step == 0)
    def _():
        halo_low[...] = lowered[:edge]
        halo_i[...] = inner[:edge]
        halo_p[...] = pair[:edge]

    base = idx[1] + step * BLOCK
    pos = (base + lax.broadcasted_iota(jnp.int32, (BLOCK, LANES), 0)).astype(F32)
    starts = given[3:4]
    begun = starts <= pos
    start = jnp.max(jnp.where(begun, starts, -1.0), axis=1, keepdims=True)
    end = jnp.min(jnp.where(begun, FAR, starts), axis=1, keepdims=True)
    within = pos[:, :1] - start
    keep = [(within >= float(3 - k)).astype(F32) for k in range(3)]

    def convolve(wide, weight, bias):
        taps = weight[...].astype(F32)
        total = bias[...].astype(F32) + wide[edge : edge + BLOCK] * taps[3:4]
        for k in range(3):
            total = total + wide[edge - 3 + k : edge - 3 + k + BLOCK] * taps[k : k + 1] * keep[k]
        return total

    conv_inner = convolve(wide_i, conv_i, bias_i)
    conv_pair = convolve(wide_p, conv_p, bias_p)
    pre_i[...] = conv_inner
    pre_p[...] = conv_pair
    values = conv_inner * jax.nn.sigmoid(conv_inner)
    maps = conv_pair[:, :LANES]
    maps = maps * jax.nn.sigmoid(maps)

    raw = dot(own, ws[...]) + given[0:1]
    dt = jnp.maximum(raw, 0.0) + jnp.log1p(jnp.exp(-jnp.abs(raw)))
    rate = jax.nn.sigmoid(raw)
    logs = -dt * jnp.exp(given[1:2])
    lane = lax.broadcasted_iota(jnp.int32, (CHUNK, LANES), 1)
    lower = triangle(False)
    for c in range(BLOCK // CHUNK):
        at = slice(c * CHUNK, (c + 1) * CHUNK)
        cum = triangle_sums(lower, logs[at])
        last = cum[CHUNK - 1 :]
        first = (base + c * CHUNK).astype(F32)
        inflow = jnp.exp(cum) * (start[at] <= first - 1.0).astype(F32)
        outflow = jnp.exp(last - cum) * (end[at] > first + (CHUNK - 1.0)).astype(F32)
        table = jnp.where(lane < CUM, dt[at], pltpu.roll(cum, CUM, 1))
        table = jnp.where(lane < INFLOW, table, pltpu.roll(inflow, INFLOW, 1))
        table = jnp.where(lane < TAIL, table, pltpu.roll(outflow, TAIL, 1))
        table = jnp.where(lane < RATE, table, pltpu.roll(rate[at], RATE, 1))
        table = jnp.where(lane < START, table, jnp.where(lane < END, start[at], end[at]))
        aux[at, :] = table
        scaled = values[at] * expand(dt[at] * outflow, 0, width)
        added = dot3(maps[at], scaled, 0, 0)
        kept = expand(jnp.broadcast_to(inflow[CHUNK - 1 :], (8, LANES)), 0, width)
        sloc[c] = state[...]
        pkl[c] = decay[...]
        state[...] = state[...] * kept[:1] + added
        decay[...] = decay[...] * kept
    fin[:CHUNK] = state[...]
    fin[CHUNK:] = jnp.concatenate([decay[:7], jnp.broadcast_to(counted[...], (1, width))], axis=0)


def masks(table, first, transposed):
    row = lax.broadcasted_iota(jnp.int32, (CHUNK, CHUNK), 0)
    col = lax.broadcasted_iota(jnp.int32, (CHUNK, CHUNK), 1)
    at = (first + col).astype(F32)
    if transposed:
        return (col >= row) & (at < table[:, END : END + 1])
    return (col <= row) & (at >= table[:, START : START + 1])


def head_split(v, pair):
    lane = lax.broadcasted_iota(jnp.int32, (v.shape[0], LANES), 1)
    part = v[:, pair * LANES : (pair + 1) * LANES]
    return jnp.concatenate(
        [jnp.where(lane < HEAD_DIM, part, 0.0), jnp.where(lane < HEAD_DIM, 0.0, part)], axis=0
    ).astype(BF16)


def intra_kernel(idx, low, wg, pre_i, pre_p, aux, given, gate, mixed):
    width = wg.shape[1]
    skip = expand(given[...], 0, width)[2:3]
    gate[...] = dot(low[...], wg[...])
    base = idx[1] + pl.program_id(0) * BLOCK
    maps, _ = silu_parts(pre_p[...])
    values, _ = silu_parts(pre_i[...])
    for c in range(BLOCK // CHUNK):
        at = slice(c * CHUNK, (c + 1) * CHUNK)
        table = aux[at, :]
        rows = jnp.transpose(table)
        joined = masks(table, base + c * CHUNK, False)
        scores = dot(maps[at, LANES:].astype(BF16), maps[at, :LANES].astype(BF16), 1, 1)
        scaled = values[at] * expand(table, DT, width)
        parts = []
        for pair in range(width // LANES):
            weights = []
            for h in (2 * pair, 2 * pair + 1):
                gap = table[:, CUM + h : CUM + h + 1] - rows[CUM + h : CUM + h + 1, :]
                weights.append((scores * jnp.exp(jnp.where(joined, gap, -1e30))).astype(BF16))
            parts.append(dot(jnp.concatenate(weights, axis=1), head_split(scaled, pair)))
        mixed[at, :] = jnp.concatenate(parts, axis=1) + values[at] * skip


def core_bit():
    return lax.rem(lax.axis_index("head"), 2)


def core_peer():
    return lax.axis_index("head") + 1 - 2 * core_bit()


def mid_kernel(
    factor, pre_c, aux, sloc, pkl, sin, local, gate, gain, wo, hid, teacher, valid,
    states, d_mixer, d_gate, gloc, pkb, fin, out, d_out, error, g_gain, g_wo,
    mix, squares, square_land, crosses, cross_land, scales, parts, land, mine, other, d_branch, out_block, weighted, keeps,
    state, wo_t, square_send, square_got, cross_send, cross_got, core_send, core_land, x_send, x_land, grad_send, grad_land,
    out_local, out_send, out_land, *, total,
):
    step = pl.program_id(0)
    half = mine.shape[0]
    blocks = 2 * half
    width = local.shape[1]
    head, core = lax.axis_index("head"), core_bit()
    beside, across = {"head": core_peer()}, {"head": lax.rem(head + 2, 4)}

    def to_head(distance):
        return {"head": lax.rem(head + distance, 4)}

    def square_copy(block, d):
        return device_copy(squares.at[block], square_land.at[d, block], (square_send, square_got), 4 * block + d, to_head(d))

    def cross_copy(block, d):
        return device_copy(crosses.at[block], cross_land.at[d, block], (cross_send, cross_got), 4 * block + d, to_head(d))

    def core_copy(slot):
        return device_copy(parts.at[slot], land.at[slot], (core_send, core_land), slot, beside)

    def x_copy(slot):
        return device_copy(mine.at[slot], other.at[slot], (x_send, x_land), slot, across)

    def grad_copy(block):
        return device_copy(d_branch.at[block], d_branch.at[block], (grad_send, grad_land), block, beside)

    def out_copies(slot):
        rows = rows_at(out, core * half + slot, BLOCK)
        here = pltpu.make_async_copy(out_block.at[slot], rows, out_local.at[slot])
        return here, device_copy(out_block.at[slot], rows, (out_send, out_land), slot, beside)

    def gate_rows(block):
        return gate[pl.ds(pl.multiple_of(block * BLOCK, BLOCK), BLOCK), :]

    def settle(slot):
        core_copy(slot).wait_recv()
        mine[slot] = (parts[slot] + land[slot]).astype(BF16)
        x_copy(slot).start()

    @pl.when(step == 0)
    def _():
        barrier = pltpu.get_barrier_semaphore()

        def greet(d):
            pl.semaphore_signal(barrier, inc=1, device_id=to_head(d), device_id_type=pl.DeviceIdType.MESH)

        loop(1, 4, greet)
        for ref in (error, g_gain, g_wo):
            ref[...] = jnp.zeros_like(ref)
        wo_t[...] = jnp.transpose(wo[...])
        pl.semaphore_wait(barrier, 3)

    @pl.when(step < blocks)
    def _():
        reads, _ = silu_parts(pre_c[...])
        for c in range(BLOCK // CHUNK):
            at = slice(c * CHUNK, (c + 1) * CHUNK)
            now = sloc[c] + pkl[c, :1] * sin[...]
            states[c] = now
            mix[step, at, :] = local[at, :] + expand(aux[at, :], INFLOW, width) * dot3(reads[at], now)
        act, _ = silu_parts(gate_rows(step))
        gated = mix[step] * act
        squares[step] = column_sums(gated * gated)
        loop(1, 4, lambda d: square_copy(step, d).start())

    @pl.when((step > blocks) & (step <= 2 * blocks) & ((step - blocks - 1) // half == core))
    def _():
        settle(lax.rem(step - blocks - 1, half))

    @pl.when((step >= blocks) & (step < 2 * blocks))
    def _():
        block = step - blocks
        slot = lax.rem(block, half)
        own = block // half == core

        def add(d, sum_row):
            square_copy(block, d).wait_recv()
            return sum_row + square_land[d, block]

        row = lax.rsqrt(lax.fori_loop(1, 4, add, squares[block]) / total + EPSILON)
        scales[block] = row
        act, _ = silu_parts(gate_rows(block))
        normed = (mix[block] * act * as_column(row, width) * gain[...]).astype(BF16)

        @pl.when(own & (core == 1))
        def _():
            core_copy(slot).wait_send()

        parts[slot] = dot(normed, wo[...])

        @pl.when(jnp.logical_not(own))
        def _():
            core_copy(slot).start()

    @pl.when((step >= 2 * blocks) & (step < 3 * blocks))
    def _():
        block = step - 2 * blocks
        slot = lax.rem(block, half)
        own = block // half == core

        @pl.when(own)
        def _():
            x_copy(slot).wait_recv()
            at = pl.ds(pl.multiple_of(slot * BLOCK, BLOCK), BLOCK)
            outf = hid[at, :].astype(F32) + (mine[slot].astype(F32) + other[slot].astype(F32))
            term = outf - teacher[at, :].astype(F32)
            masked = as_column(valid[...].astype(F32), term.shape[1]) * term
            error[...] += jnp.sum(masked * term, axis=0, keepdims=True)
            grad = masked * factor[0]
            d_out[...] = grad
            d_branch[block] = grad.astype(BF16)
            grad_copy(block).start()
            out_block[slot] = outf.astype(BF16)
            for copy in out_copies(slot):
                copy.start()

        @pl.when(jnp.logical_not(own))
        def _():
            grad_copy(block).wait_recv()

        act, _ = silu_parts(gate_rows(block))
        gated = mix[block] * act
        scaled = gated * as_column(scales[block], width)
        normed = (scaled * gain[...]).astype(BF16)
        grads = d_branch[block]
        g_wo[...] += dot(normed, grads, 0, 0)
        d_normed = dot(grads, wo_t[...])
        g_gain[...] += jnp.sum(d_normed * scaled, axis=0, keepdims=True)
        pulled = d_normed * gain[...]
        weighted[lax.rem(block, 2)] = pulled
        crosses[block] = column_sums(pulled * gated)
        loop(1, 4, lambda d: cross_copy(block, d).start())

    @pl.when(step > 2 * blocks)
    def _():
        block = step - 2 * blocks - 1

        def add(d, sum_row):
            cross_copy(block, d).wait_recv()
            return sum_row + cross_land[d, block]

        cross = lax.fori_loop(1, 4, add, crosses[block])
        act, slope = silu_parts(gate_rows(block))
        gated = mix[block] * act
        row = scales[block]
        pull = as_column(row * row * row * cross / total, width)
        d_gated = as_column(row, width) * weighted[lax.rem(block, 2)] - gated * pull
        dy = d_gated * act
        d_mixer[...] = dy
        d_gate[...] = (d_gated * mix[block] * slope).astype(BF16)
        reads, _ = silu_parts(pre_c[...])
        for c in range(BLOCK // CHUNK):
            at = slice(c * CHUNK, (c + 1) * CHUNK)
            inflow = expand(aux[at, :], INFLOW, width)
            keeps[block * (BLOCK // CHUNK) + c] = jnp.broadcast_to(inflow[CHUNK - 1 :], (8, width))
            gloc[block * (BLOCK // CHUNK) + c] = dot3(reads[at], dy[at] * inflow, 0, 0)

    @pl.when(step == 3 * blocks)
    def _():
        state[...] = jnp.zeros_like(state)
        chunks = gloc.shape[0]

        def back(i, decay):
            c = chunks - 1 - i
            added = gloc[c]
            gloc[c] = state[...]
            pkb[c] = decay
            state[...] = state[...] * keeps[c, :1] + added
            return decay * keeps[c]

        decay = lax.fori_loop(0, chunks, back, jnp.ones((8, width), F32))
        fin[:CHUNK] = state[...]
        fin[CHUNK:] = decay

        def drain(block):
            def both(d):
                square_copy(block, d).wait_send()
                cross_copy(block, d).wait_send()

            loop(1, 4, both)

            @pl.when(block // half == core)
            def _():
                grad_copy(block).wait_send()

        loop(0, blocks, drain)

        @pl.when(core == 0)
        def _():
            loop(0, half, lambda slot: core_copy(slot).wait_send())

        def finish(slot):
            x_copy(slot).wait_send()
            here, there = out_copies(slot)
            here.wait()
            there.wait()

        loop(0, half, finish)


def intra_back_kernel(idx, d_mixer, pre_i, pre_p, aux, low_t, d_gate, d_scaled, d_maps, g_wg):
    @pl.when(pl.program_id(0) == 0)
    def _():
        g_wg[...] = jnp.zeros_like(g_wg)

    g_wg[...] += dot(low_t[...], d_gate[...])
    width = d_mixer.shape[1]
    base = idx[1] + pl.program_id(0) * BLOCK
    maps, _ = silu_parts(pre_p[...])
    values, _ = silu_parts(pre_i[...])
    for c in range(BLOCK // CHUNK):
        at = slice(c * CHUNK, (c + 1) * CHUNK)
        table = aux[at, :]
        rows = jnp.transpose(table)
        joined = masks(table, base + c * CHUNK, True)
        keys = maps[at, :LANES].astype(BF16)
        reads = maps[at, LANES:].astype(BF16)
        scores = dot(keys, reads, 1, 1)
        scaled = (values[at] * expand(table, DT, width)).astype(BF16)
        grads = d_mixer[at, :]
        d_scores = jnp.zeros((CHUNK, CHUNK), F32)
        parts = []
        for pair in range(width // LANES):
            split = head_split(grads, pair)
            d_weights = dot(scaled[:, pair * LANES : (pair + 1) * LANES], split, 1, 1)
            weights = []
            for side in range(2):
                h = 2 * pair + side
                gap = rows[CUM + h : CUM + h + 1, :] - table[:, CUM + h : CUM + h + 1]
                factor = jnp.exp(jnp.where(joined, gap, -1e30))
                weights.append((scores * factor).astype(BF16))
                d_scores = d_scores + factor * d_weights[:, side * CHUNK : (side + 1) * CHUNK]
            parts.append(dot(jnp.concatenate(weights, axis=1), split))
        d_scaled[at, :] = jnp.concatenate(parts, axis=1)
        low_scores = d_scores.astype(BF16)
        d_maps[at, :] = jnp.concatenate([dot(low_scores, reads), dot(low_scores, keys, 0, 0)], axis=1)


def conv_back(grad, within, inputs, edge_inputs, weight, shifted, first, last, acc):
    rows = grad.shape[0]

    @pl.when(first)
    def _():
        for ref in shifted:
            ref[...] = jnp.zeros_like(ref)

    weight = weight[...].astype(F32)
    total = grad * weight[3:4]
    edge = jnp.zeros((8, grad.shape[1]), F32)
    acc[3:4] += jnp.sum(grad * inputs, axis=0, keepdims=True)
    acc[4:5] += jnp.sum(grad, axis=0, keepdims=True)
    for k, ref in enumerate(shifted):
        ref[8 : 8 + rows] = grad * (within >= float(3 - k)).astype(F32)
        moved = ref[3 - k : 3 - k + 8 + rows]
        total = total + moved[8:] * weight[k : k + 1]
        edge = edge + moved[:8] * weight[k : k + 1]
        outer = jnp.where(last, edge_inputs, 0.0) * moved[:8]
        acc[k : k + 1] += jnp.sum(moved[8:] * inputs, axis=0, keepdims=True) + jnp.sum(outer, axis=0, keepdims=True)
        ref[8 + rows :] = ref[8:16]
    return total, edge


def device_copy(src, dst, sems, slot, to):
    return pltpu.make_async_remote_copy(
        src_ref=src, dst_ref=dst, send_sem=sems[0].at[slot], recv_sem=sems[1].at[slot],
        device_id=to, device_id_type=pl.DeviceIdType.MESH,
    )


def loop(start, stop, body):
    def run(d, carry):
        body(d)
        return carry

    lax.fori_loop(start, stop, run, 0)


def rows_at(ref, index, size):
    return ref.at[pl.ds(pl.multiple_of(index * size, size), size)]


class SeqSum:
    def __init__(self, source, first, land1, second, land2, done, sems):
        self.source, self.first, self.land1, self.second, self.land2, self.done = source, first, land1, second, land2, done
        self.sems = [sems[i : i + 2] for i in range(0, 8, 2)]
        self.wire = first.dtype
        self.members = land2.shape[0]
        self.piece = first.shape[0] // self.members
        me = lax.axis_index("seq")
        self.side, self.place = lax.rem(me, 2), me // 2
        self.partner = {"seq": me + 1 - 2 * self.side}

    def half(self, ref, side):
        return rows_at(ref, side, self.members * self.piece)

    def member(self, d):
        return lax.rem(self.place + d, self.members)

    def to_member(self, d):
        return {"seq": 2 * self.member(d) + self.side}

    def halve(self):
        return device_copy(self.first, self.land1, self.sems[0], 0, self.partner)

    def scatter(self, d):
        src = rows_at(self.second, self.member(d), self.piece)
        return device_copy(src, self.land2.at[d], self.sems[1], d, self.to_member(d))

    def part(self, place):
        return rows_at(self.done, self.side * self.members + place, self.piece)

    def gather(self, d):
        ref = self.part(self.place)
        return device_copy(ref, ref, self.sems[2], d, self.to_member(d))

    def gathered(self, d):
        ref = self.part(lax.rem(self.place + self.members - d, self.members))
        return device_copy(ref, ref, self.sems[2], d, self.partner)

    def widen(self, side):
        ref = self.half(self.done, side)
        return device_copy(ref, ref, self.sems[3], 0, self.partner)

    def begin(self):
        self.first[...] = self.half(self.source, 1 - self.side)[...].astype(self.wire)
        self.halve().start()

    def pass_on(self):
        self.halve().wait_recv()
        self.second[...] = (self.half(self.source, self.side)[...] + self.land1[...].astype(F32)).astype(self.wire)
        loop(1, self.members, lambda d: self.scatter(d).start())

    def finish(self):
        own = rows_at(self.source, self.side * self.members + self.place, self.piece)[...]
        own = own + rows_at(self.land1, self.place, self.piece)[...].astype(F32)

        def add(d, total):
            self.scatter(d).wait_recv()
            return total + self.land2[d].astype(F32)

        self.part(self.place)[...] = lax.fori_loop(1, self.members, add, own).astype(self.wire)
        loop(1, self.members, lambda d: self.gather(d).start())

    def collect(self):
        loop(1, self.members, lambda d: self.gathered(d).wait_recv())
        self.widen(self.side).start()

    def store(self, out):
        self.half(out, self.side)[...] = self.half(self.done, self.side)[...].astype(F32)
        self.widen(1 - self.side).wait_recv()
        self.half(out, 1 - self.side)[...] = self.half(self.done, 1 - self.side)[...].astype(F32)

    def drain(self):
        self.halve().wait_send()
        self.widen(self.side).wait_send()

        def both(d):
            self.scatter(d).wait_send()
            self.gather(d).wait_send()

        loop(1, self.members, both)

    @staticmethod
    def scratch(rows, lanes, wire, size):
        members = size // 2
        half = pltpu.VMEM((members * rows, lanes), wire)
        dma = pltpu.SemaphoreType.DMA
        return [half, half, half, pltpu.VMEM((members, rows, lanes), wire), pltpu.VMEM((2 * members * rows, lanes), wire)] + [
            dma((1,)), dma((1,)), dma((members,)), dma((members,)), dma((members,)), dma((members,)), dma((1,)), dma((1,)),
        ]


SUM_REFS = 13


class HeadSum:
    def __init__(self, source, out, fold1, half, fold2, quarter, sems):
        self.source, self.out, self.fold1, self.held, self.fold2, self.quarter = source, out, fold1, half, fold2, quarter
        self.sems = [sems[i : i + 2] for i in range(0, 8, 2)]
        self.rows = source.shape[0]
        head = lax.axis_index("head")
        self.core, self.plane = lax.rem(head, 2), head // 2
        self.beside, self.across = {"head": head + 1 - 2 * self.core}, {"head": head + 2 - 4 * self.plane}

    def fold_core(self):
        return device_copy(rows_at(self.source, 1 - self.core, self.rows // 2), self.fold1, self.sems[0], 0, self.beside)

    def fold_plane(self):
        return device_copy(rows_at(self.held, 1 - self.plane, self.rows // 4), self.fold2, self.sems[1], 0, self.across)

    def spread_plane(self, plane):
        ref = rows_at(self.out, 2 * self.core + plane, self.rows // 4)
        return device_copy(ref, ref, self.sems[2], 0, self.across)

    def spread_core(self, core):
        ref = rows_at(self.out, core, self.rows // 2)
        return device_copy(ref, ref, self.sems[3], 0, self.beside)

    def fold(self):
        self.fold_core().wait_recv()
        self.held[...] = rows_at(self.source, self.core, self.rows // 2)[...] + self.fold1[...]
        self.fold_plane().start()

    def settle(self):
        self.fold_plane().wait_recv()
        self.quarter[...] = jnp.zeros_like(self.quarter)
        self.quarter[: self.rows // 4] = rows_at(self.held, self.plane, self.rows // 4)[...] + self.fold2[...]

    def spread(self, total):
        rows_at(self.out, 2 * self.core + self.plane, self.rows // 4)[...] = total[: self.rows // 4]
        self.spread_plane(self.plane).start()

    def spread_more(self):
        self.spread_plane(1 - self.plane).wait_recv()
        self.spread_core(self.core).start()

    def finish(self):
        self.spread_core(1 - self.core).wait_recv()
        self.fold_core().wait_send()
        self.fold_plane().wait_send()
        self.spread_plane(self.plane).wait_send()
        self.spread_core(self.core).wait_send()

    @staticmethod
    def scratch(rows, lanes, padded_rows):
        dma = pltpu.SemaphoreType.DMA
        shapes = [(rows // 2, lanes), (rows // 2, lanes), (rows // 4, lanes), (padded_rows, lanes)]
        return [pltpu.VMEM(shape, F32) for shape in shapes] + [dma((1,))] * 8


HEAD_REFS = 12


def finale_kernel(
    d_scaled, d_maps, pre_i, pre_p, in_i, in_p, halo_low, halo_i, halo_p, aux, gloc, pkl, gin, states, d_mixer, mixer, given,
    conv_i, conv_p, low_t, d_gate, wg, wi, ws, wp, hid, d_out, gain, error, g_wo, g_wg, g_gain, factor,
    grad_all, out_norm, out_loss, out_wo, out_wg, out_wi, out_wp, out_ws, out_conv_i, out_bias_i, out_conv_p, out_bias_p,
    out_sbias, out_dlog, out_skip, out_gain,
    shift_i0, shift_i1, shift_i2, shift_p0, shift_p1, shift_p2, small, small_p, heads,
    parts, land, mine, other, row, row_land, g_wi, g_ws, pack, g_wp, pair_small, sum_small, sum_wp, sum_pack, spread_wp, spread_small,
    grad_own, grad_other, w_t, edge, edge_core, edge_plane, edge_ahead,
    core_send, core_land, x_send, x_land, edge_send, edge_land, grad_send, grad_land, row_send, row_arrive, *more,
):
    shifted = (shift_i0, shift_i1, shift_i2, shift_p0, shift_p1, shift_p2)
    step = pl.program_id(0)
    blocks = pl.num_programs(0)
    half = blocks // 2
    first, last = step == 0, step == blocks - 1
    seq, devices = lax.axis_index("seq"), lax.axis_size("seq")
    head, core = lax.axis_index("head"), core_bit()
    width = wi.shape[1]
    model = low_t.shape[0]
    behind, ahead = lax.rem(seq + devices - 1, devices), lax.rem(seq + 1, devices)
    group = 2 * devices
    me = 2 * seq + core
    beside, across = {"head": core_peer()}, {"head": lax.rem(head + 2, 4)}
    summing = len(more) > 0

    more = list(more)

    def take(number):
        taken = more[:number]
        del more[:number]
        return taken

    seq_sums, wide = [], []
    if summing:
        head_parts = []
        for source, out in ((g_wp, spread_wp), (pair_small, spread_small)):
            refs = take(HEAD_REFS)
            head_parts.append(HeadSum(source, out, *refs[:4], refs[4:]))
        third = model // 3
        thirds = [g_wi.at[pl.ds(i * third, third)] for i in range(3)]
        outs_wi = [out_wi.at[pl.ds(i * third, third)] for i in range(3)]
        for source in (g_wo, g_wg, *thirds, pack, head_parts[0].quarter, head_parts[1].quarter):
            refs = take(SUM_REFS)
            seq_sums.append(SeqSum(source, *refs[:5], refs[5:]))
        s_wo, s_wg, *s_wi, s_pack, s_wp, s_small = seq_sums
        wide = list(zip(head_parts, (s_wp, s_small), (sum_wp, sum_small)))

    def device(distance):
        to = lax.rem(me + distance, group)
        return {"seq": to // 2, "head": head - core + lax.rem(to, 2)}

    def hand(distance):
        return device_copy(row, row_land.at[me], (row_send, row_arrive), distance, device(distance))

    def edge_copy(slot, landing, to):
        return device_copy(edge.at[slot], landing, (edge_send, edge_land), slot, to)

    def core_copy(slot):
        return device_copy(parts.at[slot], land.at[slot], (core_send, core_land), slot, beside)

    def x_copy(slot):
        return device_copy(mine.at[slot], other.at[slot], (x_send, x_land), slot, across)

    def grad_copy(slot):
        return device_copy(grad_own.at[slot], grad_other.at[slot], (grad_send, grad_land), slot, beside)

    @pl.when(first)
    def _():
        barrier = pltpu.get_barrier_semaphore()

        def greet(to):
            pl.semaphore_signal(barrier, inc=1, device_id=to, device_id_type=pl.DeviceIdType.MESH)

        loop(1, group, lambda d: greet(device(d)))
        greet(across)
        for ref in (g_wi, g_ws, pack, g_wp, pair_small, small, small_p, heads):
            ref[...] = jnp.zeros_like(ref)
        row[:1] = jnp.zeros_like(row[:1])
        row[1:] = error[...]
        filled = 0
        for weight in (wg, wi, ws, wp, wp):
            w_t[filled : filled + weight.shape[1]] = jnp.transpose(weight[...])
            filled += weight.shape[1]
        pl.semaphore_wait(barrier, group)
        if summing:
            s_wo.begin()
            s_wg.begin()

    base = seq * (blocks * BLOCK) + (blocks - 1 - step) * BLOCK
    maps, slope_p = silu_parts(pre_p[...])
    values, slope = silu_parts(pre_i[...])
    dy = d_mixer[...]
    upper = triangle(True)
    lane = lax.broadcasted_iota(jnp.int32, (CHUNK, LANES), 1)
    grown = jnp.exp(given[1:2])
    skip = expand(given[...], 0, width)[2:3]
    pieces, pieces_p, pieces_s = [], [], []
    for c in range(BLOCK // CHUNK):
        at = slice(c * CHUNK, (c + 1) * CHUNK)
        table = aux[at, :]
        sizes = expand(table, DT, width)
        inflow = expand(table, INFLOW, width)
        outflow = expand(table, TAIL, width)
        keys, reads = maps[at, :LANES], maps[at, LANES:]
        scaled = values[at] * sizes
        grad_state = gloc[c] + pkl[c, :1] * gin[...]
        state = states[c]
        passed = outflow * dot3(keys, grad_state)
        total = d_scaled[at, :] + passed
        d_reads = d_maps[at, LANES:] + dot3(dy[at] * inflow, state, 1, 1)
        d_keys = d_maps[at, :LANES] + dot3(scaled * outflow, grad_state, 1, 1)
        pieces_p.append(jnp.concatenate([d_keys, d_reads], axis=1))
        plain = mixer[at, :] - skip * values[at]
        d_cum = head_sums(dy[at] * plain - scaled * total)
        carried = jnp.sum(grad_state * state, axis=0, keepdims=True) * inflow[CHUNK - 1 :]
        carried = carried + jnp.sum(scaled * passed, axis=0, keepdims=True)
        after = head_sums(jnp.broadcast_to(carried, (8, width)))[:1]
        d_logs = triangle_sums(upper, d_cum) + after
        d_raw = (head_sums(total * values[at]) - grown * d_logs) * pltpu.roll(table, LANES - RATE, 1)
        d_raw = jnp.where(lane < 8, d_raw, 0.0)
        pieces_s.append(d_raw.astype(BF16))
        d_decay = jnp.where(lane < 8, -d_logs * table * grown, 0.0)
        heads[0:1] += jnp.sum(d_raw, axis=0, keepdims=True)
        heads[1:2] += jnp.sum(d_decay, axis=0, keepdims=True)
        pieces.append(total * sizes + dy[at] * skip)
    small[5:6] += jnp.sum(dy * values, axis=0, keepdims=True)
    grad = jnp.concatenate(pieces, axis=0) * slope
    pos = (base + lax.broadcasted_iota(jnp.int32, (BLOCK, 1), 0)).astype(F32)
    within = pos - aux[:, START : START + 1]
    whole, outer = conv_back(
        grad, within, in_i[...].astype(F32), halo_i[8:].astype(F32), conv_i, shifted[:3], first, last, small
    )
    grad_p = jnp.concatenate(pieces_p, axis=0) * slope_p
    whole_p, outer_p = conv_back(
        grad_p, within, in_p[...].astype(F32), halo_p[8:].astype(F32), conv_p, shifted[3:], first, last, small_p
    )

    inner = whole.astype(BF16)
    d_step = jnp.concatenate(pieces_s, axis=0)
    high, rest = halves(whole_p)
    part = dot(jnp.concatenate([d_gate[...], inner, d_step, high, rest], axis=1), w_t[...])
    upper = (step < half).astype(jnp.int32)
    slot = half - 1 - lax.rem(step, half)
    own = upper == core

    def settle(at):
        core_copy(at).wait_recv()
        mine[at] = (parts[at].astype(F32) + land[at].astype(F32)).astype(BF16)
        x_copy(at).start()

    @pl.when((step > 0) & ((step - 1 < half).astype(jnp.int32) == core))
    def _():
        settle(half - 1 - lax.rem(step - 1, half))

    @pl.when((step >= half) & (core == 0))
    def _():
        core_copy(slot).wait_send()

    parts[slot] = part.astype(parts.dtype)

    @pl.when(jnp.logical_not(own))
    def _():
        core_copy(slot).start()

    products = dot(low_t[...], jnp.concatenate([inner, d_step, high, rest], axis=1))
    g_wi[:model] += products[:, :width]
    g_ws[...] += products[:, width : width + LANES]
    to_pair = products[:, width + LANES :]
    g_wp[...] += to_pair[:, : to_pair.shape[1] // 2] + to_pair[:, to_pair.shape[1] // 2 :]

    def norm_back(at):
        x_copy(at).wait_recv()
        block_rows = pl.ds(at * BLOCK, BLOCK)
        d_low = mine[at].astype(F32) + other[at].astype(F32)
        if at == half - 1:
            edge_copy(2, edge_ahead, {"seq": behind}).wait_recv()
            there = ((core == 1) & (seq < devices - 1)).astype(F32)
            d_low = jnp.concatenate([d_low[: BLOCK - 8], d_low[BLOCK - 8 :] + there * edge_ahead[...]], axis=0)
        rows = hid[block_rows, :].astype(F32)
        scale = lax.rsqrt(jnp.mean(rows * rows, axis=1, keepdims=True) + EPSILON)
        row[:1] += jnp.sum(d_low * rows * scale, axis=0, keepdims=True)
        scaled = d_low * gain[...]
        pull = jnp.mean(scaled * rows, axis=1, keepdims=True) * (scale * scale * scale)
        block = (d_out[block_rows, :] + scale * scaled - rows * pull).astype(BF16)
        grad_own[at] = block
        grad_copy(at).start()
        rows_at(grad_all, core * half + at, BLOCK)[...] = block

    if summing:

        moves = (s_wo.pass_on, s_wg.pass_on, s_wo.finish, s_wg.finish, s_wo.collect)
        for number, move in enumerate(moves):

            @pl.when(step == number + 2)
            def _(move=move):
                move()

    @pl.when(last)
    def _():
        before = jnp.concatenate([jnp.zeros_like(outer), outer], axis=0).astype(BF16)
        g_wi[:model] += dot(halo_low[...], before, 0, 0)
        before_p = jnp.concatenate([jnp.zeros_like(outer_p), outer_p], axis=0)
        high_p, rest_p = halves(before_p)
        g_wp[...] += dot(halo_low[...], high_p, 0, 0) + dot(halo_low[...], rest_p, 0, 0)
        edge_in = jnp.concatenate([before, jnp.zeros((16, LANES), BF16), high_p, rest_p], axis=1)
        edge_part = dot(edge_in, w_t[width:])
        edge[0] = edge_part[8:]
        edge_copy(0, edge_core, beside).start()
        pack[:6] = small[:6]
        pack[6:7] = g_gain[...]
        step_rows = jnp.transpose(g_ws[...])[:8]
        pack[8:16] = step_rows[:, :width]
        pack[16:24] = step_rows[:, width:]
        pack[24:32, : heads.shape[1]] = heads[...]
        pair_small[:8] = small_p[...]
        if summing:
            for h_sum, _, _ in wide:
                h_sum.fold_core().start()
            s_wi[0].begin()
            s_wi[1].begin()

        if summing:
            for h_sum, _, _ in wide:
                h_sum.fold()

        @pl.when(core == 0)
        def _():
            settle(0)

        if summing:
            s_wi[2].begin()
            s_pack.begin()
        edge_copy(0, edge_core, beside).wait_recv()
        edge[1] = edge[0] + edge_core[...]
        edge_copy(1, edge_plane, across).start()
        if summing:
            s_wg.collect()
            s_wi[0].pass_on()
            s_wi[1].pass_on()
        edge_copy(1, edge_plane, across).wait_recv()
        edge[2] = edge[1] + edge_plane[...]
        edge_copy(2, edge_ahead, {"seq": behind}).start()
        for h_sum, s_sum, _ in wide:
            h_sum.settle()
            s_sum.begin()
        norm_back(2)
        norm_back(1)
        if summing:
            s_wi[2].pass_on()
            s_pack.pass_on()
            s_wi[0].finish()
        for _, s_sum, _ in wide:
            s_sum.pass_on()
        norm_back(0)
        norm_back(3)
        loop(1, group, lambda d: hand(d).start())
        if summing:
            s_wi[1].finish()
            s_wi[2].finish()
            s_pack.finish()
            for _, s_sum, _ in wide:
                s_sum.finish()
            s_wi[0].collect()
            s_wo.store(out_wo)
            s_wi[1].collect()
            s_wi[2].collect()
            for _, s_sum, _ in wide:
                s_sum.collect()
            s_pack.collect()
            s_wg.store(out_wg)
            for h_sum, s_sum, total in wide:
                s_sum.store(total)
                h_sum.spread(total)
            for s_sum, out in zip(s_wi, outs_wi):
                s_sum.store(out)
            for h_sum, _, _ in wide:
                h_sum.spread_more()
            s_pack.store(sum_pack)
            for h_sum, _, _ in wide:
                h_sum.finish()
            out_wp[...] = spread_wp[...]
            totals, pair_totals = sum_pack[:32], spread_small[:8]
            for s_sum in seq_sums:
                s_sum.drain()
        else:
            for out, ref in ((out_wo, g_wo), (out_wg, g_wg), (out_wi, g_wi), (out_wp, g_wp)):
                out[...] = ref[...]
            totals, pair_totals = pack[:32], pair_small[:8]
        heads_here = out_sbias.shape[1]
        out_conv_i[...] = totals[:4]
        out_bias_i[...] = totals[4:5]
        out_skip[...] = head_sums(totals[:8])[5:6, :heads_here]
        out_gain[...] = totals[6:7]
        out_ws[...] = jnp.transpose(jnp.concatenate([totals[8:16], totals[16:24]], axis=1))[:, :heads_here]
        out_sbias[...] = totals[24:25, :heads_here]
        out_dlog[...] = totals[25:26, :heads_here]
        out_conv_p[...] = pair_totals[:4]
        out_bias_p[...] = pair_totals[4:5]
        row_land[me] = row[...]
        loop(1, group, lambda d: hand(d).wait())
        both_rows = lax.fori_loop(1, group, lambda d, total: total + row_land[d], row_land[0])
        out_norm[...] = both_rows[:1]
        per_token = factor[0] / (group * half * BLOCK * model)
        out_loss[...] = jnp.sum(both_rows[1:], axis=1, keepdims=True) * per_token
        for at, to in enumerate((beside, across, {"seq": behind})):
            edge_copy(at, edge_core, to).wait_send()

        @pl.when(core == 1)
        def _():
            loop(0, half, lambda at: core_copy(at).wait_send())

        def drain(at):
            x_copy(at).wait_send()
            grad_copy(at).wait()
            rows_at(grad_all, (1 - core) * half + at, BLOCK)[...] = grad_other[at]

        loop(0, half, drain)


def call(kernel, grid, ins, outs, scratch=(), prefetch=0, flops=0, moved=0, collective=None, vmem=14):
    def spec(shape, block, index, **single):
        if block is None:
            return pl.BlockSpec(shape, lambda *_: (0,) * len(shape), **single)
        if isinstance(block, str):
            return pl.BlockSpec(memory_space={"smem": pltpu.SMEM, "vmem": pltpu.VMEM, "any": pl.ANY}[block])
        return pl.BlockSpec(block, index)

    scalars = [a for a, *_ in ins[:prefetch]]
    arrays = ins[prefetch:]
    extra = {} if collective is None else {"collective_id": collective, "has_side_effects": True}
    return pl.pallas_call(
        kernel,
        grid_spec=pltpu.PrefetchScalarGridSpec(
            num_scalar_prefetch=prefetch,
            grid=(grid,),
            in_specs=[spec(a.shape, block, index, pipeline_mode=pl.Buffered(1)) for a, block, index in arrays],
            out_specs=[spec(shape, block, index) for shape, _, block, index in outs],
            scratch_shapes=list(scratch),
        ),
        out_shape=[jax.ShapeDtypeStruct(shape, dtype) for shape, dtype, _, _ in outs],
        compiler_params=pltpu.CompilerParams(
            dimension_semantics=("arbitrary",), vmem_limit_bytes=vmem << 20, **extra
        ),
        cost_estimate=pl.CostEstimate(flops=int(flops), bytes_accessed=int(moved), transcendentals=0),
    )(*scalars, *[a for a, *_ in arrays])


def swap(value, axis, bit):
    route = [(i, i ^ bit) for i in range(lax.axis_size(axis))]
    return jax.tree.map(lambda v: lax.ppermute(v, axis, route), value)


def shifted(value, axis, distance):
    devices = range(lax.axis_size(axis))
    route = [(i - distance, i) for i in devices if i - distance in devices]
    return lax.ppermute(value, axis, route)


def bits(axis):
    size = lax.axis_size(axis)
    return [1 << b for b in range(size.bit_length() - 1)]


def total_over(value, axis):
    for bit in bits(axis):
        value = value + swap(value, axis, bit)
    return value


def carried(total, axis, backward):
    mine = lax.axis_index(axis)
    decays = slice(CHUNK, total.shape[0] - 1)

    def join(early, late):
        decay = late[CHUNK : CHUNK + 1]
        return jnp.concatenate([
            late[:CHUNK] + decay * early[:CHUNK], late[decays] * early[decays], late[-1:] + early[-1:],
        ])

    reached = jnp.concatenate([jnp.zeros_like(total[:CHUNK]), jnp.ones_like(total[CHUNK:])])
    for bit in bits(axis):
        other = swap(total, axis, bit)
        later = ((mine & bit) == 0) if backward else ((mine & bit) != 0)
        reached = jnp.where(later, join(other, reached), reached)
        total = jnp.where(later, join(other, total), join(total, other))
    return reached[:CHUNK], total[-1, 0]


def shards(
    hidden, teacher, doc_starts, valid_mask, norm_gain, w_gate, w_inner, w_pair, w_step, conv_inner, bias_inner,
    conv_pair, bias_pair, step_bias, decay_log, skip_gain, gate_gain, w_output,
):
    rows, model = hidden.shape
    width = w_inner.shape[1]
    pair_width = w_pair.shape[1]
    heads = step_bias.shape[0]
    blocks, chunks = rows // BLOCK, rows // CHUNK
    per = BLOCK // CHUNK
    half = blocks // 2
    inner_total = float(width * lax.axis_size("head"))
    core = lax.axis_index("head") & 1
    offset = lax.axis_index("seq") * rows
    idx = jnp.stack([core, offset]).astype(jnp.int32)
    edge_rows = 16

    given = jnp.stack([
        jnp.pad(step_bias, (0, LANES - heads)), jnp.pad(decay_log, (0, LANES - heads)), jnp.pad(skip_gain, (0, LANES - heads)),
        jnp.pad(doc_starts.astype(F32), (0, LANES - doc_starts.shape[0]), constant_values=FAR),
        *[jnp.zeros((LANES,), F32)] * 4,
    ])
    ws = jnp.pad(w_step, ((0, 0), (0, LANES - heads)))
    gain, out_gain = norm_gain[None, :], gate_gain[None, :]
    bias_i, bias_p = bias_inner[None, :], bias_pair[None, :]
    valid = valid_mask[None, :]

    tail = shifted(hidden[rows - edge_rows :], "seq", 1)

    def by(w, column=0):
        return (BLOCK, w), lambda i, *_: (i, column)

    def back(w, column=0):
        return (BLOCK, w), lambda i, *_: (blocks - 1 - i, column)

    grid3 = lambda n: ((per, n, width), lambda i, *_: (i, 0, 0))
    back3 = lambda n: ((per, n, width), lambda i, *_: (blocks - 1 - i, 0, 0))
    whole = (None, None)

    dma = pltpu.SemaphoreType.DMA

    halo_block = ((edge_rows, model), lambda i, *_: (jnp.maximum(i * (BLOCK // edge_rows) - 1, 0), 0))
    (low, low_t, in_i, in_p, pre_i, pre_p, aux, halo_low, halo_i, halo_p, sloc, pkl, fin) = call(
        project_kernel,
        blocks,
        [
            (idx, None, None), (given, *whole), (valid, (1, BLOCK), lambda i, *_: (0, i)), (hidden, *by(model)), (hidden, *halo_block), (tail, *whole),
            (gain, *whole), (w_inner, *whole), (w_pair, *whole), (ws, *whole), (conv_inner, *whole), (conv_pair, *whole),
            (bias_i, *whole), (bias_p, *whole),
        ],
        [
            ((rows, model), BF16, *by(model)), ((model, rows), BF16, (model, BLOCK), lambda i, *_: (0, i)),
            ((rows, width), BF16, *by(width)), ((rows, pair_width), BF16, *by(pair_width)),
            ((rows, width), F32, *by(width)), ((rows, pair_width), F32, *by(pair_width)), ((rows, LANES), F32, *by(LANES)),
            ((edge_rows, model), BF16, *whole), ((edge_rows, width), BF16, *whole), ((edge_rows, pair_width), BF16, *whole),
            ((chunks, CHUNK, width), F32, *grid3(CHUNK)), ((chunks, 8, width), F32, *grid3(8)),
            ((CHUNK + 8, width), F32, *whole),
        ],
        [
            pltpu.VMEM((BLOCK + edge_rows, width), F32), pltpu.VMEM((BLOCK + edge_rows, pair_width), F32),
            pltpu.VMEM((CHUNK, width), F32), pltpu.VMEM((8, width), F32), pltpu.VMEM((1, 1), F32),
        ],
        prefetch=1, flops=3e9, moved=2e7,
    )
    state_in, count = carried(fin, "seq", False)
    factor = (rows * lax.axis_size("seq")) / count
    gate, local = call(
        intra_kernel,
        blocks,
        [
            (idx, None, None), (low, *by(model)), (w_gate, *whole), (pre_i, *by(width)), (pre_p, *by(pair_width)),
            (aux, *by(LANES)), (given, *whole),
        ],
        [((rows, width), F32, *by(width)), ((rows, width), F32, *by(width))],
        prefetch=1, flops=4e9, moved=2e7,
    )
    size = lax.axis_size("seq")
    vmem = ("vmem", None)
    once = lambda w: ((rows // 2, w), lambda i: (core_bit(), 0))
    first_or_last = lambda i: jnp.where(i < blocks, i, jnp.clip(i - 2 * blocks - 1, 0, blocks - 1))
    early = lambda i: jnp.minimum(i, blocks - 1)
    late = lambda i: jnp.clip(i - 2 * blocks - 1, 0, blocks - 1)
    own_slot = lambda i: jnp.clip(i - 2 * blocks - half * core_bit(), 0, half - 1)
    early3 = lambda n: ((per, n, width), lambda i: (early(i), 0, 0))
    states, d_mixer, d_gate, gloc, pkb, fin_back, output, d_out, error, g_gain, g_wo, mixer = call(
        partial(mid_kernel, total=inner_total),
        3 * blocks + 1,
        [
            (factor.reshape(1), "smem", None), (pre_p, (BLOCK, LANES), lambda i: (first_or_last(i), 1)),
            (aux, (BLOCK, LANES), lambda i: (first_or_last(i), 0)), (sloc, *early3(CHUNK)), (pkl, *early3(8)), (state_in, *whole),
            (local, (BLOCK, width), lambda i: (early(i), 0)), (gate, *vmem), (out_gain, *whole), (w_output, *whole),
            (hidden, *once(model)), (teacher, *once(model)),
            (valid, (1, BLOCK), lambda i: (0, own_slot(i) + half * core_bit())),
        ],
        [
            ((chunks, CHUNK, width), F32, *early3(CHUNK)), ((rows, width), F32, (BLOCK, width), lambda i: (late(i), 0)),
            ((rows, width), BF16, (BLOCK, width), lambda i: (late(i), 0)), ((chunks, CHUNK, width), F32, *vmem),
            ((chunks, 8, width), F32, *vmem), ((CHUNK + 8, width), F32, *vmem), ((rows, model), BF16, "any", None),
            ((rows // 2, model), F32, (BLOCK, model), lambda i: (own_slot(i), 0)), ((1, model), F32, *whole),
            ((1, width), F32, *whole), ((width, model), F32, *whole), ((blocks, BLOCK, width), F32, *vmem),
        ],
        [
            pltpu.VMEM((blocks, 1, BLOCK), F32), pltpu.VMEM((4, blocks, 1, BLOCK), F32),
            pltpu.VMEM((blocks, 1, BLOCK), F32), pltpu.VMEM((4, blocks, 1, BLOCK), F32), pltpu.VMEM((blocks, 1, BLOCK), F32),
            pltpu.VMEM((half, BLOCK, model), F32), pltpu.VMEM((half, BLOCK, model), F32),
            pltpu.VMEM((half, BLOCK, model), BF16), pltpu.VMEM((half, BLOCK, model), BF16),
            pltpu.VMEM((blocks, BLOCK, model), BF16), pltpu.VMEM((half, BLOCK, model), BF16),
            pltpu.VMEM((2, BLOCK, width), F32), pltpu.VMEM((chunks, 8, width), F32), pltpu.VMEM((CHUNK, width), F32),
            pltpu.VMEM((model, width), BF16), dma((4 * blocks,)), dma((4 * blocks,)), dma((4 * blocks,)), dma((4 * blocks,)), dma((half,)), dma((half,)),
            dma((half,)), dma((half,)), dma((blocks,)), dma((blocks,)), dma((half,)), dma((half,)), dma((half,)),
        ],
        flops=6e9, moved=6e7, collective=2, vmem=36,
    )
    mixer = mixer.reshape(rows, width)
    grad_in, _ = carried(fin_back, "seq", True)
    d_scaled, d_maps, g_wg = call(
        intra_back_kernel,
        blocks,
        [
            (idx, None, None), (d_mixer, *by(width)), (pre_i, *by(width)), (pre_p, *by(pair_width)), (aux, *by(LANES)),
            (low_t, (model, BLOCK), lambda i, *_: (0, i)), (d_gate, *by(width)),
        ],
        [((rows, width), F32, *by(width)), ((rows, pair_width), F32, *by(pair_width)), ((model, width), F32, *whole)],
        prefetch=1, flops=6e9, moved=2e7,
    )
    summing = size <= 8

    def piece(total_rows, tile):
        return -(-total_rows // (size * tile)) * tile

    r_wo, r_w, r_pack, r_wp, r_small = piece(width, 16), piece(model, 16), 8, piece(model // 4, 8), 8
    core_wire = F32 if summing else BF16
    sum_shapes = [(r_wo, model, BF16), (r_w, width, BF16), *[(piece(model // 3, 16), width, BF16)] * 3, (r_pack, width, F32), (r_wp, pair_width, F32),
                  (r_small, pair_width, F32)]
    n_wo, n_w, n_pack = (r_wo * size, r_w * size, r_pack * size) if summing else (width, model, 64)
    scratch = [pltpu.VMEM((BLOCK + 16, width), F32)] * 3 + [pltpu.VMEM((BLOCK + 16, pair_width), F32)] * 3 + [
        pltpu.VMEM((8, width), F32), pltpu.VMEM((8, pair_width), F32), pltpu.VMEM((8, LANES), F32),
        pltpu.VMEM((half, BLOCK, model), core_wire), pltpu.VMEM((half, BLOCK, model), core_wire),
        pltpu.VMEM((half, BLOCK, model), BF16), pltpu.VMEM((half, BLOCK, model), BF16),
        pltpu.VMEM((2, model), F32), pltpu.VMEM((2 * size, 2, model), F32),
        pltpu.VMEM((n_w, width), F32), pltpu.VMEM((model, LANES), F32), pltpu.VMEM((n_pack, width), F32),
        pltpu.VMEM((model, pair_width), F32), pltpu.VMEM((32, pair_width), F32),
        pltpu.VMEM((r_small * size, pair_width), F32), pltpu.VMEM((r_wp * size, pair_width), F32),
        pltpu.VMEM((n_pack, width), F32), pltpu.VMEM((model, pair_width), F32), pltpu.VMEM((32, pair_width), F32),
        pltpu.VMEM((half, BLOCK, model), BF16), pltpu.VMEM((half, BLOCK, model), BF16),
        pltpu.VMEM((2 * width + LANES + 2 * pair_width, model), BF16),
        pltpu.VMEM((3, 8, model), F32), pltpu.VMEM((8, model), F32), pltpu.VMEM((8, model), F32), pltpu.VMEM((8, model), F32),
        dma((half,)), dma((half,)), dma((half,)), dma((half,)), dma((3,)), dma((3,)), dma((half,)), dma((half,)),
        dma((2 * size,)), dma((2 * size,)),
    ]
    if summing:
        scratch += HeadSum.scratch(model, pair_width, r_wp * size) + HeadSum.scratch(32, pair_width, r_small * size)
        for r, lanes, wire in sum_shapes:
            scratch += SeqSum.scratch(r, lanes, wire, size)
    grad_hidden, g_norm, loss, *grads, g_wp, g_ws, g_ci, g_bi, g_cp, g_bp, g_sb, g_dl, g_skip, g_gain = call(
        finale_kernel,
        blocks,
        [
            (d_scaled, *back(width)), (d_maps, *back(pair_width)), (pre_i, *back(width)), (pre_p, *back(pair_width)),
            (in_i, *back(width)), (in_p, *back(pair_width)), (halo_low, *whole), (halo_i, *whole), (halo_p, *whole),
            (aux, *back(LANES)), (gloc, *back3(CHUNK)), (pkb, *back3(8)), (grad_in, *whole), (states, *back3(CHUNK)),
            (d_mixer, *back(width)), (mixer, *back(width)), (given, *whole), (conv_inner, *whole), (conv_pair, *whole),
            (low_t, (model, BLOCK), lambda i, *_: (0, blocks - 1 - i)), (d_gate, *back(width)), (w_gate, *whole), (w_inner, *whole), (ws, *whole), (w_pair, *whole),
            (hidden, *once(model)), (d_out, *vmem), (gain, *whole), (error, *whole), (g_wo, *vmem), (g_wg, *vmem),
            (g_gain, *whole), (factor.reshape(1), "smem", None),
        ],
        [
            ((rows, model), BF16, *vmem), ((1, model), F32, *vmem), ((1, 1), F32, *vmem), ((n_wo, model), F32, *vmem),
            ((n_w, width), F32, *vmem), ((n_w, width), F32, *vmem), ((model, pair_width), F32, *vmem),
            ((model, heads), F32, *vmem), ((4, width), F32, *vmem), ((1, width), F32, *vmem), ((4, pair_width), F32, *vmem),
            ((1, pair_width), F32, *vmem), ((1, heads), F32, *vmem), ((1, heads), F32, *vmem), ((1, heads), F32, *vmem),
            ((1, width), F32, *vmem),
        ],
        scratch,
        flops=9e9, moved=8e7, collective=4, vmem=58,
    )
    if not summing:
        *grads, g_ws, g_ci, g_bi, g_sb, g_dl, g_skip, g_gain = lax.psum(
            (*grads, g_ws, g_ci, g_bi, g_sb, g_dl, g_skip, g_gain), "seq"
        )
        g_wp, g_cp, g_bp = lax.psum((g_wp, g_cp, g_bp), ("seq", "head"))
    g_wo, g_wg, g_wi = grads
    return (
        output, loss.reshape(()), grad_hidden, g_norm.reshape(-1), g_wg, g_wi, g_wp, g_ws, g_ci, g_bi.reshape(-1), g_cp,
        g_bp.reshape(-1), g_sb.reshape(-1), g_dl.reshape(-1), g_skip.reshape(-1), g_gain.reshape(-1), g_wo,
    )


def solution(mesh):
    seq, head, wide = P("seq", None), P("head"), P(None, "head")
    in_specs = (
        seq, seq, P(), P("seq"), P(), wide, wide, P(), wide, wide, head, P(), P(), head, head, head, head, P("head", None),
    )
    out_specs = (
        seq, P(), seq, P(), wide, wide, P(), wide, wide, head, P(), P(), head, head, head, head, P("head", None),
    )
    return jax.shard_map(shards, mesh=mesh, in_specs=in_specs, out_specs=out_specs, check_vma=False)
```
